32 devices in a mesh: dp: 8 (over z, x), seq: 4 (over y, core).
Axes of the slice: x: 2, y: 2, z: 4, core: 2. Of those that a mesh axis runs over, the one named last changes fastest.
Arguments:
- tokens: bfloat16 [16, 2048, 1024], P('dp', 'seq'), may hold values from -6 to 6
- cotangent: bfloat16 [16, 2048, 1024], P('dp', 'seq'), may hold values from -6 to 6
- lengths: int32 [16], replicated, may hold values from 512 to 2048, as said below
- assignment: int32 [16], replicated, may hold values from 0 to 15, as said below
- mix_norm_gain: bfloat16 [1024], P('dp'), may hold values from 0.5 to 1.5
- mix_norm_bias: bfloat16 [1024], P('dp'), may hold values from -1.75 to 1.75
- shift_key: bfloat16 [1024], P('dp'), may hold values from 0 to 1
- shift_value: bfloat16 [1024], P('dp'), may hold values from 0 to 1
- shift_recept: bfloat16 [1024], P('dp'), may hold values from 0 to 1
- time_decay: bfloat16 [1024], P('dp'), may hold values from -9 to -3.390625
- time_first: bfloat16 [1024], P('dp'), may hold values from -1 to 1
- key_weight: bfloat16 [1024, 1024], P('dp'), may hold values from -1 to 1
- value_weight: bfloat16 [1024, 1024], P('dp'), may hold values from -1 to 1
- recept_weight: bfloat16 [1024, 1024], P('dp'), may hold values from -1 to 1
- output_weight: bfloat16 [1024, 1024], P('dp'), may hold values from -3 to 3
- feed_norm_gain: bfloat16 [1024], P('dp'), may hold values from 0.5 to 1.5
- feed_norm_bias: bfloat16 [1024], P('dp'), may hold values from -1.75 to 1.75
- feed_shift_key: bfloat16 [1024], P('dp'), may hold values from 0 to 1
- feed_shift_recept: bfloat16 [1024], P('dp'), may hold values from 0 to 1
- feed_key_weight: bfloat16 [1024, 4096], P('dp'), may hold values from -1 to 1
- feed_recept_weight: bfloat16 [1024, 1024], P('dp'), may hold values from -1 to 1
- feed_value_weight: bfloat16 [4096, 1024], P('dp'), may hold values from -0.09375 to 0.09375
Outputs:
- block_out: bfloat16 [16, 2048, 1024], P('dp', 'seq')
- input_grad: bfloat16 [16, 2048, 1024], P('dp', 'seq')
- grad_mix_norm_gain: float32 [1024], P('dp')
- grad_mix_norm_bias: float32 [1024], P('dp')
- grad_shift_key: float32 [1024], P('dp')
- grad_shift_value: float32 [1024], P('dp')
- grad_shift_recept: float32 [1024], P('dp')
- grad_time_decay: float32 [1024], P('dp')
- grad_time_first: float32 [1024], P('dp')
- grad_key_weight: float32 [1024, 1024], P('dp')
- grad_value_weight: float32 [1024, 1024], P('dp')
- grad_recept_weight: float32 [1024, 1024], P('dp')
- grad_output_weight: float32 [1024, 1024], P('dp')
- grad_feed_norm_gain: float32 [1024], P('dp')
- grad_feed_norm_bias: float32 [1024], P('dp')
- grad_feed_shift_key: float32 [1024], P('dp')
- grad_feed_shift_recept: float32 [1024], P('dp')
- grad_feed_key_weight: float32 [1024, 4096], P('dp')
- grad_feed_recept_weight: float32 [1024, 1024], P('dp')
- grad_feed_value_weight: float32 [4096, 1024], P('dp')
- residual_rms: float32 [], replicated
- mix_rms: float32 [], replicated
- feed_rms: float32 [], replicated
The draws below stay inside these ranges and needn't reach their ends.
Inputs may be any that keep to these rules, and one draw needn't show every extreme that they name: lengths[i] is the valid length of sequence i; of the 2 slots of each index of dp one holds a sequence 2048 long. a permutation: slot s holds sequence assignment[s].
All inputs are finite; a program needn't handle non-finite values.
Results may differ from the reference program's by a relative error of at most 0.018.
Values may be sent and summed in bfloat16 or wider, within the bound.
No kernel may reach another device: no remote copies, remote signals or barrier semaphores. Data moves between devices by JAX's collectives and lax.ppermute only.
A program may use at most 256 MiB of HBM per device.

```python
from functools import partial
import jax
import jax.numpy as jnp
from jax import lax

D = 1024
FF = 4096
MICRO = 2
BLOCK = 32
LENGTH = 2048
LEN_MIN = 512
SEQS = 16


def slot_lengths(key):
    base_key = jax.random.fold_in(key, 11)
    first_key, second_key = jax.random.split(base_key, 2)
    raw_lengths = jax.random.randint(first_key, (SEQS,), LEN_MIN, LENGTH + 1)
    full_member = jax.random.randint(second_key, (SEQS // MICRO,), 0, MICRO)
    slot_ids = jnp.arange(SEQS)
    member = slot_ids % MICRO
    group_full = jnp.take(full_member, slot_ids // MICRO)
    raw_lengths = jnp.where(member == group_full, LENGTH, raw_lengths)
    short_slot = (full_member[0] + 1) % MICRO
    raw_lengths = jnp.where(slot_ids == short_slot, LEN_MIN, raw_lengths)
    return raw_lengths.astype(jnp.int32)


def slot_order(key):
    return jax.random.permutation(jax.random.fold_in(key, 23), SEQS).astype(jnp.int32)


def draw_assignment(key, part):
    return slot_order(key)


def draw_lengths(key, part):
    order_now = slot_order(key)
    return jnp.zeros((SEQS,), jnp.int32).at[order_now].set(slot_lengths(key))


def projection_draw(key, salt_value, row_total, column_total):
    noise_key, column_key = jax.random.split(jax.random.fold_in(key, salt_value), 2)
    noise_part = jax.random.truncated_normal(noise_key, -4.0, 4.0, (row_total, column_total), jnp.float32)
    column_part = jax.random.truncated_normal(column_key, -3.0, 3.0, (column_total,), jnp.float32) * 0.35
    return (noise_part + column_part[None, :]) * row_total ** (-0.5)


def draw_key_weight(key, part):
    return projection_draw(key, 101, D, D).astype(jnp.bfloat16)


def draw_value_weight(key, part):
    return projection_draw(key, 103, D, D).astype(jnp.bfloat16)


def draw_recept_weight(key, part):
    return projection_draw(key, 107, D, D).astype(jnp.bfloat16)


def draw_feed_key_weight(key, part):
    return projection_draw(key, 109, D, FF).astype(jnp.bfloat16)


def draw_feed_recept_weight(key, part):
    return projection_draw(key, 113, D, D).astype(jnp.bfloat16)


def block_levels(stream_key, dims, cuts, low, top_value):
    def one(axis_at, parts):
        draws = jax.random.uniform(jax.random.fold_in(jax.random.fold_in(stream_key, 6), axis_at), (parts,), jnp.float32, low / len(cuts), top_value / len(cuts))
        return jnp.repeat(jnp.exp(draws), dims[axis_at] // parts).reshape((-1,) + (1,) * (len(dims) - axis_at - 1))

    gain = one(*cuts[0])
    for cut in cuts[1:]:
        gain = gain * one(*cut)
    return gain


def normal_values(key, shape, scale, reach, shards=(), kind=jnp.bfloat16):
    values = scale * jax.random.normal(key, shape, jnp.float32)
    if shards:
        values = values * block_levels(key, shape, shards, -0.22, 0.18)
    return jnp.clip(values, -reach, reach).astype(kind)


def setup_inputs(seed: int = 0) -> dict:
    key_of = jax.random.split(jax.random.key(seed), 23)
    tokens = normal_values(key_of[0], (SEQS, LENGTH, D), 1.0, 6.0, ((0, 8), (1, 4)))
    cotangent = normal_values(key_of[1], (SEQS, LENGTH, D), 1.0, 6.0, ((0, 8), (1, 4)))
    lengths = draw_lengths(jax.random.fold_in(key_of[22], 71), 0)
    assignment = draw_assignment(jax.random.fold_in(key_of[22], 71), 0)
    mix_norm_gain = jnp.clip(1.0 + 0.1 * jax.random.normal(key_of[4], (D,), jnp.float32), 0.5, 1.5).astype(jnp.bfloat16)
    mix_norm_bias = normal_values(key_of[5], (D,), 0.3, 1.75, ((0, 8),))
    shift_key = jnp.clip(1.0 * jax.random.uniform(key_of[6], (D,), jnp.float32) ** block_levels(key_of[6], (D,), ((0, 8),), -0.2, 0.2), 0.0, 1.0).astype(jnp.bfloat16)
    shift_value = jnp.clip(1.0 * jax.random.uniform(key_of[7], (D,), jnp.float32) ** block_levels(key_of[7], (D,), ((0, 8),), -0.2, 0.2), 0.0, 1.0).astype(jnp.bfloat16)
    shift_recept = jnp.clip(1.0 * jax.random.uniform(key_of[8], (D,), jnp.float32) ** block_levels(key_of[8], (D,), ((0, 8),), -0.2, 0.2), 0.0, 1.0).astype(jnp.bfloat16)
    time_decay = jnp.clip(-9.0 + 5.609375 * jax.random.uniform(key_of[9], (D,), jnp.float32) ** block_levels(key_of[9], (D,), ((0, 8),), -0.2, 0.2), -9.0, -3.390625).astype(jnp.bfloat16)
    time_first = jnp.clip(jax.random.uniform(key_of[10], (D,), jnp.float32, -1.0, 1.0) * block_levels(key_of[10], (D,), ((0, 8),), -0.4, 0.0), -1.0, 1.0).astype(jnp.bfloat16)
    key_weight = draw_key_weight(jax.random.fold_in(key_of[22], 71), 0)
    value_weight = draw_value_weight(jax.random.fold_in(key_of[22], 71), 0)
    recept_weight = draw_recept_weight(jax.random.fold_in(key_of[22], 71), 0)
    output_weight = normal_values(key_of[14], (D, D), (max(D // 256, 1)) ** -0.5, 3.0, ((0, 8),))
    feed_norm_gain = jnp.clip(1.0 + 0.1 * jax.random.normal(key_of[15], (D,), jnp.float32), 0.5, 1.5).astype(jnp.bfloat16)
    feed_norm_bias = normal_values(key_of[16], (D,), 0.3, 1.75, ((0, 8),))
    feed_shift_key = jnp.clip(1.0 * jax.random.uniform(key_of[17], (D,), jnp.float32) ** block_levels(key_of[17], (D,), ((0, 8),), -0.2, 0.2), 0.0, 1.0).astype(jnp.bfloat16)
    feed_shift_recept = jnp.clip(1.0 * jax.random.uniform(key_of[18], (D,), jnp.float32) ** block_levels(key_of[18], (D,), ((0, 8),), -0.2, 0.2), 0.0, 1.0).astype(jnp.bfloat16)
    feed_key_weight = draw_feed_key_weight(jax.random.fold_in(key_of[22], 71), 0)
    feed_recept_weight = draw_feed_recept_weight(jax.random.fold_in(key_of[22], 71), 0)
    feed_value_weight = normal_values(key_of[21], (FF, D), FF ** -0.5, 0.09375, ((0, 8),))
    return dict(tokens=tokens, cotangent=cotangent, lengths=lengths, assignment=assignment, mix_norm_gain=mix_norm_gain, mix_norm_bias=mix_norm_bias, shift_key=shift_key, shift_value=shift_value, shift_recept=shift_recept, time_decay=time_decay, time_first=time_first, key_weight=key_weight, value_weight=value_weight, recept_weight=recept_weight, output_weight=output_weight, feed_norm_gain=feed_norm_gain, feed_norm_bias=feed_norm_bias, feed_shift_key=feed_shift_key, feed_shift_recept=feed_shift_recept, feed_key_weight=feed_key_weight, feed_recept_weight=feed_recept_weight, feed_value_weight=feed_value_weight)


norm_eps = 1e-05

@jax.custom_vjp
def low(v):
    return lax.optimization_barrier(v.astype(jnp.bfloat16)).astype(jnp.float32)

@jax.custom_vjp
def low_back(v):
    return v

def low_keep(v):
    return (low(v), None)

def low_pass(kept, grad):
    return (grad,)

def back_keep(v):
    return (v, None)

def back_low(kept, grad):
    return (low(grad),)
low.defvjp(low_keep, low_pass)
low_back.defvjp(back_keep, back_low)

def norm_rows(values, gain_vec, bias_vec):
    centre = values - lax.optimization_barrier(jnp.mean(values, axis=-1, keepdims=True))
    spread = lax.optimization_barrier(jnp.mean(centre * centre, axis=-1, keepdims=True))
    return centre * lax.rsqrt(spread + norm_eps) * gain_vec + bias_vec

def shifted(values):
    return jnp.concatenate([jnp.zeros((1, values.shape[1]), jnp.float32), values[:-1]], axis=0)

def product(left_rows, right_rows):
    return jnp.dot(left_rows, right_rows, precision=lax.Precision.HIGHEST, preferred_element_type=jnp.float32)

def decay_tables(fading_multiplier):
    offsets = jnp.arange(BLOCK).astype(jnp.float32)
    spacing = offsets[:, None] - offsets[None, :] - 1.0
    decay_table = jnp.where((spacing >= 0.0)[:, :, None], jnp.exp(-jnp.maximum(spacing, 0.0)[:, :, None] * fading_multiplier), 0.0)
    falling = jnp.exp(-offsets[:, None] * fading_multiplier)
    trailing = jnp.exp(-(BLOCK - 1.0 - offsets)[:, None] * fading_multiplier)
    return (decay_table, falling, trailing, jnp.exp(-BLOCK * fading_multiplier))

def segment_forward_sweep(sharded_arrays_group, current_boost_array, running_recurrence, segment_entries):
    decay_table, falling, trailing, whole_block = sharded_arrays_group
    num_state, den_state = running_recurrence
    lookup_segment_lines, content_segment_lines = segment_entries
    exponentiated_lookup = jnp.exp(lookup_segment_lines)
    weighted = exponentiated_lookup * content_segment_lines
    dividend_earlier = falling * num_state + lax.optimization_barrier(jnp.sum(decay_table * weighted[None, :, :], axis=1))
    divisor_earlier = falling * den_state + lax.optimization_barrier(jnp.sum(decay_table * exponentiated_lookup[None, :, :], axis=1))
    boosted_lookup_entry = jnp.exp(current_boost_array + lookup_segment_lines)
    attention_result = (dividend_earlier + boosted_lookup_entry * content_segment_lines) / (divisor_earlier + boosted_lookup_entry)
    num_after = whole_block * num_state + lax.optimization_barrier(jnp.sum(trailing * weighted, axis=0))
    den_after = whole_block * den_state + lax.optimization_barrier(jnp.sum(trailing * exponentiated_lookup, axis=0))
    return ((num_after, den_after), (attention_result, dividend_earlier, divisor_earlier))

def attention_average(lookup_line_pile, content_line_pile, fading_multiplier, current_boost_array):
    sharded_arrays_group = decay_tables(fading_multiplier)
    blocks = lookup_line_pile.shape[0] // BLOCK
    channels = lookup_line_pile.shape[1]
    training_update_routine = jax.checkpoint(partial(segment_forward_sweep, sharded_arrays_group, current_boost_array))
    initial = (jnp.zeros((channels,), jnp.float32), jnp.zeros((channels,), jnp.float32))
    unused, outputs = lax.scan(training_update_routine, initial, (lookup_line_pile.reshape(blocks, BLOCK, channels), content_line_pile.reshape(blocks, BLOCK, channels)))
    return outputs[0].reshape(blocks * BLOCK, channels)

def layer(inputs, valid_mask, learned_quantities):
    initial_layernorm_scale, initial_layernorm_offset, lagged_lookup_lines, lagged_content_lines, lagged_gating_lines, fading_log_rate, current_boost_array, lookup_weights, content_weights, gating_weights, projection_weights_final, latter_layernorm_scale, latter_layernorm_offset, channel_lagged_lookup, channel_lagged_gating, channel_lookup_weights, channel_gating_weights, channel_content_weights = learned_quantities
    normed = norm_rows(inputs, initial_layernorm_scale, initial_layernorm_offset)
    before = shifted(normed)
    key_in = low(normed * lagged_lookup_lines + before * (1.0 - lagged_lookup_lines))
    value_in = low(normed * lagged_content_lines + before * (1.0 - lagged_content_lines))
    recept_in = low(normed * lagged_gating_lines + before * (1.0 - lagged_gating_lines))
    lookup_line_pile = low_back(product(key_in, lookup_weights))
    content_line_pile = low_back(product(value_in, content_weights))
    recept_rows = low_back(product(recept_in, gating_weights))
    attention_result = attention_average(lookup_line_pile, content_line_pile, jnp.exp(fading_log_rate), current_boost_array)
    weighted = low(jax.nn.sigmoid(recept_rows) * attention_result)
    attn_out = low_back(product(weighted, projection_weights_final))
    middle = inputs + attn_out
    normed_two = norm_rows(middle, latter_layernorm_scale, latter_layernorm_offset)
    before_two = shifted(normed_two)
    feed_key_in = low(normed_two * channel_lagged_lookup + before_two * (1.0 - channel_lagged_lookup))
    feed_recept_in = low(normed_two * channel_lagged_gating + before_two * (1.0 - channel_lagged_gating))
    hidden = low_back(product(feed_key_in, channel_lookup_weights))
    squared = low(jnp.square(jax.nn.relu(hidden)))
    feed_value = low_back(product(squared, channel_content_weights))
    feed_gate = jax.nn.sigmoid(low_back(product(feed_recept_in, channel_gating_weights)))
    feed_out = feed_gate * feed_value
    keep_rows = valid_mask[:, None]
    return (keep_rows * (middle + feed_out), (attn_out, feed_out))

def reference(tokens, cotangent, lengths, assignment, mix_norm_gain, mix_norm_bias, shift_key, shift_value, shift_recept, time_decay, time_first, key_weight, value_weight, recept_weight, output_weight, feed_norm_gain, feed_norm_bias, feed_shift_key, feed_shift_recept, feed_key_weight, feed_recept_weight, feed_value_weight):
    weights = tuple((tensor.astype(jnp.float32) for tensor in (mix_norm_gain, mix_norm_bias, shift_key, shift_value, shift_recept, time_decay, time_first, key_weight, value_weight, recept_weight, output_weight, feed_norm_gain, feed_norm_bias, feed_shift_key, feed_shift_recept, feed_key_weight, feed_recept_weight, feed_value_weight)))
    slot_length = jnp.take(lengths, assignment).astype(jnp.int32)
    positions = jnp.arange(LENGTH).astype(jnp.int32)

    def one_sequence(totals, sequence_items):
        grad_sums, square_sums = totals
        rows_in, rows_cot, length_here = sequence_items
        valid_mask = (positions < length_here).astype(jnp.float32)

        def forward(inputs, learned_quantities):
            return layer(inputs, valid_mask, learned_quantities)
        outputs, pull_back, branches = jax.vjp(forward, rows_in.astype(jnp.float32), weights, has_aux=True)
        in_grad, weight_grads = pull_back(rows_cot.astype(jnp.float32))
        attn_out, feed_out = branches
        keep_rows = valid_mask[:, None]
        stats_now = jnp.stack([jnp.sum(outputs * outputs), jnp.sum(keep_rows * attn_out * attn_out), jnp.sum(keep_rows * feed_out * feed_out)])
        grad_sums = jax.tree.map(lambda total_grad, new_grad: total_grad + new_grad, grad_sums, weight_grads)
        return ((grad_sums, square_sums + stats_now), (outputs.astype(jnp.bfloat16), in_grad.astype(jnp.bfloat16)))
    zero_grads = tuple((jnp.zeros_like(tensor) for tensor in weights))
    (grad_list, square_sums), (block_out, input_grad) = lax.scan(one_sequence, (zero_grads, jnp.zeros((3,), jnp.float32)), (tokens, cotangent, slot_length))
    valid_count = jnp.sum(lengths).astype(jnp.float32) * D
    rms_values = jnp.sqrt(square_sums / valid_count)
    return (block_out, input_grad, grad_list[0], grad_list[1], grad_list[2], grad_list[3], grad_list[4], grad_list[5], grad_list[6], grad_list[7], grad_list[8], grad_list[9], grad_list[10], grad_list[11], grad_list[12], grad_list[13], grad_list[14], grad_list[15], grad_list[16], grad_list[17], rms_values[0], rms_values[1], rms_values[2])
```

```python
import functools

import jax
import jax.numpy as jnp
from jax import lax
from jax.experimental import pallas as pl
from jax.experimental.pallas import tpu as pltpu
from jax.sharding import PartitionSpec as P

D = 1024
EPS = 1e-05
F32 = jnp.float32
BF16 = jnp.bfloat16


def axes_of(letter, size):
    return tuple(f"{letter}{bit}" for bit in reversed(range(size.bit_length() - 1)))


def swap(value, key):
    return lax.ppermute(value, key, [(0, 1), (1, 0)])


def place(held, key):
    rank = lambda k: (k[0] == "s", -int(k[1:]))
    return sum(1 for other in held if rank(other) < rank(key))


def join(mine, other, key, at):
    first = lax.axis_index(key) == 0
    return jnp.stack(
        [jnp.where(first, mine, other), jnp.where(first, other, mine)], axis=at
    )


def half(value, which, at):
    return lax.dynamic_index_in_dim(value, which, at, keepdims=False)


def add_low(mine, other):
    return (mine.astype(F32) + other.astype(F32)).astype(BF16)


def tie(*values):
    return lax.optimization_barrier(values)


class Growing:
    def __init__(self, value):
        self.value, self.held = value, []

    def hop(self, key, cut=None):
        at = place(self.held, key)
        other = swap(self.value, key)
        self.held.append(key)
        if cut is None:
            self.value = join(self.value, other, key, at)
        else:
            self.value = [join(m, o, key, at) for m, o in zip(cut(self.value), cut(other))]


class Shrinking:
    def __init__(self, value, held):
        self.value, self.held = value, list(held)

    def hop(self, key):
        self.held.remove(key)
        at = place(self.held, key)
        bit = lax.axis_index(key)
        got = swap(half(self.value, 1 - bit, at), key)
        self.value = add_low(half(self.value, bit, at), got)


def grow(values, key):
    for v in values:
        v.hop(key)


def settle(items, *others):
    tied = tie(*[item.value for item in items], *others)
    for item, value in zip(items, tied):
        item.value = value
    return tied[len(items) :]


ROWS = 8


def fwd_kernel(k_ref, v_ref, r_ref, rate_ref, u_ref, a0_ref, b0_ref, w_ref, a_ref, b_ref):
    rate = rate_ref[...]
    boost = jnp.exp(u_ref[...])
    width = rate.shape[1]
    row = lax.broadcasted_iota(jnp.int32, (ROWS, width), 0)
    rowf = row.astype(F32)
    falling = jnp.exp(-rowf * rate)
    one = jnp.exp(-rate)
    steps = [(s, jnp.where(row >= s, jnp.exp(-s * rate), 0.0)) for s in (1, 2, 4)]
    inner = row >= 1

    def scan(tile, carry):
        before = jnp.where(inner, pltpu.roll(tile, 1, 0), 0.0)
        for s, factor in steps:
            before = before + factor * pltpu.roll(before, s, 0)
        before = before + falling * carry
        after = one * before[ROWS - 1 :, :] + tile[ROWS - 1 :, :]
        return before, after

    def tile_of(start, carry):
        num, den = carry
        at = pl.ds(start, ROWS)
        key = k_ref[at, :]
        val = v_ref[at, :]
        power = jnp.exp(key)
        num_before, num = scan(power * val, num)
        den_before, den = scan(power, den)
        a_ref[at, :] = num_before
        b_ref[at, :] = den_before
        now = boost * power
        mixed = (num_before + now * val) / (den_before + now)
        return jax.nn.sigmoid(r_ref[at, :]) * mixed, (num, den)

    def body(i, carry):
        start = pl.multiple_of(i * (2 * ROWS), 2 * ROWS)
        low, carry = tile_of(start, carry)
        high, carry = tile_of(pl.multiple_of(start + ROWS, ROWS), carry)
        w_ref[pl.ds(start, 2 * ROWS), :] = jnp.concatenate([low, high], axis=0).astype(BF16)
        return carry

    lax.fori_loop(
        0, k_ref.shape[0] // (2 * ROWS), body, (a0_ref[...], b0_ref[...]), unroll=2
    )


def bwd_kernel(
    k_ref, v_ref, r_ref, a_ref, b_ref, dw_ref, rate_ref, u_ref, ga_ref, gb_ref,
    dk_ref, dv_ref, first_ref, decay_ref,
):
    rate = rate_ref[...]
    boost = jnp.exp(u_ref[...])
    width = rate.shape[1]
    row = lax.broadcasted_iota(jnp.int32, (ROWS, width), 0)
    rowf = row.astype(F32)
    trailing = jnp.exp(-(ROWS - 1.0 - rowf) * rate)
    one = jnp.exp(-rate)
    steps = [(s, jnp.where(row < ROWS - s, jnp.exp(-s * rate), 0.0)) for s in (1, 2, 4)]
    inner = row < ROWS - 1

    def scan(tile, carry):
        later = jnp.where(inner, pltpu.roll(tile, ROWS - 1, 0), 0.0)
        for s, factor in steps:
            later = later + factor * pltpu.roll(later, ROWS - s, 0)
        later = later + trailing * carry
        before = one * later[:1, :] + tile[:1, :]
        return later, before

    def tile_of(start, carry):
        num, den, first, decay = carry
        at = pl.ds(start, ROWS)
        key = k_ref[at, :]
        val = v_ref[at, :]
        num_before = a_ref[at, :]
        den_before = b_ref[at, :]
        power = jnp.exp(key)
        now = boost * power
        inverse = 1.0 / (den_before + now)
        mixed = (num_before + now * val) * inverse
        gate = jax.nn.sigmoid(r_ref[at, :])
        d_weighted = dw_ref[at, :]
        d_mixed = d_weighted * gate
        p = d_mixed * inverse
        q = -p * mixed
        num_later, num = scan(p, num)
        den_later, den = scan(q, den)
        diagonal = now * (val * p + q)
        d_key = power * (val * num_later + den_later) + diagonal
        d_val = power * num_later + now * p
        first = first + diagonal
        decay = decay + (num_later * num_before + den_later * den_before)
        return (d_key, d_val), (num, den, first, decay)

    count = k_ref.shape[0] // (2 * ROWS)

    def body(i, carry):
        start = pl.multiple_of((count - 1 - i) * (2 * ROWS), 2 * ROWS)
        high, carry = tile_of(pl.multiple_of(start + ROWS, ROWS), carry)
        low, carry = tile_of(start, carry)
        at = pl.ds(start, 2 * ROWS)
        for ref, a, b in zip((dk_ref, dv_ref), low, high):
            ref[at, :] = jnp.concatenate([a, b], axis=0).astype(BF16)
        return carry

    zero = jnp.zeros((ROWS, width), F32)
    done = lax.fori_loop(0, count, body, (ga_ref[...], gb_ref[...], zero, zero), unroll=2)
    first_ref[...] = done[2]
    decay_ref[...] = done[3]


WIDTH = 256


def wkv_specs(rows):
    big = pl.BlockSpec((rows, WIDTH), lambda s, c: (s, c))
    row = pl.BlockSpec((1, WIDTH), lambda s, c: (0, c))
    state = pl.BlockSpec((None, 1, WIDTH), lambda s, c: (s, 0, c))
    partial = pl.BlockSpec((None, ROWS, WIDTH), lambda s, c: (s, 0, c))
    return big, row, state, partial


def wkv_forward(keys, vals, recepts, rate, first, num, den, seqs):
    total = keys.shape[0]
    big, row, state, _ = wkv_specs(total // seqs)
    cells = total * D
    return pl.pallas_call(
        fwd_kernel,
        grid=(seqs, D // WIDTH),
        in_specs=[big, big, big, row, row, state, state],
        out_specs=[big, big, big],
        out_shape=[
            jax.ShapeDtypeStruct((total, D), BF16),
            jax.ShapeDtypeStruct((total, D), F32),
            jax.ShapeDtypeStruct((total, D), F32),
        ],
        compiler_params=pltpu.CompilerParams(vmem_limit_bytes=32 << 20),
        cost_estimate=pl.CostEstimate(
            flops=60 * cells, bytes_accessed=22 * cells, transcendentals=4 * cells
        ),
    )(keys, vals, recepts, rate, first, num, den)


def wkv_backward(keys, vals, recepts, num_before, den_before, d_weighted, rate, first, num, den, seqs):
    total = keys.shape[0]
    big, row, state, partial = wkv_specs(total // seqs)
    cells = total * D
    return pl.pallas_call(
        bwd_kernel,
        grid=(seqs, D // WIDTH),
        in_specs=[big, big, big, big, big, big, row, row, state, state],
        out_specs=[big, big, partial, partial],
        out_shape=[
            jax.ShapeDtypeStruct((total, D), BF16),
            jax.ShapeDtypeStruct((total, D), BF16),
            jax.ShapeDtypeStruct((seqs, ROWS, D), F32),
            jax.ShapeDtypeStruct((seqs, ROWS, D), F32),
        ],
        compiler_params=pltpu.CompilerParams(vmem_limit_bytes=32 << 20),
        cost_estimate=pl.CostEstimate(
            flops=90 * cells, bytes_accessed=30 * cells, transcendentals=4 * cells
        ),
    )(keys, vals, recepts, num_before, den_before, d_weighted, rate, first, num, den)


def dot(left, right):
    return jnp.dot(left, right, preferred_element_type=F32)


def dot_back(grads, weight):
    return lax.dot_general(grads, weight, (((1,), (1,)), ((), ())), preferred_element_type=F32)


def dot_weight(inputs, grads):
    return lax.dot_general(inputs, grads, (((0,), (0,)), ((), ())), preferred_element_type=F32)


def normalize(values):
    centre = values - jnp.mean(values, axis=-1, keepdims=True)
    spread = jnp.mean(centre * centre, axis=-1, keepdims=True)
    inverse = lax.rsqrt(spread + EPS)
    return centre * inverse, inverse


def from_behind(value, axes, by):
    count = lax.axis_size(axes)
    pairs = [(i, i + by) for i in range(count) if 0 <= i + by < count]
    return lax.ppermute(value, axes, pairs)


def shifted(rows, edge):
    return jnp.concatenate([edge, rows[:, :-1]], axis=1)


def pulled(rows, edge):
    return jnp.concatenate([rows[:, 1:], edge], axis=1)


def blend(now, before, share):
    return (now * share + before * (1.0 - share)).astype(BF16)


def earlier_state(decay, num, den, axes, backward):
    count = lax.axis_size(axes)
    mine = lax.axis_index(axes)
    packed = lax.all_gather(jnp.concatenate([num, den], axis=0), axes)
    seqs = num.shape[0]
    state = jnp.zeros_like(packed[0])
    for hop in range(count - 1):
        source = count - 1 - hop if backward else hop
        longer = decay * state + packed[source]
        keep = source > mine if backward else source < mine
        state = jnp.where(keep, longer, state)
    return state[:seqs, None, :], state[seqs:, None, :]


def per_device(
    dp_axes, seq_axes,
    tokens, cotangent, lengths, assignment,
    mix_norm_gain, mix_norm_bias, shift_key, shift_value, shift_recept, time_decay, time_first,
    key_weight, value_weight, recept_weight, output_weight,
    feed_norm_gain, feed_norm_bias, feed_shift_key, feed_shift_recept,
    feed_key_weight, feed_recept_weight, feed_value_weight,
):
    seqs, span, _ = tokens.shape
    total = seqs * span
    dp, seq = lax.axis_size(dp_axes), lax.axis_size(seq_axes)
    my_dp, my_seq = lax.axis_index(dp_axes), lax.axis_index(seq_axes)
    every = dp_axes + seq_axes
    z_axes, x = dp_axes[:-1], dp_axes[-1]
    y, c = seq_axes
    ff = feed_key_weight.shape[1]
    wide, thin = ff // 2, D // 2
    flat = lambda v: v.reshape(total, v.shape[-1])
    deep = lambda v: v.reshape(seqs, span, v.shape[-1])

    shard = D // dp
    quarter = shard // seq

    def own_rows(weight):
        return lax.dynamic_slice_in_dim(weight, my_seq * quarter, quarter, 0)

    hid = feed_value_weight.shape[0]
    w_fv = lax.all_gather(
        half(feed_value_weight.reshape(2, hid // 2, D), lax.axis_index(c), 0),
        dp_axes + (c,), axis=0, tiled=True,
    )
    vectors = Growing(
        jnp.stack(
            [
                mix_norm_gain, mix_norm_bias, shift_key, shift_value, shift_recept, time_decay, time_first,
                feed_norm_gain, feed_norm_bias, feed_shift_key, feed_shift_recept,
            ]
        )
    )
    kv = Growing(jnp.stack([own_rows(key_weight), own_rows(value_weight)]))
    ro = Growing(jnp.stack([own_rows(recept_weight), own_rows(output_weight)]))
    fk_own, fr_own = own_rows(feed_key_weight), own_rows(feed_recept_weight)
    f1 = Growing(jnp.concatenate([fk_own[:, :wide], fr_own[:, :thin]], axis=1))
    f2 = Growing(jnp.concatenate([fk_own[:, wide:], fr_own[:, thin:]], axis=1))
    edge1 = from_behind(tokens[:, -1:], seq_axes, 1)

    both = lambda v: [v[..., 0, :, :], v[..., 1, :, :]]
    cols = lambda v: [v[..., :wide], v[..., wide:]]
    for z in z_axes:
        grow([vectors, kv, ro], z)
        settle([vectors, kv, ro])
    vectors.hop(x)
    kv.hop(x)
    ro.hop(y)
    f1.hop(z_axes[0])
    f2.hop(z_axes[0])
    settle([vectors, kv, ro, f1, f2])
    kv.hop(y)
    ro.hop(x)
    for z in z_axes[1:]:
        grow([f1, f2], z)
    settle([kv, ro, f1, f2])
    f1.hop(x)
    f2.hop(y)
    kv.hop(c, both)
    ro.hop(c, both)
    w_k, w_v, w_r, w_o, f1.value, f2.value = tie(*kv.value, *ro.value, f1.value, f2.value)
    w_k, w_v, w_r, w_o = [w.reshape(D, D) for w in (w_k, w_v, w_r, w_o)]
    f1.hop(y)
    f2.hop(x)

    vectors = jnp.swapaxes(vectors.value.reshape(dp, 11, D // dp), 0, 1).reshape(11, D).astype(F32)
    gain1, bias1, mix_k, mix_v, mix_r, log_rate, first, gain2, bias2, fmix_k, fmix_r = [
        vectors[i : i + 1] for i in range(11)
    ]
    rate = jnp.exp(log_rate)
    lam = jnp.exp(-rate)

    slot_ids = jnp.arange(assignment.shape[0])
    my_slots = my_dp * seqs + jnp.arange(seqs)
    seq_ids = jnp.sum(jnp.where(slot_ids[None, :] == my_slots[:, None], assignment[None, :], 0), axis=1)
    my_lens = jnp.sum(jnp.where(slot_ids[None, :] == seq_ids[:, None], lengths[None, :], 0), axis=1)
    positions = my_seq * span + jnp.arange(span)
    valid = flat((positions[None, :] < my_lens[:, None]).astype(F32)[..., None])
    inside = (my_seq > 0).astype(F32)

    xin = tokens.astype(F32)
    edge1 = (normalize(edge1.astype(F32))[0] * gain1 + bias1) * inside
    n1, inv1 = normalize(xin)
    a = n1 * gain1 + bias1
    a_prev = shifted(a, edge1)
    key_in = flat(blend(a, a_prev, mix_k))
    value_in = flat(blend(a, a_prev, mix_v))
    recept_in = flat(blend(a, a_prev, mix_r))
    keys = dot(key_in, w_k)
    vals = dot(value_in, w_v)
    recepts = dot(recept_in, w_r)

    offsets = jnp.arange(span).astype(F32)[:, None]
    power = deep(jnp.exp(keys))
    left = jnp.exp(-(span - 1.0 - offsets) * rate)
    span_decay = jnp.exp(-span * rate)
    num_end = jnp.sum(left * power * deep(vals), axis=1)
    den_end = jnp.sum(left * power, axis=1)
    num_end, den_end = settle([f1, f2], num_end, den_end)
    f1.hop(c, cols)
    f2.hop(c, cols)
    num0, den0 = earlier_state(span_decay, num_end, den_end, seq_axes, False)
    weighted, num_before, den_before = wkv_forward(keys, vals, recepts, rate, first, num0, den0, seqs)
    attn = dot(weighted, w_o)
    middle = flat(xin) + attn

    w_fk1, w_fr1 = [w.reshape(D, -1) for w in f1.value]
    w_fk2, w_fr2 = [w.reshape(D, -1) for w in f2.value]
    w_fr = jnp.concatenate([w_fr1, w_fr2], axis=1)
    edge2 = from_behind(deep(middle)[:, -1:], seq_axes, 1)
    edge2 = (normalize(edge2)[0] * gain2 + bias2) * inside
    n2, inv2 = normalize(middle)
    b = n2 * gain2 + bias2
    b_prev = flat(shifted(deep(b), edge2))
    feed_key_in = blend(b, b_prev, fmix_k)
    feed_recept_in = blend(b, b_prev, fmix_r)
    sq1 = jnp.square(jax.nn.relu(dot(feed_key_in, w_fk1))).astype(BF16)
    sq2 = jnp.square(jax.nn.relu(dot(feed_key_in, w_fk2))).astype(BF16)
    gate = jax.nn.sigmoid(dot(feed_recept_in, w_fr))
    feed_value = dot(sq1, w_fv[:wide]) + dot(sq2, w_fv[wide:])
    feed = gate * feed_value
    result = middle + feed
    block_out = deep((valid * result).astype(BF16))
    stats = jnp.stack(
        [jnp.sum(valid * result * result), jnp.sum(valid * attn * attn), jnp.sum(valid * feed * feed)]
    )

    g = flat(cotangent).astype(F32) * valid
    d_fval = (g * gate).astype(BF16)
    d_fgate = (g * feed * (1.0 - gate)).astype(BF16)
    gfv = jnp.concatenate([dot_weight(sq1, d_fval).astype(BF16), dot_weight(sq2, d_fval).astype(BF16)], axis=0)
    gfv = lax.psum_scatter(gfv, dp_axes + (c,), scatter_dimension=0, tiled=True)
    gfr = dot_weight(feed_recept_in, d_fgate).astype(BF16)
    dh1 = (2.0 * jnp.sqrt(sq1.astype(F32)) * dot_back(d_fval, w_fv[:wide])).astype(BF16)
    dh2 = (2.0 * jnp.sqrt(sq2.astype(F32)) * dot_back(d_fval, w_fv[wide:])).astype(BF16)
    gfk1 = dot_weight(feed_key_in, dh1).astype(BF16)
    gfk2 = dot_weight(feed_key_in, dh2).astype(BF16)

    lead = (2,) * len(every)
    split = lambda g_: Shrinking(g_.reshape(lead + (quarter, g_.shape[1])), every)
    r1 = split(jnp.concatenate([gfk1, gfr[:, :thin]], axis=1))
    r2 = split(jnp.concatenate([gfk2, gfr[:, thin:]], axis=1))
    dh1, dh2 = settle([r1, r2], dh1, dh2)

    r1.hop(c)
    r2.hop(c)
    d_fk = dot_back(dh1, w_fk1) + dot_back(dh2, w_fk2)
    d_fr = dot_back(d_fgate, w_fr)
    d_fk, d_fr = settle([r1, r2], d_fk, d_fr)

    r1.hop(y)
    r2.hop(x)
    gap2 = b - b_prev
    grad_fmix_k = jnp.sum(gap2 * d_fk, axis=0)
    grad_fmix_r = jnp.sum(gap2 * d_fr, axis=0)
    later = deep(d_fk * (1.0 - fmix_k) + d_fr * (1.0 - fmix_r))
    db = d_fk * fmix_k + d_fr * fmix_r + flat(pulled(later, from_behind(later[:, :1], seq_axes, -1)))
    grad_gain2 = jnp.sum(n2 * db, axis=0)
    grad_bias2 = jnp.sum(db, axis=0)
    h2 = db * gain2
    d_middle = g + inv2 * (
        h2 - jnp.mean(h2, axis=-1, keepdims=True) - n2 * jnp.mean(h2 * n2, axis=-1, keepdims=True)
    )
    d_attn = d_middle.astype(BF16)
    d_weighted = dot_back(d_attn, w_o)
    ro_o = split(dot_weight(weighted, d_attn).astype(BF16))
    (d_weighted,) = settle([r1, r2, ro_o], d_weighted)

    r1.hop(x)
    r2.hop(y)
    ro_o.hop(c)
    now = jnp.exp(first + keys)
    inverse = 1.0 / (den_before + now)
    mixed = (num_before + now * vals) * inverse
    recept = jax.nn.sigmoid(recepts)
    d_recepts = (d_weighted * mixed * recept * (1.0 - recept)).astype(BF16)
    p = deep(d_weighted * recept * inverse)
    q = -p * deep(mixed)
    fall = jnp.exp(-offsets * rate)
    ga0, gb0 = earlier_state(
        span_decay, jnp.sum(fall * p, axis=1), jnp.sum(fall * q, axis=1), seq_axes, True
    )
    ro_r = split(dot_weight(recept_in, d_recepts).astype(BF16))
    ga0, gb0 = settle([r1, r2, ro_o, ro_r], ga0, gb0)

    z1, z2 = z_axes[-1], z_axes[:-1]
    r1.hop(z1)
    r2.hop(z1)
    ro_o.hop(y)
    ro_r.hop(c)
    d_keys, d_vals, first_part, decay_part = wkv_backward(
        keys, vals, recepts, num_before, den_before, d_weighted, rate, first, ga0, gb0, seqs
    )
    d_keys, d_vals = settle([r1, r2, ro_o, ro_r], d_keys, d_vals)

    for z in reversed(z2):
        r1.hop(z)
        r2.hop(z)
    ro_o.hop(x)
    ro_r.hop(x)
    r_k = split(dot_weight(key_in, d_keys).astype(BF16))
    r_v = split(dot_weight(value_in, d_vals).astype(BF16))
    d_keys, d_vals = settle([r1, r2, ro_o, ro_r, r_k, r_v], d_keys, d_vals)

    r_k.hop(c)
    r_v.hop(c)
    ro_o.hop(z1)
    ro_r.hop(y)
    out_f = Growing(jnp.stack([r1.value, r2.value]))
    out_f.hop(y)
    d_ki = dot_back(d_keys, w_k)
    d_vi = dot_back(d_vals, w_v)
    d_ri = dot_back(d_recepts, w_r)
    d_ki, d_vi, d_ri, gfv = settle([r_k, r_v, ro_o, ro_r, out_f], d_ki, d_vi, d_ri, gfv)

    r_k.hop(y)
    r_v.hop(x)
    for z in reversed(z2):
        ro_o.hop(z)
    ro_r.hop(z1)
    out_f.hop(c)
    gap1 = flat(a - a_prev)
    grad_mix_k = jnp.sum(gap1 * d_ki, axis=0)
    grad_mix_v = jnp.sum(gap1 * d_vi, axis=0)
    grad_mix_r = jnp.sum(gap1 * d_ri, axis=0)
    later = deep(d_ki * (1.0 - mix_k) + d_vi * (1.0 - mix_v) + d_ri * (1.0 - mix_r))
    da = d_ki * mix_k + d_vi * mix_v + d_ri * mix_r + flat(
        pulled(later, from_behind(later[:, :1], seq_axes, -1))
    )
    n1f, inv1f = flat(n1), flat(inv1)
    grad_gain1 = jnp.sum(n1f * da, axis=0)
    grad_bias1 = jnp.sum(da, axis=0)
    h1 = da * gain1
    d_x = inv1f * (
        h1 - jnp.mean(h1, axis=-1, keepdims=True) - n1f * jnp.mean(h1 * n1f, axis=-1, keepdims=True)
    )
    input_grad = deep((d_middle + d_x).astype(BF16))

    small = jnp.stack(
        [
            grad_gain1, grad_bias1, grad_mix_k, grad_mix_v, grad_mix_r,
            -(lam * rate)[0] * jnp.sum(decay_part, axis=(0, 1)), jnp.sum(first_part, axis=(0, 1)),
            grad_gain2, grad_bias2, grad_fmix_k, grad_fmix_r,
            jnp.pad(stats, (0, D - 3)),
        ]
    )
    small, input_grad = settle([r_k, r_v, ro_o, ro_r, out_f], small, input_grad)
    r_k.hop(x)
    r_v.hop(y)
    for z in reversed(z2):
        ro_r.hop(z)
    out_or = Growing(jnp.stack([ro_o.value, ro_r.value]))
    gfv = add_low(gfv, swap(gfv, y))
    small = small + swap(small, every[0])
    (small, gfv) = settle([r_k, r_v, out_or], small, gfv)
    r_k.hop(z1)
    r_v.hop(z1)
    out_or.hop(y)
    out_v = Growing(gfv)
    out_v.hop(c)
    small = small + swap(small, every[1])
    (small,) = settle([r_k, r_v, out_or, out_v], small)
    for z in reversed(z2):
        r_k.hop(z)
        r_v.hop(z)
    out_or.hop(c)
    small = small + swap(small, every[2])
    out_kv = Growing(jnp.stack([r_k.value, r_v.value]))
    (small,) = settle([out_kv, out_or], small)
    out_kv.hop(y)
    for key in every[3:]:
        small = small + swap(small, key)
    out_kv.hop(c)

    wide_out = lambda v, i: v[:, :, i].reshape(shard, -1)
    fk_r1, fk_r2 = wide_out(out_f.value, 0), wide_out(out_f.value, 1)
    grad_fk = jnp.concatenate([fk_r1[:, :wide], fk_r2[:, :wide]], axis=1).astype(F32)
    grad_fr = jnp.concatenate([fk_r1[:, wide:], fk_r2[:, wide:]], axis=1).astype(F32)
    grad_fv = out_v.value.reshape(hid, D).astype(F32)
    grad_o, grad_r = [wide_out(out_or.value, i).astype(F32) for i in range(2)]
    grad_k, grad_v = [wide_out(out_kv.value, i).astype(F32) for i in range(2)]
    rows = lax.dynamic_slice_in_dim(small[:11], my_dp * shard, shard, 1)
    rms = jnp.sqrt(small[11, :3] / (jnp.sum(lengths).astype(F32) * D))
    v = [rows[i] for i in range(11)]
    return (
        block_out, input_grad,
        v[0], v[1], v[2], v[3], v[4], v[5], v[6],
        grad_k, grad_v, grad_r, grad_o,
        v[7], v[8], v[9], v[10],
        grad_fk, grad_fr, grad_fv,
        rms[0], rms[1], rms[2],
    )


def solution(mesh):
    dp_axes, seq_axes = axes_of("d", mesh.shape["dp"]), axes_of("s", mesh.shape["seq"])
    names = dp_axes + seq_axes
    fine = jax.sharding.Mesh(mesh.devices.reshape((2,) * len(names)), names)
    big, vec, mat = P(dp_axes, seq_axes, None), P(dp_axes), P(dp_axes, None)
    args = (big, big, P(), P()) + (vec,) * 7 + (mat,) * 4 + (vec,) * 4 + (mat,) * 3
    outs = (big, big) + (vec,) * 7 + (mat,) * 4 + (vec,) * 4 + (mat,) * 3 + (P(),) * 3
    return jax.shard_map(
        functools.partial(per_device, dp_axes, seq_axes),
        mesh=fine, in_specs=args, out_specs=outs, check_vma=False,
    )
```

```python
import functools

import jax
import jax.numpy as jnp
from jax import lax
from jax.experimental import pallas as pl
from jax.experimental.layout import Layout, with_layout_constraint
from jax.experimental.pallas import tpu as pltpu
from jax.sharding import PartitionSpec as P

D = 1024
EPS = 1e-05
F32 = jnp.float32
BF16 = jnp.bfloat16


LIGHT = pl.CostEstimate(flops=1 << 20, bytes_accessed=1 << 16, transcendentals=0)


def axes_of(letter, size):
    return tuple(f"{letter}{bit}" for bit in reversed(range(size.bit_length() - 1)))


def swap(value, key):
    return lax.ppermute(value, key, [(0, 1), (1, 0)])


def place(held, key):
    rank = lambda k: (k[0] == "s", -int(k[1:]))
    return sum(1 for other in held if rank(other) < rank(key))


def join(mine, other, key, at):
    first = lax.axis_index(key) == 0
    return jnp.stack(
        [jnp.where(first, mine, other), jnp.where(first, other, mine)], axis=at
    )


def half(value, which, at):
    return lax.dynamic_index_in_dim(value, which, at, keepdims=False)


def add_low(mine, other):
    return (mine.astype(F32) + other.astype(F32)).astype(BF16)


def tie(*values):
    return lax.optimization_barrier(values)


def row_major(value):
    return with_layout_constraint(value, Layout(tuple(range(value.ndim))))


class Moving:
    def start(self, key):
        self.prepare(key)
        self.go()

    def go(self):
        self.got = swap(self.send, self.key)

    def finish(self):
        pass


class Plain(Moving):
    def __init__(self, value, key):
        self.send, self.key = value, key


class Growing(Moving):
    def __init__(self, value):
        self.value, self.held = value, []

    def prepare(self, key):
        self.key, self.send = key, self.value

    def finish(self):
        at = place(self.held, self.key)
        self.held.append(self.key)
        self.value = join(self.value, self.got, self.key, at)


class Shrinking(Moving):
    def __init__(self, parts, merge, held):
        self.parts, self.merge, self.held = parts, merge, list(held)

    def prepare(self, key):
        self.key = key
        self.held.remove(key)
        self.at = place(self.held, key)
        self.bit = lax.axis_index(key)
        self.send = self.merge([half(p, 1 - self.bit, self.at) for p in self.parts])

    def finish(self):
        self.value = add_low(self.merge([half(p, self.bit, self.at) for p in self.parts]), self.got)
        self.parts, self.merge = [self.value], only


class Summing(Moving):
    def __init__(self, value):
        self.value = value

    def prepare(self, key):
        self.key, self.send = key, self.value

    def finish(self):
        self.value = self.value + self.got


def fire(items, *others):
    tied = tie(*[item.send for item in items], *others)
    for item, send in zip(items, tied):
        item.send = send
        item.go()
    return tied[len(items) :]


def only(parts):
    (part,) = parts
    return part


def stacked(parts):
    return jnp.stack(parts, axis=-3)


def settle(items, *others):
    tied = tie(*[item.got for item in items], *others)
    for item, got in zip(items, tied):
        item.got = got
        item.finish()
    return tied[len(items) :]


ROWS = 8


def fwd_kernel(k_ref, v_ref, r_ref, rate_ref, u_ref, a0_ref, b0_ref, w_ref, a_ref, b_ref):
    rate = rate_ref[...]
    boost = jnp.exp(u_ref[...])
    width = rate.shape[1]
    row = lax.broadcasted_iota(jnp.int32, (ROWS, width), 0)
    rowf = row.astype(F32)
    falling = jnp.exp(-rowf * rate)
    one = jnp.exp(-rate)
    steps = [(s, jnp.where(row >= s, jnp.exp(-s * rate), 0.0)) for s in (1, 2, 4)]
    inner = row >= 1

    def scan(tile, carry):
        before = jnp.where(inner, pltpu.roll(tile, 1, 0), 0.0)
        for s, factor in steps:
            before = before + factor * pltpu.roll(before, s, 0)
        before = before + falling * carry
        after = one * before[ROWS - 1 :, :] + tile[ROWS - 1 :, :]
        return before, after

    def tile_of(key, val, recept, carry):
        num, den = carry
        power = jnp.exp(key)
        num_before, num = scan(power * val, num)
        den_before, den = scan(power, den)
        now = boost * power
        mixed = (num_before + now * val) / (den_before + now)
        return (jax.nn.sigmoid(recept) * mixed, num_before, den_before), (num, den)

    def body(i, carry):
        at = pl.ds(pl.multiple_of(i * (2 * ROWS), 2 * ROWS), 2 * ROWS)
        key, val, recept = k_ref[at, :], v_ref[at, :].astype(F32), r_ref[at, :].astype(F32)
        low, carry = tile_of(key[:ROWS], val[:ROWS], recept[:ROWS], carry)
        high, carry = tile_of(key[ROWS:], val[ROWS:], recept[ROWS:], carry)
        for ref, a, b in zip((w_ref, a_ref, b_ref), low, high):
            ref[at, :] = jnp.concatenate([a, b], axis=0).astype(ref.dtype)
        return carry

    lax.fori_loop(
        0, k_ref.shape[0] // (2 * ROWS), body, (a0_ref[...], b0_ref[...]), unroll=2
    )


def bwd_kernel(
    k_ref, v_ref, a_ref, b_ref, p_ref, rate_ref, u_ref, ga_ref, gb_ref,
    dk_ref, dv_ref, first_ref, decay_ref,
):
    rate = rate_ref[...]
    boost = jnp.exp(u_ref[...])
    width = rate.shape[1]
    row = lax.broadcasted_iota(jnp.int32, (ROWS, width), 0)
    rowf = row.astype(F32)
    trailing = jnp.exp(-(ROWS - 1.0 - rowf) * rate)
    one = jnp.exp(-rate)
    steps = [(s, jnp.where(row < ROWS - s, jnp.exp(-s * rate), 0.0)) for s in (1, 2, 4)]
    inner = row < ROWS - 1

    def scan(tile, carry):
        later = jnp.where(inner, pltpu.roll(tile, ROWS - 1, 0), 0.0)
        for s, factor in steps:
            later = later + factor * pltpu.roll(later, ROWS - s, 0)
        later = later + trailing * carry
        before = one * later[:1, :] + tile[:1, :]
        return later, before

    def tile_of(tiles, carry):
        num, den, first, decay = carry
        key, val, num_before, den_before, p = tiles
        power = jnp.exp(key)
        now = boost * power
        q = -p * (num_before + now * val) / (den_before + now)
        num_later, num = scan(p, num)
        den_later, den = scan(q, den)
        diagonal = now * (val * p + q)
        d_key = power * (val * num_later + den_later) + diagonal
        d_val = power * num_later + now * p
        first = first + diagonal
        decay = decay + (num_later * num_before + den_later * den_before)
        return (d_key, d_val), (num, den, first, decay)

    count = k_ref.shape[0] // (2 * ROWS)

    def body(i, carry):
        at = pl.ds(pl.multiple_of((count - 1 - i) * (2 * ROWS), 2 * ROWS), 2 * ROWS)
        tiles = [ref[at, :].astype(F32) for ref in (k_ref, v_ref, a_ref, b_ref, p_ref)]
        high, carry = tile_of([tile[ROWS:] for tile in tiles], carry)
        low, carry = tile_of([tile[:ROWS] for tile in tiles], carry)
        for ref, a, b in zip((dk_ref, dv_ref), low, high):
            ref[at, :] = jnp.concatenate([a, b], axis=0).astype(BF16)
        return carry

    zero = jnp.zeros((ROWS, width), F32)
    done = lax.fori_loop(0, count, body, (ga_ref[...], gb_ref[...], zero, zero), unroll=2)
    first_ref[...] = done[2]
    decay_ref[...] = done[3]


def share_kernel(
    da_ref, w_ref, k_ref, v_ref, r_ref, a_ref, b_ref, rate_ref, u_ref,
    p_ref, dr_ref, ga_ref, gb_ref, dw_ref,
):
    dw_ref[...] = lax.dot_general(
        da_ref[...], w_ref[...], (((1,), (1,)), ((), ())), preferred_element_type=F32
    )
    rate = rate_ref[...]
    boost = jnp.exp(u_ref[...])
    rows = 2 * ROWS
    rowf = lax.broadcasted_iota(jnp.int32, (rows, rate.shape[1]), 0).astype(F32)
    near = jnp.exp(-rowf * rate)

    def body(i, carry):
        ga, gb = carry
        at = pl.ds(pl.multiple_of(i * rows, rows), rows)
        now = boost * jnp.exp(k_ref[at, :])
        inverse = 1.0 / (b_ref[at, :].astype(F32) + now)
        mixed = (a_ref[at, :].astype(F32) + now * v_ref[at, :].astype(F32)) * inverse
        gate = jax.nn.sigmoid(r_ref[at, :].astype(F32))
        d_mixed = dw_ref[at, :] * gate
        dr_ref[at, :] = (d_mixed * mixed * (1.0 - gate)).astype(BF16)
        p_low = (d_mixed * inverse).astype(BF16)
        p_ref[at, :] = p_low
        p = p_low.astype(F32)
        q = -p * mixed
        fall = near * jnp.exp(-(i * rows).astype(F32) * rate)
        return ga + fall * p, gb + fall * q

    zero = jnp.zeros((rows, rate.shape[1]), F32)
    ga, gb = lax.fori_loop(0, k_ref.shape[0] // rows, body, (zero, zero), unroll=2)
    ga_ref[...] = ga[:ROWS] + ga[ROWS:]
    gb_ref[...] = gb[:ROWS] + gb[ROWS:]


WIDTH = 256


def wkv_specs(rows):
    big = pl.BlockSpec((rows, WIDTH), lambda s, c: (s, c))
    row = pl.BlockSpec((1, WIDTH), lambda s, c: (0, c))
    state = pl.BlockSpec((None, 1, WIDTH), lambda s, c: (s, 0, c))
    partial = pl.BlockSpec((None, ROWS, WIDTH), lambda s, c: (s, 0, c))
    return big, row, state, partial


def wkv_forward(keys, vals, recepts, rate, first, num, den, seqs):
    total = keys.shape[0]
    big, row, state, _ = wkv_specs(total // seqs)
    cells = total * D
    return pl.pallas_call(
        fwd_kernel,
        grid=(seqs, D // WIDTH),
        in_specs=[big, big, big, row, row, state, state],
        out_specs=[big, big, big],
        out_shape=[
            jax.ShapeDtypeStruct((total, D), BF16),
            jax.ShapeDtypeStruct((total, D), F32),
            jax.ShapeDtypeStruct((total, D), F32),
        ],
        compiler_params=pltpu.CompilerParams(vmem_limit_bytes=58 << 20),
        cost_estimate=LIGHT,
    )(keys, vals, recepts, rate, first, num, den)


def wkv_backward(keys, vals, num_before, den_before, p, rate, first, num, den, seqs):
    total = keys.shape[0]
    big, row, state, partial = wkv_specs(total // seqs)
    cells = total * D
    return pl.pallas_call(
        bwd_kernel,
        grid=(seqs, D // WIDTH),
        in_specs=[big, big, big, big, big, row, row, state, state],
        out_specs=[big, big, partial, partial],
        out_shape=[
            jax.ShapeDtypeStruct((total, D), BF16),
            jax.ShapeDtypeStruct((total, D), BF16),
            jax.ShapeDtypeStruct((seqs, ROWS, D), F32),
            jax.ShapeDtypeStruct((seqs, ROWS, D), F32),
        ],
        compiler_params=pltpu.CompilerParams(vmem_limit_bytes=58 << 20),
        cost_estimate=LIGHT,
    )(keys, vals, num_before, den_before, p, rate, first, num, den)


def share_back(d_attn, weight, keys, vals, recepts, num_before, den_before, rate, first, seqs):
    total = keys.shape[0]
    span = total // seqs
    big, row, _, partial = wkv_specs(span)
    cells = total * D
    return pl.pallas_call(
        share_kernel,
        grid=(seqs, D // WIDTH),
        in_specs=[
            pl.BlockSpec((span, D), lambda s, c: (s, 0)),
            pl.BlockSpec((WIDTH, D), lambda s, c: (c, 0)),
            big, big, big, big, big, row, row,
        ],
        out_specs=[big, big, partial, partial],
        out_shape=[
            jax.ShapeDtypeStruct((total, D), BF16),
            jax.ShapeDtypeStruct((total, D), BF16),
            jax.ShapeDtypeStruct((seqs, ROWS, D), F32),
            jax.ShapeDtypeStruct((seqs, ROWS, D), F32),
        ],
        scratch_shapes=[pltpu.VMEM((span, WIDTH), F32)],
        compiler_params=pltpu.CompilerParams(vmem_limit_bytes=58 << 20),
        cost_estimate=LIGHT,
    )(d_attn, weight, keys, vals, recepts, num_before, den_before, rate, first)


PIECES = 8


def load_pieces(refs, held, sems):
    left, right = refs[:4], refs[4:]
    per = PIECES // held.shape[0]
    width = held.shape[2] // per
    copies = []
    for p in range(4):
        for side, ref in enumerate((left[p], right[p % 2].at[p // 2])):
            i = 2 * p + side
            to = held.at[i // per, :, pl.ds((i % per) * width, width)]
            copies.append(pltpu.make_async_copy(ref, to, sems.at[i]))
    return copies


def feed_kernel(s_ref, left_ref, x_ref, *rest):
    refs = rest[:6]
    fv_ref, xr_ref, fr_ref, mid_ref, cot_ref = rest[6:11]
    sq_ref, out_ref, dval_ref, dgate_ref, sums = rest[11:16]
    held, held_v, acc, gate_acc, sems, sems_v = rest[16:]
    copies = load_pieces(refs, held, sems)
    deep = held_v.shape[1]
    copies_v = [
        pltpu.make_async_copy(fv_ref.at[pl.ds(h * deep, deep)], held_v.at[h], sems_v.at[h])
        for h in range(2)
    ]
    first = pl.program_id(0) == 0
    width = held.shape[2]

    @pl.when(first)
    def _():
        for copy in copies + copies_v:
            copy.start()

    for p in range(4):

        @pl.when(first)
        def _(p=p):
            copies[2 * p].wait()
            copies[2 * p + 1].wait()

        hidden = jnp.maximum(jnp.dot(x_ref[...], held[p], preferred_element_type=F32), 0.0)
        at = pl.multiple_of(jnp.bitwise_xor(s_ref[0], p) * width, width)
        sq_ref[:, pl.ds(at, width)] = (hidden * hidden).astype(BF16)

    gate_acc[...] = jnp.dot(xr_ref[...], fr_ref[...], preferred_element_type=F32)
    total = None
    for h in range(2):

        @pl.when(first)
        def _(h=h):
            copies_v[h].wait()

        part = jnp.dot(sq_ref[:, pl.ds(h * deep, deep)], held_v[h], preferred_element_type=F32)
        total = part if total is None else total + part
    acc[...] = total

    left = left_ref[pl.program_id(0)]
    sums[...] = jnp.zeros_like(sums)

    def body(i, _):
        start = pl.multiple_of(i * 2 * ROWS, 2 * ROWS)
        at = pl.ds(start, 2 * ROWS)
        rows = start + lax.broadcasted_iota(jnp.int32, (2 * ROWS, 1), 0)
        keep = rows < left
        gate = jax.nn.sigmoid(gate_acc[at, :])
        feed = jnp.where(keep, gate * acc[at, :], 0.0)
        result = jnp.where(keep, mid_ref[at, :], 0.0) + feed
        g = jnp.where(keep, cot_ref[at, :].astype(F32), 0.0)
        out_ref[at, :] = result.astype(BF16)
        dval_ref[at, :] = (g * gate).astype(BF16)
        dgate_ref[at, :] = (g * feed * (1.0 - gate)).astype(BF16)
        sums[0] += fold(result * result)
        sums[1] += fold(feed * feed)
        return 0

    lax.fori_loop(0, mid_ref.shape[0] // (2 * ROWS), body, 0, unroll=2)


def feed_forward(my_seq, left, inputs, pieces, weight, gate_inputs, gate_weight, middle, cotangent, seqs):
    total = inputs.shape[0]
    width = 2 * pieces[0].shape[1]
    span = total // seqs
    ff = 4 * width
    big = pl.BlockSpec((span, D), lambda i, *_: (i, 0))
    return pl.pallas_call(
        feed_kernel,
        grid_spec=pltpu.PrefetchScalarGridSpec(
            num_scalar_prefetch=2,
            grid=(seqs,),
            in_specs=[big]
            + [pl.BlockSpec(memory_space=pl.ANY)] * 7
            + [big, pl.BlockSpec((D, D), lambda i, *_: (0, 0), pipeline_mode=pl.Buffered(1)), big, big],
            out_specs=[
                pl.BlockSpec((span, ff), lambda i, *_: (i, 0)), big, big, big,
                pl.BlockSpec((None, 2, ROWS, D), lambda i, *_: (i, 0, 0, 0)),
            ],
            scratch_shapes=[
                pltpu.VMEM((4, D, width), BF16),
                pltpu.VMEM((2, 2 * width, D), BF16),
                pltpu.VMEM((span, D), F32),
                pltpu.VMEM((span, D), F32),
                pltpu.SemaphoreType.DMA((PIECES,)),
                pltpu.SemaphoreType.DMA((2,)),
            ],
        ),
        out_shape=[
            jax.ShapeDtypeStruct((total, ff), BF16),
            jax.ShapeDtypeStruct((total, D), BF16),
            jax.ShapeDtypeStruct((total, D), BF16),
            jax.ShapeDtypeStruct((total, D), BF16),
            jax.ShapeDtypeStruct((seqs, 2, ROWS, D), F32),
        ],
        compiler_params=pltpu.CompilerParams(vmem_limit_bytes=60 << 20),
        cost_estimate=LIGHT,
    )(my_seq[None], left, inputs, *pieces, weight, gate_inputs, gate_weight, middle, cotangent)


CHUNK = 128


def stats_of(values):
    centre = values - jnp.mean(values, axis=-1, keepdims=True)
    inverse = lax.rsqrt(jnp.mean(centre * centre, axis=-1, keepdims=True) + EPS)
    return centre * inverse, inverse


def norm_back(grads, normed, inverse):
    return inverse * (
        grads
        - jnp.mean(grads, axis=-1, keepdims=True)
        - normed * jnp.mean(grads * normed, axis=-1, keepdims=True)
    )


def fold(values):
    return jnp.sum(values.reshape(values.shape[0] // ROWS, ROWS, values.shape[1]), axis=0)


def next_rows(values, carry):
    last = lax.broadcasted_iota(jnp.int32, values.shape, 0) == CHUNK - 1
    return jnp.where(last, carry, pltpu.roll(values, CHUNK - 1, 0))


def previous_rows(values, carry):
    first = lax.broadcasted_iota(jnp.int32, values.shape, 0) == 0
    return jnp.where(first, carry, pltpu.roll(values, 1, 0))


def mid_kernel(
    left_ref, w_ref, weight_ref, x_ref, gain_ref, bias_ref, mk_ref, mr_ref,
    mid_ref, fk_ref, fr_ref, first_ref, sq_ref,
):
    mid_ref[...] = jnp.dot(w_ref[...], weight_ref[...], preferred_element_type=F32)
    left = left_ref[pl.program_id(0)]
    gain, bias, mix_k, mix_r = gain_ref[...], bias_ref[...], mk_ref[...], mr_ref[...]
    sq_ref[...] = jnp.zeros_like(sq_ref)

    def body(i, carry):
        start = pl.multiple_of(i * CHUNK, CHUNK)
        at = pl.ds(start, CHUNK)
        attn = mid_ref[at, :]
        rows = start + lax.broadcasted_iota(jnp.int32, (CHUNK, 1), 0)
        sq_ref[...] += fold(jnp.where(rows < left, attn * attn, 0.0))
        middle = x_ref[at, :].astype(F32) + attn
        mid_ref[at, :] = middle
        b = stats_of(middle)[0] * gain + bias
        before = previous_rows(b, carry)
        fk_ref[at, :] = (b * mix_k + before * (1.0 - mix_k)).astype(BF16)
        fr_ref[at, :] = (b * mix_r + before * (1.0 - mix_r)).astype(BF16)

        @pl.when(i == 0)
        def _():
            first_ref[...] = b[:1, :]

        return b[CHUNK - 1 :, :]

    lax.fori_loop(0, x_ref.shape[0] // CHUNK, body, jnp.zeros_like(gain), unroll=2)


def mid_forward(left, weighted, weight, tokens, gain, bias, mix_k, mix_r, seqs):
    total = tokens.shape[0]
    span = total // seqs
    big = pl.BlockSpec((span, D), lambda s, _: (s, 0))
    row = pl.BlockSpec((1, D), lambda s, _: (0, 0))
    tile = lambda rows: pl.BlockSpec((None, rows, D), lambda s, _: (s, 0, 0))
    return pl.pallas_call(
        mid_kernel,
        grid_spec=pltpu.PrefetchScalarGridSpec(
            num_scalar_prefetch=1,
            grid=(seqs,),
            in_specs=[big, pl.BlockSpec((D, D), lambda s, _: (0, 0)), big, row, row, row, row],
            out_specs=[big, big, big, tile(1), tile(ROWS)],
        ),
        out_shape=[
            jax.ShapeDtypeStruct((total, D), F32),
            jax.ShapeDtypeStruct((total, D), BF16),
            jax.ShapeDtypeStruct((total, D), BF16),
            jax.ShapeDtypeStruct((seqs, 1, D), F32),
            jax.ShapeDtypeStruct((seqs, ROWS, D), F32),
        ],
        compiler_params=pltpu.CompilerParams(vmem_limit_bytes=58 << 20),
        cost_estimate=LIGHT,
    )(left, weighted, weight, tokens, gain, bias, mix_k, mix_r)


def down_kernel(s_ref, left_ref, dval_ref, fv_ref, sq_ref, *rest):
    refs = rest[:6]
    gate_ref, fr_ref, mid_ref, cot_ref, gain_ref, bias_ref, mk_ref, mr_ref = rest[6:14]
    dh_ref, out_ref, low_ref, first_k, first_r, tail_ref, sums = rest[14:21]
    held, held_v, acc_k, acc_r, sems, sems_v = rest[21:]
    copies = load_pieces(refs, held, sems)
    width = held_v.shape[1]
    places = [pl.multiple_of(jnp.bitwise_xor(s_ref[0], p) * width, width) for p in range(4)]
    copies_v = [
        pltpu.make_async_copy(fv_ref.at[pl.ds(places[p], width)], held_v.at[p], sems_v.at[p])
        for p in range(4)
    ]
    first = pl.program_id(0) == 0
    back = (((1,), (1,)), ((), ()))

    @pl.when(first)
    def _():
        for copy in copies_v + copies:
            copy.start()

    for p in range(4):

        @pl.when(first)
        def _(p=p):
            copies_v[p].wait()

        for side in range(2):
            part = pl.ds(side * (width // 2), width // 2)
            d_sq = lax.dot_general(dval_ref[...], held_v[p, part, :], back, preferred_element_type=F32)
            at = pl.multiple_of(places[p] + side * (width // 2), width // 2)
            squared = sq_ref[:, pl.ds(at, width // 2)].astype(F32)
            twice = 2.0 * squared * lax.rsqrt(jnp.maximum(squared, 1e-37))
            dh_ref[p, :, part] = (twice * d_sq).astype(BF16)

    acc_r[...] = lax.dot_general(gate_ref[...], fr_ref[...], back, preferred_element_type=F32)
    for h in range(2):

        @pl.when(first)
        def _(h=h):
            for copy in copies[4 * h : 4 * h + 4]:
                copy.wait()

        part = lax.dot_general(
            jnp.concatenate([dh_ref[2 * h], dh_ref[2 * h + 1]], axis=1), held[h],
            back, preferred_element_type=F32,
        )
        acc_k[...] = part if h == 0 else acc_k[...] + part

    left = left_ref[pl.program_id(0)]
    gain, bias, mix_k, mix_r = gain_ref[...], bias_ref[...], mk_ref[...], mr_ref[...]
    sums[...] = jnp.zeros_like(sums)
    count = mid_ref.shape[0] // CHUNK

    def body(i, carry):
        later_k, later_r = carry
        start = pl.multiple_of((count - 1 - i) * CHUNK, CHUNK)
        at = pl.ds(start, CHUNK)
        d_fk, d_fr = acc_k[at, :], acc_r[at, :]
        next_k, next_r = next_rows(d_fk, later_k), next_rows(d_fr, later_r)
        n, inverse = stats_of(mid_ref[at, :])
        b = n * gain + bias
        db = d_fk * mix_k + next_k * (1.0 - mix_k) + d_fr * mix_r + next_r * (1.0 - mix_r)
        sums[0] += fold(b * (d_fk - next_k))
        sums[1] += fold(b * (d_fr - next_r))
        sums[2] += fold(n * db)
        sums[3] += fold(db)
        rows = start + lax.broadcasted_iota(jnp.int32, (CHUNK, 1), 0)
        g = jnp.where(rows < left, cot_ref[at, :].astype(F32), 0.0)
        d_middle = g + norm_back(db * gain, n, inverse)
        out_ref[at, :] = d_middle
        low_ref[at, :] = d_middle.astype(BF16)

        @pl.when(i == 0)
        def _():
            tail_ref[0] = d_middle[CHUNK - 1 :, :]
            tail_ref[1] = n[CHUNK - 1 :, :]
            tail_ref[2] = jnp.broadcast_to(inverse[CHUNK - 1 :, :], gain.shape)

        return d_fk[:1, :], d_fr[:1, :]

    zero = jnp.zeros_like(gain)
    first_k[...], first_r[...] = lax.fori_loop(0, count, body, (zero, zero), unroll=2)


def down(
    my_seq, left, grads, weight, squared, pieces, gate_grads, gate_weight,
    middle, cotangent, gain, bias, mix_k, mix_r, seqs,
):
    total, ff = squared.shape
    span = total // seqs
    width = ff // 4
    big = pl.BlockSpec((span, D), lambda s, *_: (s, 0))
    alone = pl.BlockSpec((span, D), lambda s, *_: (s, 0), pipeline_mode=pl.Buffered(1))
    row = pl.BlockSpec((1, D), lambda s, *_: (0, 0))
    one = pl.BlockSpec((None, 1, D), lambda s, *_: (s, 0, 0))
    return pl.pallas_call(
        down_kernel,
        grid_spec=pltpu.PrefetchScalarGridSpec(
            num_scalar_prefetch=2,
            grid=(seqs,),
            in_specs=[
                big,
                pl.BlockSpec(memory_space=pl.ANY),
                pl.BlockSpec((span, ff), lambda s, *_: (s, 0), pipeline_mode=pl.Buffered(1)),
            ]
            + [pl.BlockSpec(memory_space=pl.ANY)] * 6
            + [big, pl.BlockSpec((D, D), lambda s, *_: (0, 0), pipeline_mode=pl.Buffered(1)), alone, big]
            + [row] * 4,
            out_specs=[
                pl.BlockSpec((4, span, width), lambda s, *_: (0, s, 0)),
                big, big, one, one,
                pl.BlockSpec((None, 3, 1, D), lambda s, *_: (s, 0, 0, 0)),
                pl.BlockSpec((None, 4, ROWS, D), lambda s, *_: (s, 0, 0, 0)),
            ],
            scratch_shapes=[
                pltpu.VMEM((2, D, 2 * width), BF16),
                pltpu.VMEM((4, width, D), BF16),
                pltpu.VMEM((span, D), F32),
                pltpu.VMEM((span, D), F32),
                pltpu.SemaphoreType.DMA((PIECES,)),
                pltpu.SemaphoreType.DMA((4,)),
            ],
        ),
        out_shape=[
            jax.ShapeDtypeStruct((4, total, width), BF16),
            jax.ShapeDtypeStruct((total, D), F32),
            jax.ShapeDtypeStruct((total, D), BF16),
            jax.ShapeDtypeStruct((seqs, 1, D), F32),
            jax.ShapeDtypeStruct((seqs, 1, D), F32),
            jax.ShapeDtypeStruct((seqs, 3, 1, D), F32),
            jax.ShapeDtypeStruct((seqs, 4, ROWS, D), F32),
        ],
        compiler_params=pltpu.CompilerParams(vmem_limit_bytes=60 << 20),
        cost_estimate=LIGHT,
    )(
        my_seq[None], left, grads, weight, squared, *pieces, gate_grads, gate_weight,
        middle, cotangent, gain, bias, mix_k, mix_r,
    )


def mix_kernel(
    dk_ref, dv_ref, dr_ref, wk_ref, wv_ref, wr_ref, x_ref, dm_ref,
    gain_ref, bias_ref, mk_ref, mv_ref, mr_ref,
    out_ref, firsts, tail_ref, sums, acc,
):
    for i, (grads, weight) in enumerate(((dk_ref, wk_ref), (dv_ref, wv_ref), (dr_ref, wr_ref))):
        acc[i] = lax.dot_general(
            grads[...], weight[...], (((1,), (1,)), ((), ())), preferred_element_type=F32
        )
    gain, bias = gain_ref[...], bias_ref[...]
    mixes = (mk_ref[...], mv_ref[...], mr_ref[...])
    sums[...] = jnp.zeros_like(sums)
    count = x_ref.shape[0] // CHUNK

    def body(i, carry):
        start = pl.multiple_of((count - 1 - i) * CHUNK, CHUNK)
        at = pl.ds(start, CHUNK)
        n, inverse = stats_of(x_ref[at, :].astype(F32))
        a = n * gain + bias
        da, heads = None, []
        for j in range(3):
            d = acc[j, at, :]
            later = next_rows(d, carry[j])
            sums[j] += fold(a * (d - later))
            part = d * mixes[j] + later * (1.0 - mixes[j])
            da = part if da is None else da + part
            heads.append(d[:1, :])
        sums[3] += fold(n * da)
        sums[4] += fold(da)
        total = dm_ref[at, :] + norm_back(da * gain, n, inverse)
        out_ref[at, :] = total.astype(BF16)

        @pl.when(i == 0)
        def _():
            tail_ref[0] = total[CHUNK - 1 :, :]
            tail_ref[1] = n[CHUNK - 1 :, :]
            tail_ref[2] = jnp.broadcast_to(inverse[CHUNK - 1 :, :], gain.shape)

        return tuple(heads)

    zero = jnp.zeros_like(gain)
    heads = lax.fori_loop(0, count, body, (zero, zero, zero), unroll=2)
    for j in range(3):
        firsts[j] = heads[j]


def mix_back(d_keys, d_vals, d_recepts, w_k, w_v, w_r, tokens, d_middle, gain, bias, mix_k, mix_v, mix_r, seqs):
    total = tokens.shape[0]
    span = total // seqs
    big = pl.BlockSpec((span, D), lambda s: (s, 0))
    row = pl.BlockSpec((1, D), lambda s: (0, 0))
    full = pl.BlockSpec((D, D), lambda s: (0, 0))
    return pl.pallas_call(
        mix_kernel,
        grid=(seqs,),
        in_specs=[big, big, big, full, full, full, big, big] + [row] * 5,
        out_specs=[
            big,
            pl.BlockSpec((None, 3, 1, D), lambda s: (s, 0, 0, 0)),
            pl.BlockSpec((None, 3, 1, D), lambda s: (s, 0, 0, 0)),
            pl.BlockSpec((None, 5, ROWS, D), lambda s: (s, 0, 0, 0)),
        ],
        out_shape=[
            jax.ShapeDtypeStruct((total, D), BF16),
            jax.ShapeDtypeStruct((seqs, 3, 1, D), F32),
            jax.ShapeDtypeStruct((seqs, 3, 1, D), F32),
            jax.ShapeDtypeStruct((seqs, 5, ROWS, D), F32),
        ],
        scratch_shapes=[pltpu.VMEM((3, span, D), F32)],
        compiler_params=pltpu.CompilerParams(vmem_limit_bytes=58 << 20),
        cost_estimate=LIGHT,
    )(d_keys, d_vals, d_recepts, w_k, w_v, w_r, tokens, d_middle, gain, bias, mix_k, mix_v, mix_r)


def put_rows(values, rows, at):
    seqs = rows.shape[0]
    whole = values.reshape(seqs, values.shape[0] // seqs, D)
    return lax.dynamic_update_slice(whole, rows.astype(values.dtype), (0, at, 0)).reshape(values.shape)


def cut_kernel(_, k, v, r, o, fk1, fk2, kv_out, ro_out, f1_out, f2_out):
    kv_out[0], kv_out[1] = k[...], v[...]
    ro_out[0], ro_out[1] = r[...], o[...]
    f1_out[...], f2_out[...] = fk1[...], fk2[...]


def cut(my_seq, quarter, key, value, recept, output, feed_key):
    shard, ff = feed_key.shape
    part = pl.BlockSpec((quarter, D), lambda i, at: (at[0], 0))
    side = lambda which: pl.BlockSpec((shard, ff // PIECES), lambda i, at: (0, 2 * at[0] + which))
    full = lambda *shape: pl.BlockSpec(shape, lambda i, at: (0,) * len(shape))
    shapes = [(2, quarter, D), (2, quarter, D)] + [(shard, ff // PIECES)] * 2
    return pl.pallas_call(
        cut_kernel,
        grid_spec=pltpu.PrefetchScalarGridSpec(
            num_scalar_prefetch=1,
            grid=(1,),
            in_specs=[part] * 4 + [side(0), side(1)],
            out_specs=[full(*shape) for shape in shapes],
        ),
        out_shape=[jax.ShapeDtypeStruct(shape, BF16) for shape in shapes],
    )(my_seq[None], key, value, recept, output, feed_key, feed_key)


def dot(left, right):
    return jnp.dot(left, right, preferred_element_type=F32)


def dot_back(grads, weight):
    return lax.dot_general(grads, weight, (((1,), (1,)), ((), ())), preferred_element_type=F32)


def dot_weight(inputs, grads):
    return lax.dot_general(inputs, grads, (((0,), (0,)), ((), ())), preferred_element_type=F32)


def normalize(values):
    centre = values - jnp.mean(values, axis=-1, keepdims=True)
    spread = jnp.mean(centre * centre, axis=-1, keepdims=True)
    inverse = lax.rsqrt(spread + EPS)
    return centre * inverse, inverse


def from_behind(value, axes, by):
    count = lax.axis_size(axes)
    pairs = [(i, i + by) for i in range(count) if 0 <= i + by < count]
    return lax.ppermute(value, axes, pairs)


def shifted(rows, edge):
    return jnp.concatenate([edge, rows[:, :-1]], axis=1)


def pulled(rows, edge):
    return jnp.concatenate([rows[:, 1:], edge], axis=1)


def blend(now, before, share):
    return (now * share + before * (1.0 - share)).astype(BF16)


def earlier_state(decay, num, den, axes, backward):
    count = lax.axis_size(axes)
    mine = lax.axis_index(axes)
    packed = lax.all_gather(jnp.concatenate([num, den], axis=0), axes)
    seqs = num.shape[0]
    state = jnp.zeros_like(packed[0])
    for hop in range(count - 1):
        source = count - 1 - hop if backward else hop
        longer = decay * state + packed[source]
        keep = source > mine if backward else source < mine
        state = jnp.where(keep, longer, state)
    return state[:seqs, None, :], state[seqs:, None, :]


def per_device(
    dp_axes, seq_axes,
    tokens, cotangent, lengths, assignment,
    mix_norm_gain, mix_norm_bias, shift_key, shift_value, shift_recept, time_decay, time_first,
    key_weight, value_weight, recept_weight, output_weight,
    feed_norm_gain, feed_norm_bias, feed_shift_key, feed_shift_recept,
    feed_key_weight, feed_recept_weight, feed_value_weight,
):
    seqs, span, _ = tokens.shape
    total = seqs * span
    dp, seq = lax.axis_size(dp_axes), lax.axis_size(seq_axes)
    my_dp, my_seq = lax.axis_index(dp_axes), lax.axis_index(seq_axes)
    every = dp_axes + seq_axes
    z_axes, x = dp_axes[:-1], dp_axes[-1]
    y, c = seq_axes
    ff = feed_key_weight.shape[1]
    flat = lambda v: v.reshape(total, v.shape[-1])
    deep = lambda v: v.reshape(seqs, span, v.shape[-1])

    shard = D // dp
    quarter = shard // seq

    def own_rows(weight):
        return lax.dynamic_slice_in_dim(weight, my_seq * quarter, quarter, 0)

    hid = feed_value_weight.shape[0]
    kv, ro, f1, f2 = [
        Growing(part)
        for part in cut(
            my_seq, quarter, key_weight, value_weight, recept_weight, output_weight,
            feed_key_weight,
        )
    ]
    kv.start(z_axes[0])
    ro.start(z_axes[0])
    kv.value, tokens, *vectors = tie(
        kv.value, tokens,
        mix_norm_gain, mix_norm_bias, shift_key, shift_value, shift_recept, time_decay, time_first,
        feed_norm_gain, feed_norm_bias, feed_shift_key, feed_shift_recept,
    )
    vectors = Growing(jnp.stack(vectors))
    vectors.start(z_axes[0])
    edge1 = from_behind(tokens[:, -1:], seq_axes, 1)
    for z in z_axes[1:]:
        settle([kv, ro, vectors])
        kv.start(z)
        ro.start(z)
        vectors.start(z)
    f1.value, f2.value = settle([kv, ro, vectors], f1.value, f2.value)
    kv.start(x)
    ro.start(y)
    vectors.start(x)
    f1.start(z_axes[0])
    f2.start(z_axes[0])
    halves = lambda w: half(w.reshape(2, w.shape[0] // 2, D), lax.axis_index(c), 0)
    gathered = lambda w: lax.all_gather(w, dp_axes + (c,), axis=0, tiled=True)
    (fr_part,) = settle([kv, ro, vectors, f1, f2], halves(feed_recept_weight))
    w_fr = gathered(fr_part)
    kv.start(y)
    ro.start(x)
    for z in z_axes[1:]:
        f1.start(z)
        f2.start(z)
        if z != z_axes[-1]:
            settle([f1, f2])
    (fv_part,) = settle([f1, f2, kv, ro], halves(feed_value_weight))
    w_fv = gathered(fv_part)
    kv.start(c)
    ro.start(c)
    f1.start(x)
    f2y = swap(f2.value, y)
    (f2y,) = settle([kv, ro, f1], f2y)
    pick = lambda v, i: jnp.moveaxis(v, -3, 0)[i].reshape(D, D)
    w_k, w_v, w_r, w_o = pick(kv.value, 0), pick(kv.value, 1), pick(ro.value, 0), pick(ro.value, 1)
    f1_0 = row_major(f1.value).reshape(D, -1)
    f2.value = jnp.stack([f2.value, f2y], axis=len(f2.held))

    vectors = jnp.swapaxes(vectors.value.reshape(dp, 11, D // dp), 0, 1).reshape(11, D).astype(F32)
    gain1, bias1, mix_k, mix_v, mix_r, log_rate, first, gain2, bias2, fmix_k, fmix_r = [
        vectors[i : i + 1] for i in range(11)
    ]
    rate = jnp.exp(log_rate)
    lam = jnp.exp(-rate)

    slot_ids = jnp.arange(assignment.shape[0])
    my_slots = my_dp * seqs + jnp.arange(seqs)
    seq_ids = jnp.sum(jnp.where(slot_ids[None, :] == my_slots[:, None], assignment[None, :], 0), axis=1)
    my_lens = jnp.sum(jnp.where(slot_ids[None, :] == seq_ids[:, None], lengths[None, :], 0), axis=1)
    positions = my_seq * span + jnp.arange(span)
    valid = flat((positions[None, :] < my_lens[:, None]).astype(F32)[..., None])
    inside = (my_seq > 0).astype(F32)

    xin = tokens.astype(F32)
    edge1 = (normalize(edge1.astype(F32))[0] * gain1 + bias1) * inside
    n1, inv1 = normalize(xin)
    a = n1 * gain1 + bias1
    a_prev = shifted(a, edge1)
    key_in = flat(blend(a, a_prev, mix_k))
    value_in = flat(blend(a, a_prev, mix_v))
    recept_in = flat(blend(a, a_prev, mix_r))
    keys = dot(key_in, w_k)
    vals = dot(value_in, w_v)
    recepts = dot(recept_in, w_r)

    offsets = jnp.arange(span).astype(F32)[:, None]
    power = deep(jnp.exp(keys))
    left = jnp.exp(-(span - 1.0 - offsets) * rate)
    span_decay = jnp.exp(-span * rate)
    num_end = jnp.sum(left * power * deep(vals), axis=1)
    vals, recepts = vals.astype(BF16), recepts.astype(BF16)
    den_end = jnp.sum(left * power, axis=1)
    num0, den0 = earlier_state(span_decay, num_end, den_end, seq_axes, False)
    f1_y = Plain(f1_0, y)
    f2.prepare(x)
    num0, den0 = fire([f1_y, f2], num0, den0)
    weighted, num_before, den_before = wkv_forward(keys, vals, recepts, rate, first, num0, den0, seqs)
    (weighted,) = settle([f1_y, f2], weighted)
    f1_y = f1_y.got
    f2_0 = row_major(jnp.moveaxis(f2.value, -3, 0)).reshape(2, D, -1)
    f1_c, f1_yc, f2_c = Plain(f1_0, c), Plain(f1_y, c), Plain(f2_0, c)
    (weighted,) = fire([f1_c, f1_yc, f2_c], weighted)
    last_row = tokens[:, -1].astype(F32) + dot(deep(weighted)[:, -1], w_o)
    edge2 = from_behind(last_row[:, None], seq_axes, 1)
    left_rows = (my_lens - my_seq * span).astype(jnp.int32)
    flat_tokens = flat(tokens)
    middle, feed_key_in, feed_recept_in, b_first, attn_sq = mid_forward(
        left_rows, weighted, w_o, flat_tokens, gain2, bias2, fmix_k, fmix_r, seqs
    )

    edge2 = (normalize(edge2)[0] * gain2 + bias2) * inside
    feed_key_in = put_rows(feed_key_in, blend(b_first, edge2, fmix_k), 0)
    feed_recept_in = put_rows(feed_recept_in, blend(b_first, edge2, fmix_r), 0)
    (feed_key_in,) = settle([f1_c, f1_yc, f2_c], feed_key_in)
    f1_c, f1_yc, f2_c = f1_c.got, f1_yc.got, f2_c.got
    pieces = (f1_0, f1_c, f1_y, f1_yc, f2_0, f2_c)
    sq, block_out, d_fval, d_fgate, squares = feed_forward(
        my_seq, left_rows, feed_key_in, pieces, w_fv, feed_recept_in, w_fr, middle, flat(cotangent), seqs
    )
    block_out = deep(block_out)
    stats = jnp.stack([jnp.sum(squares[:, 0]), jnp.sum(attn_sq), jnp.sum(squares[:, 1])])

    gfv = dot_weight(sq, d_fval).astype(BF16)
    gfv = lax.psum_scatter(gfv, dp_axes + (c,), scatter_dimension=0, tiled=True)
    gfr = dot_weight(feed_recept_in, d_fgate).astype(BF16)
    dh, d_middle, d_attn, first_k, first_r, tail, sums2 = down(
        my_seq, left_rows, d_fval, w_fv, sq, pieces, d_fgate, w_fr,
        middle, flat(cotangent), gain2, bias2, fmix_k, fmix_r, seqs,
    )
    gfk_1 = dot_weight(feed_key_in, dh[1]).astype(BF16)
    gfk_3 = dot_weight(feed_key_in, dh[3]).astype(BF16)

    lead = (2,) * len(every)
    split = lambda g_: Shrinking([g_.reshape(lead + (quarter, D))], only, every)
    side = ff // PIECES
    got_1, got_3 = Plain(gfk_1, c), Plain(gfk_3, c)
    (dh,) = fire([got_1, got_3], dh)
    gfk_0 = dot_weight(feed_key_in, dh[0]).astype(BF16)
    gfk_2 = dot_weight(feed_key_in, dh[2]).astype(BF16)
    edge3 = from_behind(first_k * (1.0 - fmix_k) + first_r * (1.0 - fmix_r), seq_axes, -1)
    d_middle, gfk_0, gfk_2, tail, sums2 = settle([got_1, got_3], d_middle, gfk_0, gfk_2, tail, sums2)
    low = lambda mine, got, at: add_low(mine[:, at : at + side], got.got[:, at : at + side])
    by_dp = lambda g_: g_.reshape((2,) * len(dp_axes) + (shard, g_.shape[1]))
    got_a = Plain(low(gfk_2, got_3, 0), y)
    r2 = Shrinking([by_dp(low(gfk_0, got_1, side)), by_dp(low(gfk_2, got_3, side))], stacked, dp_axes)
    r2.prepare(x)
    (d_attn,) = fire([got_a, r2], d_attn)
    a_0 = low(gfk_0, got_1, 0)

    d_last = tail[:, 0] + norm_back(edge3 * gain2, tail[:, 1], tail[:, 2])
    d_middle = put_rows(d_middle, d_last, span - 1)
    d_attn = put_rows(d_attn, d_last.astype(BF16), span - 1)
    small2 = sums2.sum((0, 2)) + jnp.concatenate(
        [
            -jnp.sum(edge2 * first_k, axis=0), -jnp.sum(edge2 * first_r, axis=0),
            jnp.sum(tail[:, 1] * edge3, axis=0), jnp.sum(edge3, axis=0),
        ]
    )
    p, d_recepts, ga_part, gb_part = share_back(
        d_attn, w_o, keys, vals, recepts, num_before, den_before, rate, first, seqs
    )
    r_o = dot_weight(weighted, d_attn).astype(BF16)
    r_r = dot_weight(recept_in, d_recepts).astype(BF16)
    ga_part, r_o, r_r = settle([r2, got_a], ga_part, r_o, r_r)

    orf = jnp.concatenate([r_o, r_r, gfr], axis=1)
    orf = lax.psum_scatter(orf, dp_axes + (c,), scatter_dimension=0, tiled=True)
    r1 = Shrinking([by_dp(add_low(a_0, got_a.got))], only, dp_axes)
    r1.prepare(x)
    b_got = Plain(r2.value[..., 1, :, :], y)
    ga0, gb0 = earlier_state(span_decay, ga_part.sum(1), gb_part.sum(1), seq_axes, True)
    ga0, gb0 = fire([r1, b_got], ga0, gb0)
    d_keys, d_vals, first_part, decay_part = wkv_backward(
        keys, vals, num_before, den_before, p, rate, first, ga0, gb0, seqs
    )
    d_keys, d_vals, gfv, first_part, decay_part = settle(
        [r1, b_got], d_keys, d_vals, gfv, first_part, decay_part
    )
    z1, z2 = z_axes[-1], z_axes[:-1]
    rows_of = lambda g_: g_.reshape(lead + (quarter, D))
    r_kv = Shrinking(
        [
            rows_of(dot_weight(key_in, d_keys).astype(BF16)),
            rows_of(dot_weight(value_in, d_vals).astype(BF16)),
        ],
        stacked, every,
    )
    r_kv.prepare(c)
    r_f = Shrinking([r1.value, add_low(r2.value[..., 0, :, :], b_got.got)], stacked, r1.held)
    r_f.prepare(z1)
    gfv_got = Plain(gfv, y)
    small2, first_part, decay_part = fire([r_kv, r_f, gfv_got], small2, first_part, decay_part)
    small2 = jnp.concatenate(
        [
            -(lam * rate) * jnp.sum(decay_part, axis=(0, 1))[None], jnp.sum(first_part, axis=(0, 1))[None],
            small2, jnp.pad(stats, (0, D - 3))[None],
        ]
    )
    d_keys, small2 = settle([r_kv, gfv_got], d_keys, small2)

    r_kv.prepare(y)
    out_v = Growing(add_low(gfv, gfv_got.got))
    out_v.prepare(c)
    d_keys, d_middle = fire([r_kv, out_v], d_keys, d_middle)
    mix_outs = mix_back(
        d_keys, d_vals, d_recepts, w_k, w_v, w_r, flat_tokens, d_middle,
        gain1, bias1, mix_k, mix_v, mix_r, seqs,
    )
    input_grad, firsts, tail1, sums1 = settle([r_kv, r_f, out_v], *mix_outs)

    r_kv.prepare(x)
    for z in reversed(z2):
        r_f.prepare(z)
        if z != z2[0]:
            r_f.go()
            settle([r_f])
    (firsts,) = fire([r_kv, r_f], firsts)
    mixes = (mix_k, mix_v, mix_r)
    edge4 = from_behind(sum(firsts[:, i] * (1.0 - m) for i, m in enumerate(mixes)), seq_axes, -1)
    input_last = (tail1[:, 0] + norm_back(edge4 * gain1, tail1[:, 1], tail1[:, 2])).astype(BF16)
    input_grad = deep(put_rows(input_grad, input_last, span - 1))
    small1 = sums1.sum((0, 2)) + jnp.concatenate(
        [
            -jnp.sum(edge1[:, None] * firsts, axis=(0, 2)),
            jnp.sum(tail1[:, 1] * edge4, axis=0), jnp.sum(edge4, axis=0),
        ]
    )

    small = jnp.concatenate([small1, small2])
    small, input_grad = settle([r_kv, r_f], small, input_grad)
    out_f = Growing(r_f.value)
    out_f.start(y)
    small = Summing(small)
    r_kv.start(z1)
    small.start(c)
    (orf,) = settle([r_kv, small, out_f], orf)
    out_f.start(c)
    for z in reversed(z2):
        r_kv.start(z)
        if z != z2[0]:
            settle([r_kv])
    small.start(y)
    orf_got = swap(orf, y)
    (orf_got,) = settle([r_kv, small, out_f], orf_got)
    orf = add_low(orf, orf_got)
    orf_c = swap(orf, c)
    own = r_kv.value
    small.start(x)
    at_y, at_c = swap(own, y), swap(own, c)
    at_both = lax.ppermute(own, (y, c), [(i, 3 - i) for i in range(4)])
    at_y, at_c, at_both, orf_c = settle([small], at_y, at_c, at_both, orf_c)
    for z in (z1, *reversed(z2)):
        small.start(z)
        small.finish()
    small = small.value
    out_kv = join(join(own, at_c, c, 0), join(at_y, at_both, c, 0), y, 0)

    wide_out = lambda v, i: v[:, :, i].reshape(shard, -1)
    out_f = out_f.value.reshape(2 * seq, shard, side)
    grad_fk = jnp.concatenate([out_f[i] for i in range(2 * seq)], axis=1).astype(F32)
    grad_fv = out_v.value.reshape(hid, D).astype(F32)
    orf = join(orf, orf_c, c, 0).reshape(shard, 3 * D).astype(F32)
    grad_o, grad_r, grad_fr = [orf[:, i * D : i * D + D] for i in range(3)]
    grad_k, grad_v = [wide_out(out_kv, i).astype(F32) for i in range(2)]
    rows = lax.dynamic_slice_in_dim(small[:11], my_dp * shard, shard, 1)
    rms = jnp.sqrt(small[11, :3] / (jnp.sum(lengths).astype(F32) * D))
    v = [rows[i] for i in range(11)]
    return (
        block_out, input_grad,
        v[3], v[4], v[0], v[1], v[2], v[5], v[6],
        grad_k, grad_v, grad_r, grad_o,
        v[9], v[10], v[7], v[8],
        grad_fk, grad_fr, grad_fv,
        rms[0], rms[1], rms[2],
    )


def solution(mesh):
    dp_axes, seq_axes = axes_of("d", mesh.shape["dp"]), axes_of("s", mesh.shape["seq"])
    names = dp_axes + seq_axes
    fine = jax.sharding.Mesh(mesh.devices.reshape((2,) * len(names)), names)
    big, vec, mat = P(dp_axes, seq_axes, None), P(dp_axes), P(dp_axes, None)
    args = (big, big, P(), P()) + (vec,) * 7 + (mat,) * 4 + (vec,) * 4 + (mat,) * 3
    outs = (big, big) + (vec,) * 7 + (mat,) * 4 + (vec,) * 4 + (mat,) * 3 + (P(),) * 3
    return jax.shard_map(
        functools.partial(per_device, dp_axes, seq_axes),
        mesh=fine, in_specs=args, out_specs=outs, check_vma=False,
    )
```

```python
import functools

import jax
import jax.numpy as jnp
from jax import lax
from jax.experimental import pallas as pl
from jax.experimental.layout import Layout, with_layout_constraint
from jax.experimental.pallas import tpu as pltpu
from jax.sharding import PartitionSpec as P

D = 1024
EPS = 1e-05
F32 = jnp.float32
BF16 = jnp.bfloat16


LIGHT = pl.CostEstimate(flops=1 << 20, bytes_accessed=1 << 16, transcendentals=0)


def axes_of(letter, size):
    return tuple(f"{letter}{bit}" for bit in reversed(range(size.bit_length() - 1)))


def swap(value, key):
    return lax.ppermute(value, key, [(0, 1), (1, 0)])


def place(held, key):
    rank = lambda k: (k[0] == "s", -int(k[1:]))
    return sum(1 for other in held if rank(other) < rank(key))


def join(mine, other, key, at):
    shape = mine.shape[:at] + (2,) + mine.shape[at:]
    side = lax.broadcasted_iota(jnp.int32, shape, at)
    return jnp.where(side == lax.axis_index(key), jnp.expand_dims(mine, at), jnp.expand_dims(other, at))


def half(value, which, at):
    return lax.dynamic_index_in_dim(value, which, at, keepdims=False)


def add_low(mine, other):
    return (mine.astype(F32) + other.astype(F32)).astype(BF16)


def tie(*values):
    return lax.optimization_barrier(values)


def row_major(value):
    return with_layout_constraint(value, Layout(tuple(range(value.ndim))))


class Moving:
    def start(self, key):
        self.prepare(key)
        self.go()

    def go(self):
        self.got = swap(self.send, self.key)

    def finish(self):
        pass


class Plain(Moving):
    def __init__(self, value, key):
        self.send, self.key = value, key


class Growing(Moving):
    def __init__(self, value):
        self.value, self.held = value, []

    def prepare(self, key):
        self.key, self.send = key, self.value

    def finish(self):
        at = place(self.held, self.key)
        self.held.append(self.key)
        self.value = join(self.value, self.got, self.key, at)


class Shrinking(Moving):
    def __init__(self, parts, merge, held):
        self.parts, self.merge, self.held = parts, merge, list(held)

    def prepare(self, key):
        self.key = key
        self.held.remove(key)
        self.at = place(self.held, key)
        self.bit = lax.axis_index(key)
        self.send = self.merge([half(p, 1 - self.bit, self.at) for p in self.parts])

    def finish(self):
        self.value = add_low(self.merge([half(p, self.bit, self.at) for p in self.parts]), self.got)
        self.parts, self.merge = [self.value], only


class Summing(Moving):
    def __init__(self, value):
        self.value = value

    def prepare(self, key):
        self.key, self.send = key, self.value

    def finish(self):
        self.value = self.value + self.got


def fire(items, *others):
    tied = tie(*[item.send for item in items], *others)
    for item, send in zip(items, tied):
        item.send = send
        item.go()
    return tied[len(items) :]


def only(parts):
    (part,) = parts
    return part


def stacked(parts):
    return jnp.stack(parts, axis=-3)


def settle(items, *others):
    tied = tie(*[item.got for item in items], *others)
    for item, got in zip(items, tied):
        item.got = got
        item.finish()
    return tied[len(items) :]


ROWS = 8


def fwd_kernel(k_ref, v_ref, r_ref, rate_ref, u_ref, a0_ref, b0_ref, w_ref, a_ref, b_ref):
    rate = rate_ref[...]
    boost = jnp.exp(u_ref[...])
    width = rate.shape[1]
    row = lax.broadcasted_iota(jnp.int32, (ROWS, width), 0)
    rowf = row.astype(F32)
    falling = jnp.exp(-rowf * rate)
    one = jnp.exp(-rate)
    steps = [(s, jnp.where(row >= s, jnp.exp(-s * rate), 0.0)) for s in (1, 2, 4)]
    inner = row >= 1

    def scan(tile, carry):
        before = jnp.where(inner, pltpu.roll(tile, 1, 0), 0.0)
        for s, factor in steps:
            before = before + factor * pltpu.roll(before, s, 0)
        before = before + falling * carry
        after = one * before[ROWS - 1 :, :] + tile[ROWS - 1 :, :]
        return before, after

    def tile_of(key, val, recept, carry):
        num, den = carry
        power = jnp.exp(key)
        num_before, num = scan(power * val, num)
        den_before, den = scan(power, den)
        now = boost * power
        mixed = (num_before + now * val) / (den_before + now)
        return (jax.nn.sigmoid(recept) * mixed, num_before, den_before), (num, den)

    def body(i, carry):
        at = pl.ds(pl.multiple_of(i * (2 * ROWS), 2 * ROWS), 2 * ROWS)
        key, val, recept = k_ref[at, :], v_ref[at, :].astype(F32), r_ref[at, :].astype(F32)
        low, carry = tile_of(key[:ROWS], val[:ROWS], recept[:ROWS], carry)
        high, carry = tile_of(key[ROWS:], val[ROWS:], recept[ROWS:], carry)
        for ref, a, b in zip((w_ref, a_ref, b_ref), low, high):
            ref[at, :] = jnp.concatenate([a, b], axis=0).astype(ref.dtype)
        return carry

    lax.fori_loop(
        0, k_ref.shape[0] // (2 * ROWS), body, (a0_ref[...], b0_ref[...]), unroll=2
    )


def bwd_kernel(
    k_ref, v_ref, a_ref, b_ref, p_ref, rate_ref, u_ref, ga_ref, gb_ref,
    dk_ref, dv_ref, first_ref, decay_ref,
):
    rate = rate_ref[...]
    boost = jnp.exp(u_ref[...])
    width = rate.shape[1]
    row = lax.broadcasted_iota(jnp.int32, (ROWS, width), 0)
    rowf = row.astype(F32)
    trailing = jnp.exp(-(ROWS - 1.0 - rowf) * rate)
    one = jnp.exp(-rate)
    steps = [(s, jnp.where(row < ROWS - s, jnp.exp(-s * rate), 0.0)) for s in (1, 2, 4)]
    inner = row < ROWS - 1

    def scan(tile, carry):
        later = jnp.where(inner, pltpu.roll(tile, ROWS - 1, 0), 0.0)
        for s, factor in steps:
            later = later + factor * pltpu.roll(later, ROWS - s, 0)
        later = later + trailing * carry
        before = one * later[:1, :] + tile[:1, :]
        return later, before

    def tile_of(tiles, carry):
        num, den, first, decay = carry
        key, val, num_before, den_before, p = tiles
        power = jnp.exp(key)
        now = boost * power
        q = -p * (num_before + now * val) / (den_before + now)
        num_later, num = scan(p, num)
        den_later, den = scan(q, den)
        diagonal = now * (val * p + q)
        d_key = power * (val * num_later + den_later) + diagonal
        d_val = power * num_later + now * p
        first = first + diagonal
        decay = decay + (num_later * num_before + den_later * den_before)
        return (d_key, d_val), (num, den, first, decay)

    count = k_ref.shape[0] // (2 * ROWS)

    def body(i, carry):
        at = pl.ds(pl.multiple_of((count - 1 - i) * (2 * ROWS), 2 * ROWS), 2 * ROWS)
        tiles = [ref[at, :].astype(F32) for ref in (k_ref, v_ref, a_ref, b_ref, p_ref)]
        high, carry = tile_of([tile[ROWS:] for tile in tiles], carry)
        low, carry = tile_of([tile[:ROWS] for tile in tiles], carry)
        for ref, a, b in zip((dk_ref, dv_ref), low, high):
            ref[at, :] = jnp.concatenate([a, b], axis=0).astype(BF16)
        return carry

    zero = jnp.zeros((ROWS, width), F32)
    done = lax.fori_loop(0, count, body, (ga_ref[...], gb_ref[...], zero, zero), unroll=2)
    first_ref[...] = done[2]
    decay_ref[...] = done[3]


def share_kernel(
    da_ref, w_ref, k_ref, v_ref, r_ref, a_ref, b_ref, rate_ref, u_ref,
    p_ref, dr_ref, ga_ref, gb_ref, dw_ref,
):
    dw_ref[...] = lax.dot_general(
        da_ref[...], w_ref[...], (((1,), (1,)), ((), ())), preferred_element_type=F32
    )
    rate = rate_ref[...]
    boost = jnp.exp(u_ref[...])
    rows = 2 * ROWS
    rowf = lax.broadcasted_iota(jnp.int32, (rows, rate.shape[1]), 0).astype(F32)
    near = jnp.exp(-rowf * rate)

    def body(i, carry):
        ga, gb = carry
        at = pl.ds(pl.multiple_of(i * rows, rows), rows)
        now = boost * jnp.exp(k_ref[at, :])
        inverse = 1.0 / (b_ref[at, :].astype(F32) + now)
        mixed = (a_ref[at, :].astype(F32) + now * v_ref[at, :].astype(F32)) * inverse
        gate = jax.nn.sigmoid(r_ref[at, :].astype(F32))
        d_mixed = dw_ref[at, :] * gate
        dr_ref[at, :] = (d_mixed * mixed * (1.0 - gate)).astype(BF16)
        p_low = (d_mixed * inverse).astype(BF16)
        p_ref[at, :] = p_low
        p = p_low.astype(F32)
        q = -p * mixed
        fall = near * jnp.exp(-(i * rows).astype(F32) * rate)
        return ga + fall * p, gb + fall * q

    zero = jnp.zeros((rows, rate.shape[1]), F32)
    ga, gb = lax.fori_loop(0, k_ref.shape[0] // rows, body, (zero, zero), unroll=2)
    ga_ref[...] = ga[:ROWS] + ga[ROWS:]
    gb_ref[...] = gb[:ROWS] + gb[ROWS:]


WIDTH = 256


def wkv_specs(rows):
    big = pl.BlockSpec((rows, WIDTH), lambda s, c: (s, c))
    row = pl.BlockSpec((1, WIDTH), lambda s, c: (0, c))
    state = pl.BlockSpec((None, 1, WIDTH), lambda s, c: (s, 0, c))
    partial = pl.BlockSpec((None, ROWS, WIDTH), lambda s, c: (s, 0, c))
    return big, row, state, partial


def wkv_forward(keys, vals, recepts, rate, first, num, den, seqs):
    total = keys.shape[0]
    big, row, state, _ = wkv_specs(total // seqs)
    cells = total * D
    return pl.pallas_call(
        fwd_kernel,
        grid=(seqs, D // WIDTH),
        in_specs=[big, big, big, row, row, state, state],
        out_specs=[big, big, big],
        out_shape=[
            jax.ShapeDtypeStruct((total, D), BF16),
            jax.ShapeDtypeStruct((total, D), F32),
            jax.ShapeDtypeStruct((total, D), F32),
        ],
        compiler_params=pltpu.CompilerParams(vmem_limit_bytes=58 << 20),
        cost_estimate=LIGHT,
    )(keys, vals, recepts, rate, first, num, den)


def wkv_backward(keys, vals, num_before, den_before, p, rate, first, num, den, seqs):
    total = keys.shape[0]
    big, row, state, partial = wkv_specs(total // seqs)
    cells = total * D
    return pl.pallas_call(
        bwd_kernel,
        grid=(seqs, D // WIDTH),
        in_specs=[big, big, big, big, big, row, row, state, state],
        out_specs=[big, big, partial, partial],
        out_shape=[
            jax.ShapeDtypeStruct((total, D), BF16),
            jax.ShapeDtypeStruct((total, D), BF16),
            jax.ShapeDtypeStruct((seqs, ROWS, D), F32),
            jax.ShapeDtypeStruct((seqs, ROWS, D), F32),
        ],
        compiler_params=pltpu.CompilerParams(vmem_limit_bytes=58 << 20),
        cost_estimate=LIGHT,
    )(keys, vals, num_before, den_before, p, rate, first, num, den)


def share_back(d_attn, weight, keys, vals, recepts, num_before, den_before, rate, first, seqs):
    total = keys.shape[0]
    span = total // seqs
    big, row, _, partial = wkv_specs(span)
    cells = total * D
    return pl.pallas_call(
        share_kernel,
        grid=(seqs, D // WIDTH),
        in_specs=[
            pl.BlockSpec((span, D), lambda s, c: (s, 0)),
            pl.BlockSpec((WIDTH, D), lambda s, c: (c, 0)),
            big, big, big, big, big, row, row,
        ],
        out_specs=[big, big, partial, partial],
        out_shape=[
            jax.ShapeDtypeStruct((total, D), BF16),
            jax.ShapeDtypeStruct((total, D), BF16),
            jax.ShapeDtypeStruct((seqs, ROWS, D), F32),
            jax.ShapeDtypeStruct((seqs, ROWS, D), F32),
        ],
        scratch_shapes=[pltpu.VMEM((span, WIDTH), F32)],
        compiler_params=pltpu.CompilerParams(vmem_limit_bytes=58 << 20),
        cost_estimate=LIGHT,
    )(d_attn, weight, keys, vals, recepts, num_before, den_before, rate, first)


PIECES = 8


def load_pieces(refs, held, sems):
    left, right = refs[:4], refs[4:]
    per = PIECES // held.shape[0]
    width = held.shape[2] // per
    copies = []
    for p in range(4):
        for side, ref in enumerate((left[p], right[p % 2].at[p // 2])):
            i = 2 * p + side
            to = held.at[i // per, :, pl.ds((i % per) * width, width)]
            copies.append(pltpu.make_async_copy(ref, to, sems.at[i]))
    return copies


def feed_kernel(s_ref, left_ref, x_ref, *rest):
    refs = rest[:6]
    fv_ref, xr_ref, fr_ref, mid_ref, cot_ref = rest[6:11]
    sq_ref, out_ref, dval_ref, dgate_ref, sums = rest[11:16]
    held, held_v, acc, gate_acc, sems, sems_v = rest[16:]
    copies = load_pieces(refs, held, sems)
    deep = held_v.shape[1]
    copies_v = [
        pltpu.make_async_copy(fv_ref.at[pl.ds(h * deep, deep)], held_v.at[h], sems_v.at[h])
        for h in range(2)
    ]
    first = pl.program_id(0) == 0
    width = held.shape[2]

    @pl.when(first)
    def _():
        for copy in copies + copies_v:
            copy.start()

    for p in range(4):

        @pl.when(first)
        def _(p=p):
            copies[2 * p].wait()
            copies[2 * p + 1].wait()

        hidden = jnp.maximum(jnp.dot(x_ref[...], held[p], preferred_element_type=F32), 0.0)
        at = pl.multiple_of(jnp.bitwise_xor(s_ref[0], p) * width, width)
        sq_ref[:, pl.ds(at, width)] = (hidden * hidden).astype(BF16)

    gate_acc[...] = jnp.dot(xr_ref[...], fr_ref[...], preferred_element_type=F32)
    total = None
    for h in range(2):

        @pl.when(first)
        def _(h=h):
            copies_v[h].wait()

        part = jnp.dot(sq_ref[:, pl.ds(h * deep, deep)], held_v[h], preferred_element_type=F32)
        total = part if total is None else total + part
    acc[...] = total

    left = left_ref[pl.program_id(0)]
    sums[...] = jnp.zeros_like(sums)

    def body(i, _):
        start = pl.multiple_of(i * 2 * ROWS, 2 * ROWS)
        at = pl.ds(start, 2 * ROWS)
        rows = start + lax.broadcasted_iota(jnp.int32, (2 * ROWS, 1), 0)
        keep = rows < left
        gate = jax.nn.sigmoid(gate_acc[at, :])
        feed = jnp.where(keep, gate * acc[at, :], 0.0)
        result = jnp.where(keep, mid_ref[at, :], 0.0) + feed
        g = jnp.where(keep, cot_ref[at, :].astype(F32), 0.0)
        out_ref[at, :] = result.astype(BF16)
        dval_ref[at, :] = (g * gate).astype(BF16)
        dgate_ref[at, :] = (g * feed * (1.0 - gate)).astype(BF16)
        sums[0] += fold(result * result)
        sums[1] += fold(feed * feed)
        return 0

    lax.fori_loop(0, mid_ref.shape[0] // (2 * ROWS), body, 0, unroll=2)


def feed_forward(my_seq, left, inputs, pieces, weight, gate_inputs, gate_weight, middle, cotangent, seqs):
    total = inputs.shape[0]
    width = 2 * pieces[0].shape[1]
    span = total // seqs
    ff = 4 * width
    big = pl.BlockSpec((span, D), lambda i, *_: (i, 0))
    return pl.pallas_call(
        feed_kernel,
        grid_spec=pltpu.PrefetchScalarGridSpec(
            num_scalar_prefetch=2,
            grid=(seqs,),
            in_specs=[big]
            + [pl.BlockSpec(memory_space=pl.ANY)] * 7
            + [big, pl.BlockSpec((D, D), lambda i, *_: (0, 0), pipeline_mode=pl.Buffered(1)), big, big],
            out_specs=[
                pl.BlockSpec((span, ff), lambda i, *_: (i, 0)), big, big, big,
                pl.BlockSpec((None, 2, ROWS, D), lambda i, *_: (i, 0, 0, 0)),
            ],
            scratch_shapes=[
                pltpu.VMEM((4, D, width), BF16),
                pltpu.VMEM((2, 2 * width, D), BF16),
                pltpu.VMEM((span, D), F32),
                pltpu.VMEM((span, D), F32),
                pltpu.SemaphoreType.DMA((PIECES,)),
                pltpu.SemaphoreType.DMA((2,)),
            ],
        ),
        out_shape=[
            jax.ShapeDtypeStruct((total, ff), BF16),
            jax.ShapeDtypeStruct((total, D), BF16),
            jax.ShapeDtypeStruct((total, D), BF16),
            jax.ShapeDtypeStruct((total, D), BF16),
            jax.ShapeDtypeStruct((seqs, 2, ROWS, D), F32),
        ],
        compiler_params=pltpu.CompilerParams(vmem_limit_bytes=60 << 20),
        cost_estimate=LIGHT,
    )(my_seq[None], left, inputs, *pieces, weight, gate_inputs, gate_weight, middle, cotangent)


CHUNK = 128


def stats_of(values):
    centre = values - jnp.mean(values, axis=-1, keepdims=True)
    inverse = lax.rsqrt(jnp.mean(centre * centre, axis=-1, keepdims=True) + EPS)
    return centre * inverse, inverse


def norm_back(grads, normed, inverse):
    return inverse * (
        grads
        - jnp.mean(grads, axis=-1, keepdims=True)
        - normed * jnp.mean(grads * normed, axis=-1, keepdims=True)
    )


def fold(values):
    return jnp.sum(values.reshape(values.shape[0] // ROWS, ROWS, values.shape[1]), axis=0)


def next_rows(values, carry):
    last = lax.broadcasted_iota(jnp.int32, values.shape, 0) == CHUNK - 1
    return jnp.where(last, carry, pltpu.roll(values, CHUNK - 1, 0))


def previous_rows(values, carry):
    first = lax.broadcasted_iota(jnp.int32, values.shape, 0) == 0
    return jnp.where(first, carry, pltpu.roll(values, 1, 0))


def mid_kernel(
    left_ref, w_ref, weight_ref, x_ref, gain_ref, bias_ref, mk_ref, mr_ref,
    mid_ref, fk_ref, fr_ref, first_ref, sq_ref,
):
    mid_ref[...] = jnp.dot(w_ref[...], weight_ref[...], preferred_element_type=F32)
    left = left_ref[pl.program_id(0)]
    gain, bias, mix_k, mix_r = gain_ref[...], bias_ref[...], mk_ref[...], mr_ref[...]
    sq_ref[...] = jnp.zeros_like(sq_ref)

    def body(i, carry):
        start = pl.multiple_of(i * CHUNK, CHUNK)
        at = pl.ds(start, CHUNK)
        attn = mid_ref[at, :]
        rows = start + lax.broadcasted_iota(jnp.int32, (CHUNK, 1), 0)
        sq_ref[...] += fold(jnp.where(rows < left, attn * attn, 0.0))
        middle = x_ref[at, :].astype(F32) + attn
        mid_ref[at, :] = middle
        b = stats_of(middle)[0] * gain + bias
        before = previous_rows(b, carry)
        fk_ref[at, :] = (b * mix_k + before * (1.0 - mix_k)).astype(BF16)
        fr_ref[at, :] = (b * mix_r + before * (1.0 - mix_r)).astype(BF16)

        @pl.when(i == 0)
        def _():
            first_ref[...] = b[:1, :]

        return b[CHUNK - 1 :, :]

    lax.fori_loop(0, x_ref.shape[0] // CHUNK, body, jnp.zeros_like(gain), unroll=2)


def mid_forward(left, weighted, weight, tokens, gain, bias, mix_k, mix_r, seqs):
    total = tokens.shape[0]
    span = total // seqs
    big = pl.BlockSpec((span, D), lambda s, _: (s, 0))
    row = pl.BlockSpec((1, D), lambda s, _: (0, 0))
    tile = lambda rows: pl.BlockSpec((None, rows, D), lambda s, _: (s, 0, 0))
    return pl.pallas_call(
        mid_kernel,
        grid_spec=pltpu.PrefetchScalarGridSpec(
            num_scalar_prefetch=1,
            grid=(seqs,),
            in_specs=[big, pl.BlockSpec((D, D), lambda s, _: (0, 0)), big, row, row, row, row],
            out_specs=[big, big, big, tile(1), tile(ROWS)],
        ),
        out_shape=[
            jax.ShapeDtypeStruct((total, D), F32),
            jax.ShapeDtypeStruct((total, D), BF16),
            jax.ShapeDtypeStruct((total, D), BF16),
            jax.ShapeDtypeStruct((seqs, 1, D), F32),
            jax.ShapeDtypeStruct((seqs, ROWS, D), F32),
        ],
        compiler_params=pltpu.CompilerParams(vmem_limit_bytes=58 << 20),
        cost_estimate=LIGHT,
    )(left, weighted, weight, tokens, gain, bias, mix_k, mix_r)


def down_kernel(s_ref, left_ref, dval_ref, fv_ref, sq_ref, *rest):
    refs = rest[:6]
    gate_ref, fr_ref, mid_ref, cot_ref, gain_ref, bias_ref, mk_ref, mr_ref = rest[6:14]
    dh_ref, out_ref, low_ref, first_k, first_r, tail_ref, sums = rest[14:21]
    held, held_v, held_sq, acc_k, acc_r, sems, sems_v, sems_sq = rest[21:]
    copies = load_pieces(refs, held, sems)
    width = held_v.shape[1]
    places = [pl.multiple_of(jnp.bitwise_xor(s_ref[0], p) * width, width) for p in range(4)]
    copies_v = [
        pltpu.make_async_copy(fv_ref.at[pl.ds(places[p], width)], held_v.at[p], sems_v.at[p])
        for p in range(4)
    ]
    span = held_sq.shape[1]
    rows = pl.ds(pl.multiple_of(pl.program_id(0) * span, span), span)
    copies_sq = [
        pltpu.make_async_copy(sq_ref.at[rows, pl.ds(places[p], width)], held_sq.at[p], sems_sq.at[p])
        for p in range(4)
    ]
    first = pl.program_id(0) == 0
    back = (((1,), (1,)), ((), ()))
    for copy in copies_sq[:1]:
        copy.start()

    @pl.when(first)
    def _():
        copies_v[0].start()

    for copy in copies_sq[1:]:
        copy.start()

    @pl.when(first)
    def _():
        for copy in copies_v[1:] + copies:
            copy.start()

    for p in range(4):
        copies_sq[p].wait()

        @pl.when(first)
        def _(p=p):
            copies_v[p].wait()

        for side in range(2):
            part = pl.ds(side * (width // 2), width // 2)
            d_sq = lax.dot_general(dval_ref[...], held_v[p, part, :], back, preferred_element_type=F32)
            squared = held_sq[p, :, part].astype(F32)
            twice = 2.0 * squared * lax.rsqrt(jnp.maximum(squared, 1e-37))
            dh_ref[p, :, part] = (twice * d_sq).astype(BF16)

    acc_r[...] = lax.dot_general(gate_ref[...], fr_ref[...], back, preferred_element_type=F32)
    for h in range(2):

        @pl.when(first)
        def _(h=h):
            for copy in copies[4 * h : 4 * h + 4]:
                copy.wait()

        part = lax.dot_general(
            jnp.concatenate([dh_ref[2 * h], dh_ref[2 * h + 1]], axis=1), held[h],
            back, preferred_element_type=F32,
        )
        acc_k[...] = part if h == 0 else acc_k[...] + part

    left = left_ref[pl.program_id(0)]
    gain, bias, mix_k, mix_r = gain_ref[...], bias_ref[...], mk_ref[...], mr_ref[...]
    sums[...] = jnp.zeros_like(sums)
    count = mid_ref.shape[0] // CHUNK

    def body(i, carry):
        later_k, later_r = carry
        start = pl.multiple_of((count - 1 - i) * CHUNK, CHUNK)
        at = pl.ds(start, CHUNK)
        d_fk, d_fr = acc_k[at, :], acc_r[at, :]
        next_k, next_r = next_rows(d_fk, later_k), next_rows(d_fr, later_r)
        n, inverse = stats_of(mid_ref[at, :])
        b = n * gain + bias
        db = d_fk * mix_k + next_k * (1.0 - mix_k) + d_fr * mix_r + next_r * (1.0 - mix_r)
        sums[0] += fold(b * (d_fk - next_k))
        sums[1] += fold(b * (d_fr - next_r))
        sums[2] += fold(n * db)
        sums[3] += fold(db)
        rows = start + lax.broadcasted_iota(jnp.int32, (CHUNK, 1), 0)
        g = jnp.where(rows < left, cot_ref[at, :].astype(F32), 0.0)
        d_middle = g + norm_back(db * gain, n, inverse)
        out_ref[at, :] = d_middle
        low_ref[at, :] = d_middle.astype(BF16)

        @pl.when(i == 0)
        def _():
            tail_ref[0] = d_middle[CHUNK - 1 :, :]
            tail_ref[1] = n[CHUNK - 1 :, :]
            tail_ref[2] = jnp.broadcast_to(inverse[CHUNK - 1 :, :], gain.shape)

        return d_fk[:1, :], d_fr[:1, :]

    zero = jnp.zeros_like(gain)
    first_k[...], first_r[...] = lax.fori_loop(0, count, body, (zero, zero), unroll=2)


def down(
    my_seq, left, grads, weight, squared, pieces, gate_grads, gate_weight,
    middle, cotangent, gain, bias, mix_k, mix_r, seqs,
):
    total, ff = squared.shape
    span = total // seqs
    width = ff // 4
    big = pl.BlockSpec((span, D), lambda s, *_: (s, 0))
    alone = pl.BlockSpec((span, D), lambda s, *_: (s, 0), pipeline_mode=pl.Buffered(1))
    row = pl.BlockSpec((1, D), lambda s, *_: (0, 0))
    one = pl.BlockSpec((None, 1, D), lambda s, *_: (s, 0, 0))
    return pl.pallas_call(
        down_kernel,
        grid_spec=pltpu.PrefetchScalarGridSpec(
            num_scalar_prefetch=2,
            grid=(seqs,),
            in_specs=[
                big,
                pl.BlockSpec(memory_space=pl.ANY),
                pl.BlockSpec(memory_space=pl.ANY),
            ]
            + [pl.BlockSpec(memory_space=pl.ANY)] * 6
            + [big, pl.BlockSpec((D, D), lambda s, *_: (0, 0), pipeline_mode=pl.Buffered(1)), alone, big]
            + [row] * 4,
            out_specs=[
                pl.BlockSpec((4, span, width), lambda s, *_: (0, s, 0)),
                big, big, one, one,
                pl.BlockSpec((None, 3, 1, D), lambda s, *_: (s, 0, 0, 0)),
                pl.BlockSpec((None, 4, ROWS, D), lambda s, *_: (s, 0, 0, 0)),
            ],
            scratch_shapes=[
                pltpu.VMEM((2, D, 2 * width), BF16),
                pltpu.VMEM((4, width, D), BF16),
                pltpu.VMEM((4, span, width), BF16),
                pltpu.VMEM((span, D), F32),
                pltpu.VMEM((span, D), F32),
                pltpu.SemaphoreType.DMA((PIECES,)),
                pltpu.SemaphoreType.DMA((4,)),
                pltpu.SemaphoreType.DMA((4,)),
            ],
        ),
        out_shape=[
            jax.ShapeDtypeStruct((4, total, width), BF16),
            jax.ShapeDtypeStruct((total, D), F32),
            jax.ShapeDtypeStruct((total, D), BF16),
            jax.ShapeDtypeStruct((seqs, 1, D), F32),
            jax.ShapeDtypeStruct((seqs, 1, D), F32),
            jax.ShapeDtypeStruct((seqs, 3, 1, D), F32),
            jax.ShapeDtypeStruct((seqs, 4, ROWS, D), F32),
        ],
        compiler_params=pltpu.CompilerParams(vmem_limit_bytes=60 << 20),
        cost_estimate=LIGHT,
    )(
        my_seq[None], left, grads, weight, squared, *pieces, gate_grads, gate_weight,
        middle, cotangent, gain, bias, mix_k, mix_r,
    )


def mix_kernel(
    dk_ref, dv_ref, dr_ref, wk_ref, wv_ref, wr_ref, x_ref, dm_ref,
    gain_ref, bias_ref, mk_ref, mv_ref, mr_ref,
    out_ref, firsts, tail_ref, sums, acc, held, sems,
):
    first = pl.program_id(0) == 0
    copies = [
        pltpu.make_async_copy(ref, held.at[i], sems.at[i]) for i, ref in enumerate((wk_ref, wv_ref, wr_ref))
    ]

    @pl.when(first)
    def _():
        for copy in copies:
            copy.start()

    for i, grads in enumerate((dk_ref, dv_ref, dr_ref)):

        @pl.when(first)
        def _(i=i):
            copies[i].wait()

        acc[i] = lax.dot_general(
            grads[...], held[i], (((1,), (1,)), ((), ())), preferred_element_type=F32
        )
    gain, bias = gain_ref[...], bias_ref[...]
    mixes = (mk_ref[...], mv_ref[...], mr_ref[...])
    sums[...] = jnp.zeros_like(sums)
    count = x_ref.shape[0] // CHUNK

    def body(i, carry):
        start = pl.multiple_of((count - 1 - i) * CHUNK, CHUNK)
        at = pl.ds(start, CHUNK)
        n, inverse = stats_of(x_ref[at, :].astype(F32))
        a = n * gain + bias
        da, heads = None, []
        for j in range(3):
            d = acc[j, at, :]
            later = next_rows(d, carry[j])
            sums[j] += fold(a * (d - later))
            part = d * mixes[j] + later * (1.0 - mixes[j])
            da = part if da is None else da + part
            heads.append(d[:1, :])
        sums[3] += fold(n * da)
        sums[4] += fold(da)
        total = dm_ref[at, :] + norm_back(da * gain, n, inverse)
        out_ref[at, :] = total.astype(BF16)

        @pl.when(i == 0)
        def _():
            tail_ref[0] = total[CHUNK - 1 :, :]
            tail_ref[1] = n[CHUNK - 1 :, :]
            tail_ref[2] = jnp.broadcast_to(inverse[CHUNK - 1 :, :], gain.shape)

        return tuple(heads)

    zero = jnp.zeros_like(gain)
    heads = lax.fori_loop(0, count, body, (zero, zero, zero), unroll=2)
    for j in range(3):
        firsts[j] = heads[j]


def mix_back(d_keys, d_vals, d_recepts, w_k, w_v, w_r, tokens, d_middle, gain, bias, mix_k, mix_v, mix_r, seqs):
    total = tokens.shape[0]
    span = total // seqs
    big = pl.BlockSpec((span, D), lambda s: (s, 0))
    row = pl.BlockSpec((1, D), lambda s: (0, 0))
    full = pl.BlockSpec(memory_space=pl.ANY)
    return pl.pallas_call(
        mix_kernel,
        grid=(seqs,),
        in_specs=[big, big, big, full, full, full, big, big] + [row] * 5,
        out_specs=[
            big,
            pl.BlockSpec((None, 3, 1, D), lambda s: (s, 0, 0, 0)),
            pl.BlockSpec((None, 3, 1, D), lambda s: (s, 0, 0, 0)),
            pl.BlockSpec((None, 5, ROWS, D), lambda s: (s, 0, 0, 0)),
        ],
        out_shape=[
            jax.ShapeDtypeStruct((total, D), BF16),
            jax.ShapeDtypeStruct((seqs, 3, 1, D), F32),
            jax.ShapeDtypeStruct((seqs, 3, 1, D), F32),
            jax.ShapeDtypeStruct((seqs, 5, ROWS, D), F32),
        ],
        scratch_shapes=[
            pltpu.VMEM((3, span, D), F32),
            pltpu.VMEM((3, D, D), BF16),
            pltpu.SemaphoreType.DMA((3,)),
        ],
        compiler_params=pltpu.CompilerParams(vmem_limit_bytes=58 << 20),
        cost_estimate=LIGHT,
    )(d_keys, d_vals, d_recepts, w_k, w_v, w_r, tokens, d_middle, gain, bias, mix_k, mix_v, mix_r)


def put_rows(values, rows, at):
    seqs = rows.shape[0]
    whole = values.reshape(seqs, values.shape[0] // seqs, D)
    return lax.dynamic_update_slice(whole, rows.astype(values.dtype), (0, at, 0)).reshape(values.shape)


def cut_kernel(_, k, v, r, o, fk1, fk2, rows, kv_out, ro_out, f1_out, f2_out, row_out):
    kv_out[0], kv_out[1] = k[...], v[...]
    ro_out[0], ro_out[1] = r[...], o[...]
    f1_out[...], f2_out[...] = fk1[...], fk2[...]
    last = rows.shape[1] - 1
    row_out[...] = rows[...].astype(F32)[:, last:, :]


def cut(my_seq, quarter, key, value, recept, output, feed_key, tokens):
    seqs, span, _ = tokens.shape
    shard, ff = feed_key.shape
    part = pl.BlockSpec((quarter, D), lambda i, at: (at[0], 0))
    side = lambda which: pl.BlockSpec((shard, ff // PIECES), lambda i, at: (0, 2 * at[0] + which))
    full = lambda *shape: pl.BlockSpec(shape, lambda i, at: (0,) * len(shape))
    shapes = [(2, quarter, D), (2, quarter, D)] + [(shard, ff // PIECES)] * 2 + [(seqs, 1, D)]
    kinds = [BF16] * 4 + [F32]
    return pl.pallas_call(
        cut_kernel,
        grid_spec=pltpu.PrefetchScalarGridSpec(
            num_scalar_prefetch=1,
            grid=(1,),
            in_specs=[part] * 4
            + [side(0), side(1), pl.BlockSpec((seqs, 2 * ROWS, D), lambda i, at: (0, span // (2 * ROWS) - 1, 0))],
            out_specs=[full(*shape) for shape in shapes],
        ),
        out_shape=[jax.ShapeDtypeStruct(shape, kind) for shape, kind in zip(shapes, kinds)],
    )(my_seq[None], key, value, recept, output, feed_key, feed_key, tokens)


def dot(left, right):
    return jnp.dot(left, right, preferred_element_type=F32)


def dot_back(grads, weight):
    return lax.dot_general(grads, weight, (((1,), (1,)), ((), ())), preferred_element_type=F32)


def dot_weight(inputs, grads):
    return lax.dot_general(inputs, grads, (((0,), (0,)), ((), ())), preferred_element_type=F32)


def normalize(values):
    centre = values - jnp.mean(values, axis=-1, keepdims=True)
    spread = jnp.mean(centre * centre, axis=-1, keepdims=True)
    inverse = lax.rsqrt(spread + EPS)
    return centre * inverse, inverse


def from_behind(value, axes, by):
    count = lax.axis_size(axes)
    pairs = [(i, i + by) for i in range(count) if 0 <= i + by < count]
    return lax.ppermute(value, axes, pairs)


def shifted(rows, edge):
    return jnp.concatenate([edge, rows[:, :-1]], axis=1)


def pulled(rows, edge):
    return jnp.concatenate([rows[:, 1:], edge], axis=1)


def blend(now, before, share):
    return (now * share + before * (1.0 - share)).astype(BF16)


def earlier_state(decay, num, den, axes, backward):
    count = lax.axis_size(axes)
    mine = lax.axis_index(axes)
    packed = lax.all_gather(jnp.concatenate([num, den], axis=0), axes)
    seqs = num.shape[0]
    state = jnp.zeros_like(packed[0])
    for hop in range(count - 1):
        source = count - 1 - hop if backward else hop
        longer = decay * state + packed[source]
        keep = source > mine if backward else source < mine
        state = jnp.where(keep, longer, state)
    return state[:seqs, None, :], state[seqs:, None, :]


def per_device(
    dp_axes, seq_axes,
    tokens, cotangent, lengths, assignment,
    mix_norm_gain, mix_norm_bias, shift_key, shift_value, shift_recept, time_decay, time_first,
    key_weight, value_weight, recept_weight, output_weight,
    feed_norm_gain, feed_norm_bias, feed_shift_key, feed_shift_recept,
    feed_key_weight, feed_recept_weight, feed_value_weight,
):
    seqs, span, _ = tokens.shape
    total = seqs * span
    dp, seq = lax.axis_size(dp_axes), lax.axis_size(seq_axes)
    my_dp, my_seq = lax.axis_index(dp_axes), lax.axis_index(seq_axes)
    every = dp_axes + seq_axes
    z_axes, x = dp_axes[:-1], dp_axes[-1]
    y, c = seq_axes
    ff = feed_key_weight.shape[1]
    flat = lambda v: v.reshape(total, v.shape[-1])
    deep = lambda v: v.reshape(seqs, span, v.shape[-1])

    shard = D // dp
    quarter = shard // seq

    def own_rows(weight):
        return lax.dynamic_slice_in_dim(weight, my_seq * quarter, quarter, 0)

    hid = feed_value_weight.shape[0]
    halves = lambda w: half(w.reshape(2, w.shape[0] // 2, D), lax.axis_index(c), 0)
    gathered = lambda w: lax.all_gather(w, dp_axes + (c,), axis=0, tiled=True)
    w_fr = gathered(halves(feed_recept_weight))
    *cuts, last_token = cut(
        my_seq, quarter, key_weight, value_weight, recept_weight, output_weight, feed_key_weight, tokens
    )
    kv, ro, f1, f2 = [Growing(part) for part in cuts]
    kv.start(z_axes[0])
    ro.start(z_axes[0])
    kv.value, tokens, *vectors = tie(
        kv.value, tokens,
        mix_norm_gain, mix_norm_bias, shift_key, shift_value, shift_recept, time_decay, time_first,
        feed_norm_gain, feed_norm_bias, feed_shift_key, feed_shift_recept,
    )
    vectors = Growing(jnp.stack(vectors))
    vectors.start(z_axes[0])
    edge1 = from_behind(last_token, seq_axes, 1)
    for z in z_axes[1:]:
        (edge1,) = settle([kv, ro, vectors], edge1)
        kv.start(z)
        ro.start(z)
        vectors.start(z)
    f1.value, f2.value = settle([kv, ro, vectors], f1.value, f2.value)
    kv.start(x)
    ro.start(y)
    vectors.start(x)
    f1.start(z_axes[0])
    f2.start(z_axes[0])
    settle([kv, ro, vectors, f1, f2])
    kv.start(y)
    ro.start(x)
    for z in z_axes[1:]:
        f1.start(z)
        f2.start(z)
        if z != z_axes[-1]:
            settle([f1, f2])
    fv_part, w_fr = settle([f1, f2, kv, ro], halves(feed_value_weight), w_fr)
    w_fv = gathered(fv_part)
    kv.prepare(c)
    ro.prepare(c)
    f1.prepare(x)
    f2y = Plain(f2.value, y)
    tokens, vectors.value = fire([kv, ro, f1, f2y], tokens, vectors.value)
    settle([kv, ro])
    pick = lambda v, i: jnp.moveaxis(v, -3, 0)[i].reshape(D, D)
    w_k, w_v, w_r, w_o = pick(kv.value, 0), pick(kv.value, 1), pick(ro.value, 0), pick(ro.value, 1)
    vectors = jnp.swapaxes(vectors.value.reshape(dp, 11, D // dp), 0, 1).reshape(11, D).astype(F32)
    gain1, bias1, mix_k, mix_v, mix_r, log_rate, first, gain2, bias2, fmix_k, fmix_r = [
        vectors[i : i + 1] for i in range(11)
    ]
    rate = jnp.exp(log_rate)
    lam = jnp.exp(-rate)

    slot_ids = jnp.arange(assignment.shape[0])
    my_slots = my_dp * seqs + jnp.arange(seqs)
    seq_ids = jnp.sum(jnp.where(slot_ids[None, :] == my_slots[:, None], assignment[None, :], 0), axis=1)
    my_lens = jnp.sum(jnp.where(slot_ids[None, :] == seq_ids[:, None], lengths[None, :], 0), axis=1)
    positions = my_seq * span + jnp.arange(span)
    valid = flat((positions[None, :] < my_lens[:, None]).astype(F32)[..., None])
    inside = (my_seq > 0).astype(F32)

    xin = tokens.astype(F32)
    edge1 = (normalize(edge1)[0] * gain1 + bias1) * inside
    n1, inv1 = normalize(xin)
    a = n1 * gain1 + bias1
    a_prev = shifted(a, edge1)
    key_in = flat(blend(a, a_prev, mix_k))
    value_in = flat(blend(a, a_prev, mix_v))
    recept_in = flat(blend(a, a_prev, mix_r))
    keys = dot(key_in, w_k)
    vals = dot(value_in, w_v)
    recepts = dot(recept_in, w_r)

    offsets = jnp.arange(span).astype(F32)[:, None]
    power = deep(jnp.exp(keys))
    left = jnp.exp(-(span - 1.0 - offsets) * rate)
    span_decay = jnp.exp(-span * rate)
    num_end = jnp.sum(left * power * deep(vals), axis=1)
    vals, recepts = vals.astype(BF16), recepts.astype(BF16)
    den_end = jnp.sum(left * power, axis=1)
    num0, den0 = earlier_state(span_decay, num_end, den_end, seq_axes, False)
    num0, den0 = settle([f1, f2y], num0, den0)
    f2y = f2y.got
    f1_0 = row_major(f1.value).reshape(D, -1)
    f2.value = jnp.stack([f2.value, f2y], axis=len(f2.held))
    f1_y = Plain(f1_0, y)
    f2.prepare(x)
    num0, den0 = fire([f1_y, f2], num0, den0)
    weighted, num_before, den_before = wkv_forward(keys, vals, recepts, rate, first, num0, den0, seqs)
    (weighted,) = settle([f1_y, f2], weighted)
    f1_y = f1_y.got
    f2_0 = row_major(jnp.moveaxis(f2.value, -3, 0)).reshape(2, D, -1)
    f1_c, f1_yc, f2_c = Plain(f1_0, c), Plain(f1_y, c), Plain(f2_0, c)
    (weighted,) = fire([f1_c, f1_yc, f2_c], weighted)
    last_row = last_token[:, 0] + dot(deep(weighted)[:, -1], w_o)
    edge2 = from_behind(last_row[:, None], seq_axes, 1)
    left_rows = (my_lens - my_seq * span).astype(jnp.int32)
    flat_tokens = flat(tokens)
    middle, feed_key_in, feed_recept_in, b_first, attn_sq = mid_forward(
        left_rows, weighted, w_o, flat_tokens, gain2, bias2, fmix_k, fmix_r, seqs
    )

    edge2 = (normalize(edge2)[0] * gain2 + bias2) * inside
    feed_key_in = put_rows(feed_key_in, blend(b_first, edge2, fmix_k), 0)
    feed_recept_in = put_rows(feed_recept_in, blend(b_first, edge2, fmix_r), 0)
    (feed_key_in,) = settle([f1_c, f1_yc, f2_c], feed_key_in)
    f1_c, f1_yc, f2_c = f1_c.got, f1_yc.got, f2_c.got
    pieces = (f1_0, f1_c, f1_y, f1_yc, f2_0, f2_c)
    sq, block_out, d_fval, d_fgate, squares = feed_forward(
        my_seq, left_rows, feed_key_in, pieces, w_fv, feed_recept_in, w_fr, middle, flat(cotangent), seqs
    )
    block_out = deep(block_out)
    stats = jnp.stack([jnp.sum(squares[:, 0]), jnp.sum(attn_sq), jnp.sum(squares[:, 1])])

    gfv = dot_weight(sq, d_fval).astype(BF16)
    gfv = lax.psum_scatter(gfv, dp_axes + (c,), scatter_dimension=0, tiled=True)
    gfr = dot_weight(feed_recept_in, d_fgate).astype(BF16)
    dh, d_middle, d_attn, first_k, first_r, tail, sums2 = down(
        my_seq, left_rows, d_fval, w_fv, sq, pieces, d_fgate, w_fr,
        middle, flat(cotangent), gain2, bias2, fmix_k, fmix_r, seqs,
    )
    gfk_1 = dot_weight(feed_key_in, dh[1]).astype(BF16)
    gfk_3 = dot_weight(feed_key_in, dh[3]).astype(BF16)

    lead = (2,) * len(every)
    split = lambda g_: Shrinking([g_.reshape(lead + (quarter, D))], only, every)
    side = ff // PIECES
    got_1, got_3 = Plain(gfk_1, c), Plain(gfk_3, c)
    (dh,) = fire([got_1, got_3], dh)
    gfk_0 = dot_weight(feed_key_in, dh[0]).astype(BF16)
    gfk_2 = dot_weight(feed_key_in, dh[2]).astype(BF16)
    edge3 = from_behind(first_k * (1.0 - fmix_k) + first_r * (1.0 - fmix_r), seq_axes, -1)
    d_middle, gfk_0, gfk_2, tail, sums2 = settle([got_1, got_3], d_middle, gfk_0, gfk_2, tail, sums2)
    low = lambda mine, got, at: add_low(mine[:, at : at + side], got.got[:, at : at + side])
    by_dp = lambda g_: g_.reshape((2,) * len(dp_axes) + (shard, g_.shape[1]))
    got_a = Plain(low(gfk_2, got_3, 0), y)
    r2 = Shrinking([by_dp(low(gfk_0, got_1, side)), by_dp(low(gfk_2, got_3, side))], stacked, dp_axes)
    r2.prepare(x)
    (d_attn,) = fire([got_a, r2], d_attn)
    a_0 = low(gfk_0, got_1, 0)

    d_last = tail[:, 0] + norm_back(edge3 * gain2, tail[:, 1], tail[:, 2])
    d_middle = put_rows(d_middle, d_last, span - 1)
    d_attn = put_rows(d_attn, d_last.astype(BF16), span - 1)
    small2 = sums2.sum((0, 2)) + jnp.concatenate(
        [
            -jnp.sum(edge2 * first_k, axis=0), -jnp.sum(edge2 * first_r, axis=0),
            jnp.sum(tail[:, 1] * edge3, axis=0), jnp.sum(edge3, axis=0),
        ]
    )
    p, d_recepts, ga_part, gb_part = share_back(
        d_attn, w_o, keys, vals, recepts, num_before, den_before, rate, first, seqs
    )
    r_o = dot_weight(weighted, d_attn).astype(BF16)
    r_r = dot_weight(recept_in, d_recepts).astype(BF16)
    ga_part, r_o, r_r = settle([r2, got_a], ga_part, r_o, r_r)

    orf = jnp.concatenate([r_o, r_r, gfr], axis=1)
    orf = lax.psum_scatter(orf, dp_axes + (c,), scatter_dimension=0, tiled=True)
    r1 = Shrinking([by_dp(add_low(a_0, got_a.got))], only, dp_axes)
    r1.prepare(x)
    b_got = Plain(r2.value[..., 1, :, :], y)
    ga0, gb0 = earlier_state(span_decay, ga_part.sum(1), gb_part.sum(1), seq_axes, True)
    ga0, gb0 = fire([r1, b_got], ga0, gb0)
    d_keys, d_vals, first_part, decay_part = wkv_backward(
        keys, vals, num_before, den_before, p, rate, first, ga0, gb0, seqs
    )
    d_keys, d_vals, gfv, first_part, decay_part = settle(
        [r1, b_got], d_keys, d_vals, gfv, first_part, decay_part
    )
    z1, z2 = z_axes[-1], z_axes[:-1]
    rows_of = lambda g_: g_.reshape(lead + (quarter, D))
    r_kv = Shrinking(
        [
            rows_of(dot_weight(key_in, d_keys).astype(BF16)),
            rows_of(dot_weight(value_in, d_vals).astype(BF16)),
        ],
        stacked, every,
    )
    r_kv.prepare(c)
    r_f = Shrinking([r1.value, add_low(r2.value[..., 0, :, :], b_got.got)], stacked, r1.held)
    r_f.prepare(z1)
    gfv_got = Plain(gfv, y)
    small2, first_part, decay_part = fire([r_kv, r_f, gfv_got], small2, first_part, decay_part)
    small2 = jnp.concatenate(
        [
            -(lam * rate) * jnp.sum(decay_part, axis=(0, 1))[None], jnp.sum(first_part, axis=(0, 1))[None],
            small2, jnp.pad(stats, (0, D - 3))[None],
        ]
    )
    d_keys, small2 = settle([r_kv, gfv_got], d_keys, small2)

    r_kv.prepare(y)
    out_v = Growing(add_low(gfv, gfv_got.got))
    out_v.prepare(c)
    d_keys, d_middle = fire([r_kv, out_v], d_keys, d_middle)
    mix_outs = mix_back(
        d_keys, d_vals, d_recepts, w_k, w_v, w_r, flat_tokens, d_middle,
        gain1, bias1, mix_k, mix_v, mix_r, seqs,
    )
    input_grad, firsts, tail1, sums1 = settle([r_kv, r_f, out_v], *mix_outs)

    r_kv.prepare(x)
    for z in reversed(z2):
        r_f.prepare(z)
        if z != z2[0]:
            r_f.go()
            settle([r_f])
    (firsts,) = fire([r_kv, r_f], firsts)
    mixes = (mix_k, mix_v, mix_r)
    edge4 = from_behind(sum(firsts[:, i] * (1.0 - m) for i, m in enumerate(mixes)), seq_axes, -1)
    input_last = (tail1[:, 0] + norm_back(edge4 * gain1, tail1[:, 1], tail1[:, 2])).astype(BF16)
    input_grad = deep(put_rows(input_grad, input_last, span - 1))
    small1 = sums1.sum((0, 2)) + jnp.concatenate(
        [
            -jnp.sum(edge1[:, None] * firsts, axis=(0, 2)),
            jnp.sum(tail1[:, 1] * edge4, axis=0), jnp.sum(edge4, axis=0),
        ]
    )

    small = jnp.concatenate([small1, small2])
    small, input_grad = settle([r_kv], small, input_grad)
    small = Summing(small)
    r_kv.start(z1)
    small.start(c)
    small.finish()
    small.start(y)
    (orf,) = settle([r_kv, small, r_f], orf)
    for z in reversed(z2):
        r_kv.start(z)
        if z != z2[0]:
            settle([r_kv])
    out_f = Growing(r_f.value)
    out_f.start(y)
    orf_got = swap(orf, y)
    small.start(x)
    small.finish()
    small.start(z1)
    (orf_got,) = settle([r_kv, small, out_f], orf_got)
    out_f.start(c)
    orf = add_low(orf, orf_got)
    orf_c = swap(orf, c)
    own = r_kv.value
    last_z = list(reversed(z2))
    for z in last_z[:-1]:
        small.start(z)
        small.finish()
    small.start(last_z[-1])
    at_y, at_c = swap(own, y), swap(own, c)
    at_both = lax.ppermute(own, (y, c), [(i, 3 - i) for i in range(4)])
    at_y, at_c, at_both, orf_c = settle([small, out_f], at_y, at_c, at_both, orf_c)
    small = small.value
    out_kv = join(join(own, at_c, c, 0), join(at_y, at_both, c, 0), y, 0)

    wide_out = lambda v, i: v[:, :, i].reshape(shard, -1)
    out_f = out_f.value.reshape(2 * seq, shard, side)
    grad_fk = jnp.concatenate([out_f[i] for i in range(2 * seq)], axis=1).astype(F32)
    grad_fv = out_v.value.reshape(hid, D).astype(F32)
    orf = join(orf, orf_c, c, 0).reshape(shard, 3 * D).astype(F32)
    grad_o, grad_r, grad_fr = [orf[:, i * D : i * D + D] for i in range(3)]
    grad_k, grad_v = [wide_out(out_kv, i).astype(F32) for i in range(2)]
    rows = lax.dynamic_slice_in_dim(small[:11], my_dp * shard, shard, 1)
    rms = jnp.sqrt(small[11, :3] / (jnp.sum(lengths).astype(F32) * D))
    v = [rows[i] for i in range(11)]
    return (
        block_out, input_grad,
        v[3], v[4], v[0], v[1], v[2], v[5], v[6],
        grad_k, grad_v, grad_r, grad_o,
        v[9], v[10], v[7], v[8],
        grad_fk, grad_fr, grad_fv,
        rms[0], rms[1], rms[2],
    )


def solution(mesh):
    dp_axes, seq_axes = axes_of("d", mesh.shape["dp"]), axes_of("s", mesh.shape["seq"])
    names = dp_axes + seq_axes
    fine = jax.sharding.Mesh(mesh.devices.reshape((2,) * len(names)), names)
    big, vec, mat = P(dp_axes, seq_axes, None), P(dp_axes), P(dp_axes, None)
    args = (big, big, P(), P()) + (vec,) * 7 + (mat,) * 4 + (vec,) * 4 + (mat,) * 3
    outs = (big, big) + (vec,) * 7 + (mat,) * 4 + (vec,) * 4 + (mat,) * 3 + (P(),) * 3
    return jax.shard_map(
        functools.partial(per_device, dp_axes, seq_axes),
        mesh=fine, in_specs=args, out_specs=outs, check_vma=False,
    )
```

```python
import functools

import jax
import jax.numpy as jnp
from jax import lax
from jax.experimental import pallas as pl
from jax.experimental.layout import Layout, with_layout_constraint
from jax.experimental.pallas import tpu as pltpu
from jax.sharding import PartitionSpec as P

D = 1024
EPS = 1e-05
F32 = jnp.float32
BF16 = jnp.bfloat16


LIGHT = pl.CostEstimate(flops=1 << 20, bytes_accessed=1 << 16, transcendentals=0)


def axes_of(letter, size):
    return tuple(f"{letter}{bit}" for bit in reversed(range(size.bit_length() - 1)))


def swap(value, key):
    return lax.ppermute(value, key, [(0, 1), (1, 0)])


def place(held, key):
    rank = lambda k: (k[0] == "s", -int(k[1:]))
    return sum(1 for other in held if rank(other) < rank(key))


def join(mine, other, key, at):
    shape = mine.shape[:at] + (2,) + mine.shape[at:]
    side = lax.broadcasted_iota(jnp.int32, shape, at)
    return jnp.where(side == lax.axis_index(key), jnp.expand_dims(mine, at), jnp.expand_dims(other, at))


def half(value, which, at):
    return lax.dynamic_index_in_dim(value, which, at, keepdims=False)


def add_low(mine, other):
    return (mine.astype(F32) + other.astype(F32)).astype(BF16)


def tie(*values):
    return lax.optimization_barrier(values)


def row_major(value):
    return with_layout_constraint(value, Layout(tuple(range(value.ndim))))


class Moving:
    def start(self, key):
        self.prepare(key)
        self.go()

    def go(self):
        self.got = swap(self.send, self.key)

    def finish(self):
        pass


class Plain(Moving):
    def __init__(self, value, key):
        self.send, self.key = value, key


class Growing(Moving):
    def __init__(self, value):
        self.value, self.held = value, []

    def prepare(self, key):
        self.key, self.send = key, self.value

    def finish(self):
        at = place(self.held, self.key)
        self.held.append(self.key)
        self.value = join(self.value, self.got, self.key, at)


class Shrinking(Moving):
    def __init__(self, parts, merge, held):
        self.parts, self.merge, self.held = parts, merge, list(held)

    def prepare(self, key):
        self.key = key
        self.held.remove(key)
        self.at = place(self.held, key)
        self.bit = lax.axis_index(key)
        self.send = self.merge([half(p, 1 - self.bit, self.at) for p in self.parts])

    def finish(self):
        self.value = add_low(self.merge([half(p, self.bit, self.at) for p in self.parts]), self.got)
        self.parts, self.merge = [self.value], only


class Summing(Moving):
    def __init__(self, value):
        self.value = value

    def prepare(self, key):
        self.key, self.send = key, self.value

    def finish(self):
        self.value = self.value + self.got


def fire(items, *others):
    tied = tie(*[item.send for item in items], *others)
    for item, send in zip(items, tied):
        item.send = send
        item.go()
    return tied[len(items) :]


def only(parts):
    (part,) = parts
    return part


def stacked(parts):
    return jnp.stack(parts, axis=-3)


def settle(items, *others):
    tied = tie(*[item.got for item in items], *others)
    for item, got in zip(items, tied):
        item.got = got
        item.finish()
    return tied[len(items) :]


ROWS = 8


def fwd_kernel(k_ref, v_ref, r_ref, rate_ref, u_ref, a0_ref, b0_ref, w_ref, a_ref, b_ref):
    rate = rate_ref[...]
    boost = jnp.exp(u_ref[...])
    width = rate.shape[1]
    row = lax.broadcasted_iota(jnp.int32, (ROWS, width), 0)
    rowf = row.astype(F32)
    falling = jnp.exp(-rowf * rate)
    one = jnp.exp(-rate)
    steps = [(s, jnp.where(row >= s, jnp.exp(-s * rate), 0.0)) for s in (1, 2, 4)]
    inner = row >= 1

    def scan(tile, carry):
        before = jnp.where(inner, pltpu.roll(tile, 1, 0), 0.0)
        for s, factor in steps:
            before = before + factor * pltpu.roll(before, s, 0)
        before = before + falling * carry
        after = one * before[ROWS - 1 :, :] + tile[ROWS - 1 :, :]
        return before, after

    def tile_of(key, val, recept, carry):
        num, den = carry
        power = jnp.exp(key)
        num_before, num = scan(power * val, num)
        den_before, den = scan(power, den)
        now = boost * power
        mixed = (num_before + now * val) / (den_before + now)
        return (jax.nn.sigmoid(recept) * mixed, num_before, den_before), (num, den)

    def body(i, carry):
        at = pl.ds(pl.multiple_of(i * (2 * ROWS), 2 * ROWS), 2 * ROWS)
        key, val, recept = k_ref[at, :], v_ref[at, :].astype(F32), r_ref[at, :].astype(F32)
        low, carry = tile_of(key[:ROWS], val[:ROWS], recept[:ROWS], carry)
        high, carry = tile_of(key[ROWS:], val[ROWS:], recept[ROWS:], carry)
        for ref, a, b in zip((w_ref, a_ref, b_ref), low, high):
            ref[at, :] = jnp.concatenate([a, b], axis=0).astype(ref.dtype)
        return carry

    lax.fori_loop(
        0, k_ref.shape[0] // (2 * ROWS), body, (a0_ref[...], b0_ref[...]), unroll=2
    )


def bwd_kernel(
    k_ref, v_ref, a_ref, b_ref, p_ref, rate_ref, u_ref, ga_ref, gb_ref,
    dk_ref, dv_ref, first_ref, decay_ref,
):
    rate = rate_ref[...]
    boost = jnp.exp(u_ref[...])
    width = rate.shape[1]
    row = lax.broadcasted_iota(jnp.int32, (ROWS, width), 0)
    rowf = row.astype(F32)
    trailing = jnp.exp(-(ROWS - 1.0 - rowf) * rate)
    one = jnp.exp(-rate)
    steps = [(s, jnp.where(row < ROWS - s, jnp.exp(-s * rate), 0.0)) for s in (1, 2, 4)]
    inner = row < ROWS - 1

    def scan(tile, carry):
        later = jnp.where(inner, pltpu.roll(tile, ROWS - 1, 0), 0.0)
        for s, factor in steps:
            later = later + factor * pltpu.roll(later, ROWS - s, 0)
        later = later + trailing * carry
        before = one * later[:1, :] + tile[:1, :]
        return later, before

    def tile_of(tiles, carry):
        num, den, first, decay = carry
        key, val, num_before, den_before, p = tiles
        power = jnp.exp(key)
        now = boost * power
        q = -p * (num_before + now * val) / (den_before + now)
        num_later, num = scan(p, num)
        den_later, den = scan(q, den)
        diagonal = now * (val * p + q)
        d_key = power * (val * num_later + den_later) + diagonal
        d_val = power * num_later + now * p
        first = first + diagonal
        decay = decay + (num_later * num_before + den_later * den_before)
        return (d_key, d_val), (num, den, first, decay)

    count = k_ref.shape[0] // (2 * ROWS)

    def body(i, carry):
        at = pl.ds(pl.multiple_of((count - 1 - i) * (2 * ROWS), 2 * ROWS), 2 * ROWS)
        tiles = [ref[at, :].astype(F32) for ref in (k_ref, v_ref, a_ref, b_ref, p_ref)]
        high, carry = tile_of([tile[ROWS:] for tile in tiles], carry)
        low, carry = tile_of([tile[:ROWS] for tile in tiles], carry)
        for ref, a, b in zip((dk_ref, dv_ref), low, high):
            ref[at, :] = jnp.concatenate([a, b], axis=0).astype(BF16)
        return carry

    zero = jnp.zeros((ROWS, width), F32)
    done = lax.fori_loop(0, count, body, (ga_ref[...], gb_ref[...], zero, zero), unroll=2)
    first_ref[...] = done[2]
    decay_ref[...] = done[3]


def share_kernel(
    da_ref, w_ref, k_ref, v_ref, r_ref, a_ref, b_ref, rate_ref, u_ref,
    p_ref, dr_ref, ga_ref, gb_ref, dw_ref,
):
    dw_ref[...] = lax.dot_general(
        da_ref[...], w_ref[...], (((1,), (1,)), ((), ())), preferred_element_type=F32
    )
    rate = rate_ref[...]
    boost = jnp.exp(u_ref[...])
    rows = 2 * ROWS
    rowf = lax.broadcasted_iota(jnp.int32, (rows, rate.shape[1]), 0).astype(F32)
    near = jnp.exp(-rowf * rate)

    def body(i, carry):
        ga, gb = carry
        at = pl.ds(pl.multiple_of(i * rows, rows), rows)
        now = boost * jnp.exp(k_ref[at, :])
        inverse = 1.0 / (b_ref[at, :].astype(F32) + now)
        mixed = (a_ref[at, :].astype(F32) + now * v_ref[at, :].astype(F32)) * inverse
        gate = jax.nn.sigmoid(r_ref[at, :].astype(F32))
        d_mixed = dw_ref[at, :] * gate
        dr_ref[at, :] = (d_mixed * mixed * (1.0 - gate)).astype(BF16)
        p_low = (d_mixed * inverse).astype(BF16)
        p_ref[at, :] = p_low
        p = p_low.astype(F32)
        q = -p * mixed
        fall = near * jnp.exp(-(i * rows).astype(F32) * rate)
        return ga + fall * p, gb + fall * q

    zero = jnp.zeros((rows, rate.shape[1]), F32)
    ga, gb = lax.fori_loop(0, k_ref.shape[0] // rows, body, (zero, zero), unroll=2)
    ga_ref[...] = ga[:ROWS] + ga[ROWS:]
    gb_ref[...] = gb[:ROWS] + gb[ROWS:]


WIDTH = 256


def wkv_specs(rows):
    big = pl.BlockSpec((rows, WIDTH), lambda s, c: (s, c))
    row = pl.BlockSpec((1, WIDTH), lambda s, c: (0, c))
    state = pl.BlockSpec((None, 1, WIDTH), lambda s, c: (s, 0, c))
    partial = pl.BlockSpec((None, ROWS, WIDTH), lambda s, c: (s, 0, c))
    return big, row, state, partial


def wkv_forward(keys, vals, recepts, rate, first, num, den, seqs):
    total = keys.shape[0]
    big, row, state, _ = wkv_specs(total // seqs)
    cells = total * D
    return pl.pallas_call(
        fwd_kernel,
        grid=(seqs, D // WIDTH),
        in_specs=[big, big, big, row, row, state, state],
        out_specs=[big, big, big],
        out_shape=[
            jax.ShapeDtypeStruct((total, D), BF16),
            jax.ShapeDtypeStruct((total, D), F32),
            jax.ShapeDtypeStruct((total, D), F32),
        ],
        compiler_params=pltpu.CompilerParams(vmem_limit_bytes=58 << 20),
        cost_estimate=LIGHT,
    )(keys, vals, recepts, rate, first, num, den)


def wkv_backward(keys, vals, num_before, den_before, p, rate, first, num, den, seqs):
    total = keys.shape[0]
    big, row, state, partial = wkv_specs(total // seqs)
    cells = total * D
    return pl.pallas_call(
        bwd_kernel,
        grid=(seqs, D // WIDTH),
        in_specs=[big, big, big, big, big, row, row, state, state],
        out_specs=[big, big, partial, partial],
        out_shape=[
            jax.ShapeDtypeStruct((total, D), BF16),
            jax.ShapeDtypeStruct((total, D), BF16),
            jax.ShapeDtypeStruct((seqs, ROWS, D), F32),
            jax.ShapeDtypeStruct((seqs, ROWS, D), F32),
        ],
        compiler_params=pltpu.CompilerParams(vmem_limit_bytes=58 << 20),
        cost_estimate=LIGHT,
    )(keys, vals, num_before, den_before, p, rate, first, num, den)


def share_back(d_attn, weight, keys, vals, recepts, num_before, den_before, rate, first, seqs):
    total = keys.shape[0]
    span = total // seqs
    big, row, _, partial = wkv_specs(span)
    cells = total * D
    return pl.pallas_call(
        share_kernel,
        grid=(seqs, D // WIDTH),
        in_specs=[
            pl.BlockSpec((span, D), lambda s, c: (s, 0)),
            pl.BlockSpec((WIDTH, D), lambda s, c: (c, 0)),
            big, big, big, big, big, row, row,
        ],
        out_specs=[big, big, partial, partial],
        out_shape=[
            jax.ShapeDtypeStruct((total, D), BF16),
            jax.ShapeDtypeStruct((total, D), BF16),
            jax.ShapeDtypeStruct((seqs, ROWS, D), F32),
            jax.ShapeDtypeStruct((seqs, ROWS, D), F32),
        ],
        scratch_shapes=[pltpu.VMEM((span, WIDTH), F32)],
        compiler_params=pltpu.CompilerParams(vmem_limit_bytes=58 << 20),
        cost_estimate=LIGHT,
    )(d_attn, weight, keys, vals, recepts, num_before, den_before, rate, first)


PIECES = 8


def load_pieces(refs, held, sems):
    left, right = refs[:4], refs[4:]
    per = 4 // held.shape[0]
    whole = held.shape[2] // per
    copies = []
    for p in range(4):
        at = (p % per) * whole
        for ref in (left[p], right[p % 2].at[p // 2]):
            width = ref.shape[-1]
            copies.append(
                pltpu.make_async_copy(ref, held.at[p // per, :, pl.ds(at, width)], sems.at[len(copies)])
            )
            at += width
    return copies


def feed_kernel(s_ref, left_ref, x_ref, *rest):
    refs = rest[:6]
    fv_ref, xr_ref, fr_ref, mid_ref, cot_ref = rest[6:11]
    sq_ref, out_ref, dval_ref, dgate_ref, sums = rest[11:16]
    held, held_v, acc, gate_acc, sems, sems_v = rest[16:]
    copies = load_pieces(refs, held, sems)
    deep = held_v.shape[1]
    copies_v = [
        pltpu.make_async_copy(fv_ref.at[pl.ds(h * deep, deep)], held_v.at[h], sems_v.at[h])
        for h in range(2)
    ]
    first = pl.program_id(0) == 0
    width = held.shape[2]

    @pl.when(first)
    def _():
        for copy in copies + copies_v:
            copy.start()

    for p in range(4):

        @pl.when(first)
        def _(p=p):
            copies[2 * p].wait()
            copies[2 * p + 1].wait()

        hidden = jnp.maximum(jnp.dot(x_ref[...], held[p], preferred_element_type=F32), 0.0)
        at = pl.multiple_of(jnp.bitwise_xor(s_ref[0], p) * width, width)
        sq_ref[:, pl.ds(at, width)] = (hidden * hidden).astype(BF16)

    gate_acc[...] = jnp.dot(xr_ref[...], fr_ref[...], preferred_element_type=F32)
    total = None
    for h in range(2):

        @pl.when(first)
        def _(h=h):
            copies_v[h].wait()

        part = jnp.dot(sq_ref[:, pl.ds(h * deep, deep)], held_v[h], preferred_element_type=F32)
        total = part if total is None else total + part
    acc[...] = total

    left = left_ref[pl.program_id(0)]
    sums[...] = jnp.zeros_like(sums)

    def body(i, _):
        start = pl.multiple_of(i * 2 * ROWS, 2 * ROWS)
        at = pl.ds(start, 2 * ROWS)
        rows = start + lax.broadcasted_iota(jnp.int32, (2 * ROWS, 1), 0)
        keep = rows < left
        gate = jax.nn.sigmoid(gate_acc[at, :])
        feed = jnp.where(keep, gate * acc[at, :], 0.0)
        result = jnp.where(keep, mid_ref[at, :], 0.0) + feed
        g = jnp.where(keep, cot_ref[at, :].astype(F32), 0.0)
        out_ref[at, :] = result.astype(BF16)
        dval_ref[at, :] = (g * gate).astype(BF16)
        dgate_ref[at, :] = (g * feed * (1.0 - gate)).astype(BF16)
        sums[0] += fold(result * result)
        sums[1] += fold(feed * feed)
        return 0

    lax.fori_loop(0, mid_ref.shape[0] // (2 * ROWS), body, 0, unroll=2)


def feed_forward(my_seq, left, inputs, pieces, weight, gate_inputs, gate_weight, middle, cotangent, seqs):
    total = inputs.shape[0]
    width = pieces[0].shape[1] + pieces[4].shape[2]
    span = total // seqs
    ff = 4 * width
    big = pl.BlockSpec((span, D), lambda i, *_: (i, 0))
    return pl.pallas_call(
        feed_kernel,
        grid_spec=pltpu.PrefetchScalarGridSpec(
            num_scalar_prefetch=2,
            grid=(seqs,),
            in_specs=[big]
            + [pl.BlockSpec(memory_space=pl.ANY)] * 7
            + [big, pl.BlockSpec((D, D), lambda i, *_: (0, 0), pipeline_mode=pl.Buffered(1)), big, big],
            out_specs=[
                pl.BlockSpec((span, ff), lambda i, *_: (i, 0)), big, big, big,
                pl.BlockSpec((None, 2, ROWS, D), lambda i, *_: (i, 0, 0, 0)),
            ],
            scratch_shapes=[
                pltpu.VMEM((4, D, width), BF16),
                pltpu.VMEM((2, 2 * width, D), BF16),
                pltpu.VMEM((span, D), F32),
                pltpu.VMEM((span, D), F32),
                pltpu.SemaphoreType.DMA((PIECES,)),
                pltpu.SemaphoreType.DMA((2,)),
            ],
        ),
        out_shape=[
            jax.ShapeDtypeStruct((total, ff), BF16),
            jax.ShapeDtypeStruct((total, D), BF16),
            jax.ShapeDtypeStruct((total, D), BF16),
            jax.ShapeDtypeStruct((total, D), BF16),
            jax.ShapeDtypeStruct((seqs, 2, ROWS, D), F32),
        ],
        compiler_params=pltpu.CompilerParams(vmem_limit_bytes=60 << 20),
        cost_estimate=LIGHT,
    )(my_seq[None], left, inputs, *pieces, weight, gate_inputs, gate_weight, middle, cotangent)


CHUNK = 128


def stats_of(values):
    centre = values - jnp.mean(values, axis=-1, keepdims=True)
    inverse = lax.rsqrt(jnp.mean(centre * centre, axis=-1, keepdims=True) + EPS)
    return centre * inverse, inverse


def norm_back(grads, normed, inverse):
    return inverse * (
        grads
        - jnp.mean(grads, axis=-1, keepdims=True)
        - normed * jnp.mean(grads * normed, axis=-1, keepdims=True)
    )


def fold(values):
    return jnp.sum(values.reshape(values.shape[0] // ROWS, ROWS, values.shape[1]), axis=0)


def next_rows(values, carry):
    last = lax.broadcasted_iota(jnp.int32, values.shape, 0) == CHUNK - 1
    return jnp.where(last, carry, pltpu.roll(values, CHUNK - 1, 0))


def previous_rows(values, carry):
    first = lax.broadcasted_iota(jnp.int32, values.shape, 0) == 0
    return jnp.where(first, carry, pltpu.roll(values, 1, 0))


def mid_kernel(
    left_ref, w_ref, weight_ref, x_ref, gain_ref, bias_ref, mk_ref, mr_ref,
    mid_ref, fk_ref, fr_ref, first_ref, sq_ref,
):
    mid_ref[...] = jnp.dot(w_ref[...], weight_ref[...], preferred_element_type=F32)
    left = left_ref[pl.program_id(0)]
    gain, bias, mix_k, mix_r = gain_ref[...], bias_ref[...], mk_ref[...], mr_ref[...]
    sq_ref[...] = jnp.zeros_like(sq_ref)

    def body(i, carry):
        start = pl.multiple_of(i * CHUNK, CHUNK)
        at = pl.ds(start, CHUNK)
        attn = mid_ref[at, :]
        rows = start + lax.broadcasted_iota(jnp.int32, (CHUNK, 1), 0)
        sq_ref[...] += fold(jnp.where(rows < left, attn * attn, 0.0))
        middle = x_ref[at, :].astype(F32) + attn
        mid_ref[at, :] = middle
        b = stats_of(middle)[0] * gain + bias
        before = previous_rows(b, carry)
        fk_ref[at, :] = (b * mix_k + before * (1.0 - mix_k)).astype(BF16)
        fr_ref[at, :] = (b * mix_r + before * (1.0 - mix_r)).astype(BF16)

        @pl.when(i == 0)
        def _():
            first_ref[...] = b[:1, :]

        return b[CHUNK - 1 :, :]

    lax.fori_loop(0, x_ref.shape[0] // CHUNK, body, jnp.zeros_like(gain), unroll=2)


def mid_forward(left, weighted, weight, tokens, gain, bias, mix_k, mix_r, seqs):
    total = tokens.shape[0]
    span = total // seqs
    big = pl.BlockSpec((span, D), lambda s, _: (s, 0))
    row = pl.BlockSpec((1, D), lambda s, _: (0, 0))
    tile = lambda rows: pl.BlockSpec((None, rows, D), lambda s, _: (s, 0, 0))
    return pl.pallas_call(
        mid_kernel,
        grid_spec=pltpu.PrefetchScalarGridSpec(
            num_scalar_prefetch=1,
            grid=(seqs,),
            in_specs=[big, pl.BlockSpec((D, D), lambda s, _: (0, 0)), big, row, row, row, row],
            out_specs=[big, big, big, tile(1), tile(ROWS)],
        ),
        out_shape=[
            jax.ShapeDtypeStruct((total, D), F32),
            jax.ShapeDtypeStruct((total, D), BF16),
            jax.ShapeDtypeStruct((total, D), BF16),
            jax.ShapeDtypeStruct((seqs, 1, D), F32),
            jax.ShapeDtypeStruct((seqs, ROWS, D), F32),
        ],
        compiler_params=pltpu.CompilerParams(vmem_limit_bytes=58 << 20),
        cost_estimate=LIGHT,
    )(left, weighted, weight, tokens, gain, bias, mix_k, mix_r)


def down_kernel(s_ref, left_ref, dval_ref, fv_ref, sq_ref, *rest):
    refs = rest[:6]
    gate_ref, fr_ref, mid_ref, cot_ref, gain_ref, bias_ref, mk_ref, mr_ref = rest[6:14]
    dh_ref, out_ref, low_ref, first_k, first_r, tail_ref, sums = rest[14:21]
    held, held_v, held_sq, acc_k, acc_r, sems, sems_v, sems_sq = rest[21:]
    copies = load_pieces(refs, held, sems)
    width = held_v.shape[1]
    places = [pl.multiple_of(jnp.bitwise_xor(s_ref[0], p) * width, width) for p in range(4)]
    copies_v = [
        pltpu.make_async_copy(fv_ref.at[pl.ds(places[p], width)], held_v.at[p], sems_v.at[p])
        for p in range(4)
    ]
    span = held_sq.shape[1]
    rows = pl.ds(pl.multiple_of(pl.program_id(0) * span, span), span)
    copies_sq = [
        pltpu.make_async_copy(sq_ref.at[rows, pl.ds(places[p], width)], held_sq.at[p], sems_sq.at[p])
        for p in range(4)
    ]
    first = pl.program_id(0) == 0
    back = (((1,), (1,)), ((), ()))
    for copy in copies_sq[:1]:
        copy.start()

    @pl.when(first)
    def _():
        copies_v[0].start()

    for copy in copies_sq[1:]:
        copy.start()

    @pl.when(first)
    def _():
        for copy in copies_v[1:] + copies:
            copy.start()

    for p in range(4):
        copies_sq[p].wait()

        @pl.when(first)
        def _(p=p):
            copies_v[p].wait()

        for side in range(2):
            part = pl.ds(side * (width // 2), width // 2)
            d_sq = lax.dot_general(dval_ref[...], held_v[p, part, :], back, preferred_element_type=F32)
            squared = held_sq[p, :, part].astype(F32)
            twice = 2.0 * squared * lax.rsqrt(jnp.maximum(squared, 1e-37))
            dh_ref[p, :, part] = (twice * d_sq).astype(BF16)

    acc_r[...] = lax.dot_general(gate_ref[...], fr_ref[...], back, preferred_element_type=F32)
    for h in range(2):

        @pl.when(first)
        def _(h=h):
            for copy in copies[4 * h : 4 * h + 4]:
                copy.wait()

        part = lax.dot_general(
            jnp.concatenate([dh_ref[2 * h], dh_ref[2 * h + 1]], axis=1), held[h],
            back, preferred_element_type=F32,
        )
        acc_k[...] = part if h == 0 else acc_k[...] + part

    left = left_ref[pl.program_id(0)]
    gain, bias, mix_k, mix_r = gain_ref[...], bias_ref[...], mk_ref[...], mr_ref[...]
    sums[...] = jnp.zeros_like(sums)
    count = mid_ref.shape[0] // CHUNK

    def body(i, carry):
        later_k, later_r = carry
        start = pl.multiple_of((count - 1 - i) * CHUNK, CHUNK)
        at = pl.ds(start, CHUNK)
        d_fk, d_fr = acc_k[at, :], acc_r[at, :]
        next_k, next_r = next_rows(d_fk, later_k), next_rows(d_fr, later_r)
        n, inverse = stats_of(mid_ref[at, :])
        b = n * gain + bias
        db = d_fk * mix_k + next_k * (1.0 - mix_k) + d_fr * mix_r + next_r * (1.0 - mix_r)
        sums[0] += fold(b * (d_fk - next_k))
        sums[1] += fold(b * (d_fr - next_r))
        sums[2] += fold(n * db)
        sums[3] += fold(db)
        rows = start + lax.broadcasted_iota(jnp.int32, (CHUNK, 1), 0)
        g = jnp.where(rows < left, cot_ref[at, :].astype(F32), 0.0)
        d_middle = g + norm_back(db * gain, n, inverse)
        out_ref[at, :] = d_middle
        low_ref[at, :] = d_middle.astype(BF16)

        @pl.when(i == 0)
        def _():
            tail_ref[0] = d_middle[CHUNK - 1 :, :]
            tail_ref[1] = n[CHUNK - 1 :, :]
            tail_ref[2] = jnp.broadcast_to(inverse[CHUNK - 1 :, :], gain.shape)

        return d_fk[:1, :], d_fr[:1, :]

    zero = jnp.zeros_like(gain)
    first_k[...], first_r[...] = lax.fori_loop(0, count, body, (zero, zero), unroll=2)


def down(
    my_seq, left, grads, weight, squared, pieces, gate_grads, gate_weight,
    middle, cotangent, gain, bias, mix_k, mix_r, seqs,
):
    total, ff = squared.shape
    span = total // seqs
    width = ff // 4
    big = pl.BlockSpec((span, D), lambda s, *_: (s, 0))
    alone = pl.BlockSpec((span, D), lambda s, *_: (s, 0), pipeline_mode=pl.Buffered(1))
    row = pl.BlockSpec((1, D), lambda s, *_: (0, 0))
    one = pl.BlockSpec((None, 1, D), lambda s, *_: (s, 0, 0))
    return pl.pallas_call(
        down_kernel,
        grid_spec=pltpu.PrefetchScalarGridSpec(
            num_scalar_prefetch=2,
            grid=(seqs,),
            in_specs=[
                big,
                pl.BlockSpec(memory_space=pl.ANY),
                pl.BlockSpec(memory_space=pl.ANY),
            ]
            + [pl.BlockSpec(memory_space=pl.ANY)] * 6
            + [big, pl.BlockSpec((D, D), lambda s, *_: (0, 0), pipeline_mode=pl.Buffered(1)), alone, big]
            + [row] * 4,
            out_specs=[
                pl.BlockSpec((4, span, width), lambda s, *_: (0, s, 0)),
                big, big, one, one,
                pl.BlockSpec((None, 3, 1, D), lambda s, *_: (s, 0, 0, 0)),
                pl.BlockSpec((None, 4, ROWS, D), lambda s, *_: (s, 0, 0, 0)),
            ],
            scratch_shapes=[
                pltpu.VMEM((2, D, 2 * width), BF16),
                pltpu.VMEM((4, width, D), BF16),
                pltpu.VMEM((4, span, width), BF16),
                pltpu.VMEM((span, D), F32),
                pltpu.VMEM((span, D), F32),
                pltpu.SemaphoreType.DMA((PIECES,)),
                pltpu.SemaphoreType.DMA((4,)),
                pltpu.SemaphoreType.DMA((4,)),
            ],
        ),
        out_shape=[
            jax.ShapeDtypeStruct((4, total, width), BF16),
            jax.ShapeDtypeStruct((total, D), F32),
            jax.ShapeDtypeStruct((total, D), BF16),
            jax.ShapeDtypeStruct((seqs, 1, D), F32),
            jax.ShapeDtypeStruct((seqs, 1, D), F32),
            jax.ShapeDtypeStruct((seqs, 3, 1, D), F32),
            jax.ShapeDtypeStruct((seqs, 4, ROWS, D), F32),
        ],
        compiler_params=pltpu.CompilerParams(vmem_limit_bytes=60 << 20),
        cost_estimate=LIGHT,
    )(
        my_seq[None], left, grads, weight, squared, *pieces, gate_grads, gate_weight,
        middle, cotangent, gain, bias, mix_k, mix_r,
    )


def mix_kernel(
    dk_ref, dv_ref, dr_ref, wk_ref, wv_ref, wr_ref, x_ref, dm_ref,
    gain_ref, bias_ref, mk_ref, mv_ref, mr_ref,
    out_ref, firsts, tail_ref, sums, acc, held, sems,
):
    first = pl.program_id(0) == 0
    copies = [
        pltpu.make_async_copy(ref, held.at[i], sems.at[i]) for i, ref in enumerate((wk_ref, wv_ref, wr_ref))
    ]

    @pl.when(first)
    def _():
        for copy in copies:
            copy.start()

    for i, grads in enumerate((dk_ref, dv_ref, dr_ref)):

        @pl.when(first)
        def _(i=i):
            copies[i].wait()

        acc[i] = lax.dot_general(
            grads[...], held[i], (((1,), (1,)), ((), ())), preferred_element_type=F32
        )
    gain, bias = gain_ref[...], bias_ref[...]
    mixes = (mk_ref[...], mv_ref[...], mr_ref[...])
    sums[...] = jnp.zeros_like(sums)
    count = x_ref.shape[0] // CHUNK

    def body(i, carry):
        start = pl.multiple_of((count - 1 - i) * CHUNK, CHUNK)
        at = pl.ds(start, CHUNK)
        n, inverse = stats_of(x_ref[at, :].astype(F32))
        a = n * gain + bias
        da, heads = None, []
        for j in range(3):
            d = acc[j, at, :]
            later = next_rows(d, carry[j])
            sums[j] += fold(a * (d - later))
            part = d * mixes[j] + later * (1.0 - mixes[j])
            da = part if da is None else da + part
            heads.append(d[:1, :])
        sums[3] += fold(n * da)
        sums[4] += fold(da)
        total = dm_ref[at, :] + norm_back(da * gain, n, inverse)
        out_ref[at, :] = total.astype(BF16)

        @pl.when(i == 0)
        def _():
            tail_ref[0] = total[CHUNK - 1 :, :]
            tail_ref[1] = n[CHUNK - 1 :, :]
            tail_ref[2] = jnp.broadcast_to(inverse[CHUNK - 1 :, :], gain.shape)

        return tuple(heads)

    zero = jnp.zeros_like(gain)
    heads = lax.fori_loop(0, count, body, (zero, zero, zero), unroll=2)
    for j in range(3):
        firsts[j] = heads[j]


def mix_back(d_keys, d_vals, d_recepts, w_k, w_v, w_r, tokens, d_middle, gain, bias, mix_k, mix_v, mix_r, seqs):
    total = tokens.shape[0]
    span = total // seqs
    big = pl.BlockSpec((span, D), lambda s: (s, 0))
    row = pl.BlockSpec((1, D), lambda s: (0, 0))
    full = pl.BlockSpec(memory_space=pl.ANY)
    return pl.pallas_call(
        mix_kernel,
        grid=(seqs,),
        in_specs=[big, big, big, full, full, full, big, big] + [row] * 5,
        out_specs=[
            big,
            pl.BlockSpec((None, 3, 1, D), lambda s: (s, 0, 0, 0)),
            pl.BlockSpec((None, 3, 1, D), lambda s: (s, 0, 0, 0)),
            pl.BlockSpec((None, 5, ROWS, D), lambda s: (s, 0, 0, 0)),
        ],
        out_shape=[
            jax.ShapeDtypeStruct((total, D), BF16),
            jax.ShapeDtypeStruct((seqs, 3, 1, D), F32),
            jax.ShapeDtypeStruct((seqs, 3, 1, D), F32),
            jax.ShapeDtypeStruct((seqs, 5, ROWS, D), F32),
        ],
        scratch_shapes=[
            pltpu.VMEM((3, span, D), F32),
            pltpu.VMEM((3, D, D), BF16),
            pltpu.SemaphoreType.DMA((3,)),
        ],
        compiler_params=pltpu.CompilerParams(vmem_limit_bytes=58 << 20),
        cost_estimate=LIGHT,
    )(d_keys, d_vals, d_recepts, w_k, w_v, w_r, tokens, d_middle, gain, bias, mix_k, mix_v, mix_r)


def put_rows(values, rows, at):
    seqs = rows.shape[0]
    whole = values.reshape(seqs, values.shape[0] // seqs, D)
    return lax.dynamic_update_slice(whole, rows.astype(values.dtype), (0, at, 0)).reshape(values.shape)


def cut_kernel(_, k, v, r, o, fk, rows, kv_out, ro_out, f1_out, f2_out, row_out):
    kv_out[0], kv_out[1] = k[...], v[...]
    ro_out[0], ro_out[1] = r[...], o[...]
    left = f1_out.shape[1]
    f1_out[...], f2_out[...] = fk[:, :left], fk[:, left:]
    last = rows.shape[1] - 1
    row_out[...] = rows[...].astype(F32)[:, last:, :]


def cut(my_seq, quarter, key, value, recept, output, feed_key, tokens):
    seqs, span, _ = tokens.shape
    shard, ff = feed_key.shape
    part = pl.BlockSpec((quarter, D), lambda i, at: (at[0], 0))
    side = pl.BlockSpec((shard, ff // 4), lambda i, at: (0, at[0]))
    left = ff // 32 * 5
    full = lambda *shape: pl.BlockSpec(shape, lambda i, at: (0,) * len(shape))
    shapes = [(2, quarter, D), (2, quarter, D)] + [(shard, left), (shard, ff // 4 - left), (seqs, 1, D)]
    kinds = [BF16] * 4 + [F32]
    return pl.pallas_call(
        cut_kernel,
        grid_spec=pltpu.PrefetchScalarGridSpec(
            num_scalar_prefetch=1,
            grid=(1,),
            in_specs=[part] * 4
            + [side, pl.BlockSpec((seqs, 2 * ROWS, D), lambda i, at: (0, span // (2 * ROWS) - 1, 0))],
            out_specs=[full(*shape) for shape in shapes],
        ),
        out_shape=[jax.ShapeDtypeStruct(shape, kind) for shape, kind in zip(shapes, kinds)],
    )(my_seq[None], key, value, recept, output, feed_key, tokens)


def dot(left, right):
    return jnp.dot(left, right, preferred_element_type=F32)


def dot_back(grads, weight):
    return lax.dot_general(grads, weight, (((1,), (1,)), ((), ())), preferred_element_type=F32)


def dot_weight(inputs, grads):
    return lax.dot_general(inputs, grads, (((0,), (0,)), ((), ())), preferred_element_type=F32)


def normalize(values):
    centre = values - jnp.mean(values, axis=-1, keepdims=True)
    spread = jnp.mean(centre * centre, axis=-1, keepdims=True)
    inverse = lax.rsqrt(spread + EPS)
    return centre * inverse, inverse


def from_behind(value, axes, by):
    count = lax.axis_size(axes)
    pairs = [(i, i + by) for i in range(count) if 0 <= i + by < count]
    return lax.ppermute(value, axes, pairs)


def shifted(rows, edge):
    return jnp.concatenate([edge, rows[:, :-1]], axis=1)


def pulled(rows, edge):
    return jnp.concatenate([rows[:, 1:], edge], axis=1)


def blend(now, before, share):
    return (now * share + before * (1.0 - share)).astype(BF16)


def earlier_state(decay, num, den, axes, backward):
    count = lax.axis_size(axes)
    mine = lax.axis_index(axes)
    packed = lax.all_gather(jnp.concatenate([num, den], axis=0), axes)
    seqs = num.shape[0]
    state = jnp.zeros_like(packed[0])
    for hop in range(count - 1):
        source = count - 1 - hop if backward else hop
        longer = decay * state + packed[source]
        keep = source > mine if backward else source < mine
        state = jnp.where(keep, longer, state)
    return state[:seqs, None, :], state[seqs:, None, :]


def per_device(
    dp_axes, seq_axes,
    tokens, cotangent, lengths, assignment,
    mix_norm_gain, mix_norm_bias, shift_key, shift_value, shift_recept, time_decay, time_first,
    key_weight, value_weight, recept_weight, output_weight,
    feed_norm_gain, feed_norm_bias, feed_shift_key, feed_shift_recept,
    feed_key_weight, feed_recept_weight, feed_value_weight,
):
    seqs, span, _ = tokens.shape
    total = seqs * span
    dp, seq = lax.axis_size(dp_axes), lax.axis_size(seq_axes)
    my_dp, my_seq = lax.axis_index(dp_axes), lax.axis_index(seq_axes)
    every = dp_axes + seq_axes
    z_axes, x = dp_axes[:-1], dp_axes[-1]
    y, c = seq_axes
    ff = feed_key_weight.shape[1]
    flat = lambda v: v.reshape(total, v.shape[-1])
    deep = lambda v: v.reshape(seqs, span, v.shape[-1])

    shard = D // dp
    quarter = shard // seq

    def own_rows(weight):
        return lax.dynamic_slice_in_dim(weight, my_seq * quarter, quarter, 0)

    hid = feed_value_weight.shape[0]
    halves = lambda w: half(w.reshape(2, w.shape[0] // 2, D), lax.axis_index(c), 0)
    gathered = lambda w: lax.all_gather(w, dp_axes + (c,), axis=0, tiled=True)
    w_fr = gathered(halves(feed_recept_weight))
    *cuts, last_token = cut(
        my_seq, quarter, key_weight, value_weight, recept_weight, output_weight, feed_key_weight, tokens
    )
    kv, ro, f1, f2 = [Growing(part) for part in cuts]
    kv.start(z_axes[0])
    ro.start(z_axes[0])
    kv.value, tokens, *vectors = tie(
        kv.value, tokens,
        mix_norm_gain, mix_norm_bias, shift_key, shift_value, shift_recept, time_decay, time_first,
        feed_norm_gain, feed_norm_bias, feed_shift_key, feed_shift_recept,
    )
    vectors = Growing(jnp.stack(vectors))
    vectors.start(z_axes[0])
    edge1 = from_behind(last_token, seq_axes, 1)
    for z in z_axes[1:]:
        (edge1,) = settle([kv, ro, vectors], edge1)
        kv.start(z)
        ro.start(z)
        vectors.start(z)
    f1.value, f2.value = settle([kv, ro, vectors], f1.value, f2.value)
    kv.start(x)
    ro.start(y)
    vectors.start(x)
    f1.start(z_axes[0])
    f2.start(z_axes[0])
    settle([kv, ro, vectors, f1, f2])
    kv.start(y)
    ro.start(x)
    for z in z_axes[1:]:
        f1.start(z)
        f2.start(z)
        if z != z_axes[-1]:
            settle([f1, f2])
    fv_part, w_fr = settle([f1, f2, kv, ro], halves(feed_value_weight), w_fr)
    w_fv = gathered(fv_part)
    kv.prepare(c)
    ro.prepare(c)
    f1.prepare(x)
    f2y = Plain(f2.value, y)
    tokens, vectors.value = fire([kv, ro, f1, f2y], tokens, vectors.value)
    settle([kv, ro])
    pick = lambda v, i: jnp.moveaxis(v, -3, 0)[i].reshape(D, D)
    w_k, w_v, w_r, w_o = pick(kv.value, 0), pick(kv.value, 1), pick(ro.value, 0), pick(ro.value, 1)
    vectors = jnp.swapaxes(vectors.value.reshape(dp, 11, D // dp), 0, 1).reshape(11, D).astype(F32)
    gain1, bias1, mix_k, mix_v, mix_r, log_rate, first, gain2, bias2, fmix_k, fmix_r = [
        vectors[i : i + 1] for i in range(11)
    ]
    rate = jnp.exp(log_rate)
    lam = jnp.exp(-rate)

    slot_ids = jnp.arange(assignment.shape[0])
    my_slots = my_dp * seqs + jnp.arange(seqs)
    seq_ids = jnp.sum(jnp.where(slot_ids[None, :] == my_slots[:, None], assignment[None, :], 0), axis=1)
    my_lens = jnp.sum(jnp.where(slot_ids[None, :] == seq_ids[:, None], lengths[None, :], 0), axis=1)
    positions = my_seq * span + jnp.arange(span)
    valid = flat((positions[None, :] < my_lens[:, None]).astype(F32)[..., None])
    inside = (my_seq > 0).astype(F32)

    xin = tokens.astype(F32)
    edge1 = (normalize(edge1)[0] * gain1 + bias1) * inside
    n1, inv1 = normalize(xin)
    a = n1 * gain1 + bias1
    a_prev = shifted(a, edge1)
    key_in = flat(blend(a, a_prev, mix_k))
    value_in = flat(blend(a, a_prev, mix_v))
    recept_in = flat(blend(a, a_prev, mix_r))
    keys = dot(key_in, w_k)
    vals = dot(value_in, w_v)
    recepts = dot(recept_in, w_r)

    offsets = jnp.arange(span).astype(F32)[:, None]
    power = deep(jnp.exp(keys))
    left = jnp.exp(-(span - 1.0 - offsets) * rate)
    span_decay = jnp.exp(-span * rate)
    num_end = jnp.sum(left * power * deep(vals), axis=1)
    vals, recepts = vals.astype(BF16), recepts.astype(BF16)
    den_end = jnp.sum(left * power, axis=1)
    num0, den0 = earlier_state(span_decay, num_end, den_end, seq_axes, False)
    num0, den0 = settle([f1, f2y], num0, den0)
    f2y = f2y.got
    f1_0 = row_major(f1.value).reshape(D, -1)
    f2.value = jnp.stack([f2.value, f2y], axis=len(f2.held))
    f1_y = Plain(f1_0, y)
    f2.prepare(x)
    num0, den0 = fire([f1_y, f2], num0, den0)
    weighted, num_before, den_before = wkv_forward(keys, vals, recepts, rate, first, num0, den0, seqs)
    (weighted,) = settle([f1_y, f2], weighted)
    f1_y = f1_y.got
    f2_0 = row_major(jnp.moveaxis(f2.value, -3, 0)).reshape(2, D, -1)
    f1_c, f1_yc, f2_c = Plain(f1_0, c), Plain(f1_y, c), Plain(f2_0, c)
    (weighted,) = fire([f1_c, f1_yc, f2_c], weighted)
    last_row = last_token[:, 0] + dot(deep(weighted)[:, -1], w_o)
    edge2 = from_behind(last_row[:, None], seq_axes, 1)
    left_rows = (my_lens - my_seq * span).astype(jnp.int32)
    flat_tokens = flat(tokens)
    middle, feed_key_in, feed_recept_in, b_first, attn_sq = mid_forward(
        left_rows, weighted, w_o, flat_tokens, gain2, bias2, fmix_k, fmix_r, seqs
    )

    edge2 = (normalize(edge2)[0] * gain2 + bias2) * inside
    feed_key_in = put_rows(feed_key_in, blend(b_first, edge2, fmix_k), 0)
    feed_recept_in = put_rows(feed_recept_in, blend(b_first, edge2, fmix_r), 0)
    (feed_key_in,) = settle([f1_c, f1_yc, f2_c], feed_key_in)
    f1_c, f1_yc, f2_c = f1_c.got, f1_yc.got, f2_c.got
    pieces = (f1_0, f1_c, f1_y, f1_yc, f2_0, f2_c)
    sq, block_out, d_fval, d_fgate, squares = feed_forward(
        my_seq, left_rows, feed_key_in, pieces, w_fv, feed_recept_in, w_fr, middle, flat(cotangent), seqs
    )
    block_out = deep(block_out)
    stats = jnp.stack([jnp.sum(squares[:, 0]), jnp.sum(attn_sq), jnp.sum(squares[:, 1])])

    gfv = dot_weight(sq, d_fval).astype(BF16)
    gfv = lax.psum_scatter(gfv, dp_axes + (c,), scatter_dimension=0, tiled=True)
    gfr = dot_weight(feed_recept_in, d_fgate).astype(BF16)
    dh, d_middle, d_attn, first_k, first_r, tail, sums2 = down(
        my_seq, left_rows, d_fval, w_fv, sq, pieces, d_fgate, w_fr,
        middle, flat(cotangent), gain2, bias2, fmix_k, fmix_r, seqs,
    )
    gfk_1 = dot_weight(feed_key_in, dh[1]).astype(BF16)
    gfk_3 = dot_weight(feed_key_in, dh[3]).astype(BF16)

    lead = (2,) * len(every)
    split = lambda g_: Shrinking([g_.reshape(lead + (quarter, D))], only, every)
    side = ff // PIECES
    got_1, got_3 = Plain(gfk_1, c), Plain(gfk_3, c)
    (dh,) = fire([got_1, got_3], dh)
    gfk_0 = dot_weight(feed_key_in, dh[0]).astype(BF16)
    gfk_2 = dot_weight(feed_key_in, dh[2]).astype(BF16)
    edge3 = from_behind(first_k * (1.0 - fmix_k) + first_r * (1.0 - fmix_r), seq_axes, -1)
    d_middle, gfk_0, gfk_2, tail, sums2 = settle([got_1, got_3], d_middle, gfk_0, gfk_2, tail, sums2)
    low = lambda mine, got, at: add_low(mine[:, at : at + side], got.got[:, at : at + side])
    by_dp = lambda g_: g_.reshape((2,) * len(dp_axes) + (shard, g_.shape[1]))
    got_a = Plain(low(gfk_2, got_3, 0), y)
    r2 = Shrinking([by_dp(low(gfk_0, got_1, side)), by_dp(low(gfk_2, got_3, side))], stacked, dp_axes)
    r2.prepare(x)
    (d_attn,) = fire([got_a, r2], d_attn)
    a_0 = low(gfk_0, got_1, 0)

    d_last = tail[:, 0] + norm_back(edge3 * gain2, tail[:, 1], tail[:, 2])
    d_middle = put_rows(d_middle, d_last, span - 1)
    d_attn = put_rows(d_attn, d_last.astype(BF16), span - 1)
    small2 = sums2.sum((0, 2)) + jnp.concatenate(
        [
            -jnp.sum(edge2 * first_k, axis=0), -jnp.sum(edge2 * first_r, axis=0),
            jnp.sum(tail[:, 1] * edge3, axis=0), jnp.sum(edge3, axis=0),
        ]
    )
    p, d_recepts, ga_part, gb_part = share_back(
        d_attn, w_o, keys, vals, recepts, num_before, den_before, rate, first, seqs
    )
    r_o = dot_weight(weighted, d_attn).astype(BF16)
    r_r = dot_weight(recept_in, d_recepts).astype(BF16)
    ga_part, r_o, r_r = settle([r2, got_a], ga_part, r_o, r_r)

    orf = jnp.concatenate([r_o, r_r, gfr], axis=1)
    orf = lax.psum_scatter(orf, dp_axes + (c,), scatter_dimension=0, tiled=True)
    r1 = Shrinking([by_dp(add_low(a_0, got_a.got))], only, dp_axes)
    r1.prepare(x)
    b_got = Plain(r2.value[..., 1, :, :], y)
    ga0, gb0 = earlier_state(span_decay, ga_part.sum(1), gb_part.sum(1), seq_axes, True)
    ga0, gb0 = fire([r1, b_got], ga0, gb0)
    d_keys, d_vals, first_part, decay_part = wkv_backward(
        keys, vals, num_before, den_before, p, rate, first, ga0, gb0, seqs
    )
    d_keys, d_vals, gfv, first_part, decay_part = settle(
        [r1, b_got], d_keys, d_vals, gfv, first_part, decay_part
    )
    z1, z2 = z_axes[-1], z_axes[:-1]
    rows_of = lambda g_: g_.reshape(lead + (quarter, D))
    r_kv = Shrinking(
        [
            rows_of(dot_weight(key_in, d_keys).astype(BF16)),
            rows_of(dot_weight(value_in, d_vals).astype(BF16)),
        ],
        stacked, every,
    )
    r_kv.prepare(c)
    r_f = Shrinking([r1.value, add_low(r2.value[..., 0, :, :], b_got.got)], stacked, r1.held)
    r_f.prepare(z1)
    gfv_got = Plain(gfv, y)
    small2, first_part, decay_part = fire([r_kv, r_f, gfv_got], small2, first_part, decay_part)
    small2 = jnp.concatenate(
        [
            -(lam * rate) * jnp.sum(decay_part, axis=(0, 1))[None], jnp.sum(first_part, axis=(0, 1))[None],
            small2, jnp.pad(stats, (0, D - 3))[None],
        ]
    )
    d_keys, small2 = settle([r_kv, gfv_got], d_keys, small2)

    r_kv.prepare(y)
    out_v = Growing(add_low(gfv, gfv_got.got))
    out_v.prepare(c)
    d_keys, d_middle = fire([r_kv, out_v], d_keys, d_middle)
    mix_outs = mix_back(
        d_keys, d_vals, d_recepts, w_k, w_v, w_r, flat_tokens, d_middle,
        gain1, bias1, mix_k, mix_v, mix_r, seqs,
    )
    input_grad, firsts, tail1, sums1 = settle([r_kv, r_f, out_v], *mix_outs)

    r_kv.prepare(x)
    for z in reversed(z2):
        r_f.prepare(z)
        if z != z2[0]:
            r_f.go()
            settle([r_f])
    (firsts,) = fire([r_kv, r_f], firsts)
    mixes = (mix_k, mix_v, mix_r)
    edge4 = from_behind(sum(firsts[:, i] * (1.0 - m) for i, m in enumerate(mixes)), seq_axes, -1)
    input_last = (tail1[:, 0] + norm_back(edge4 * gain1, tail1[:, 1], tail1[:, 2])).astype(BF16)
    input_grad = deep(put_rows(input_grad, input_last, span - 1))
    small1 = sums1.sum((0, 2)) + jnp.concatenate(
        [
            -jnp.sum(edge1[:, None] * firsts, axis=(0, 2)),
            jnp.sum(tail1[:, 1] * edge4, axis=0), jnp.sum(edge4, axis=0),
        ]
    )

    small = jnp.concatenate([small1, small2])
    small, input_grad = settle([r_kv], small, input_grad)
    small = Summing(small)
    r_kv.start(z1)
    small.start(c)
    small.finish()
    small.start(y)
    (orf,) = settle([r_kv, small, r_f], orf)
    for z in reversed(z2):
        r_kv.start(z)
        if z != z2[0]:
            settle([r_kv])
    out_f = Growing(r_f.value)
    out_f.start(y)
    orf_got = swap(orf, y)
    small.start(x)
    small.finish()
    small.start(z1)
    grad_fv = out_v.value.reshape(hid, D).astype(F32)
    orf_got, grad_fv = settle([r_kv, small, out_f], orf_got, grad_fv)
    out_f.start(c)
    orf = add_low(orf, orf_got)
    orf_c = swap(orf, c)
    own = r_kv.value
    last_z = list(reversed(z2))
    for z in last_z[:-1]:
        small.start(z)
        small.finish()
    small.start(last_z[-1])
    at_y, at_c = swap(own, y), swap(own, c)
    at_both = lax.ppermute(own, (y, c), [(i, 3 - i) for i in range(4)])
    at_y, at_c, at_both, orf_c = settle([small, out_f], at_y, at_c, at_both, orf_c)
    small = small.value
    out_kv = join(join(own, at_c, c, 0), join(at_y, at_both, c, 0), y, 0)

    wide_out = lambda v, i: v[:, :, i].reshape(shard, -1)
    out_f = out_f.value.reshape(2 * seq, shard, side)
    grad_fk = jnp.concatenate([out_f[i] for i in range(2 * seq)], axis=1).astype(F32)
    orf = join(orf, orf_c, c, 0).reshape(shard, 3 * D).astype(F32)
    grad_o, grad_r, grad_fr = [orf[:, i * D : i * D + D] for i in range(3)]
    grad_k, grad_v = [wide_out(out_kv, i).astype(F32) for i in range(2)]
    rows = lax.dynamic_slice_in_dim(small[:11], my_dp * shard, shard, 1)
    rms = jnp.sqrt(small[11, :3] / (jnp.sum(lengths).astype(F32) * D))
    v = [rows[i] for i in range(11)]
    return (
        block_out, input_grad,
        v[3], v[4], v[0], v[1], v[2], v[5], v[6],
        grad_k, grad_v, grad_r, grad_o,
        v[9], v[10], v[7], v[8],
        grad_fk, grad_fr, grad_fv,
        rms[0], rms[1], rms[2],
    )


def solution(mesh):
    dp_axes, seq_axes = axes_of("d", mesh.shape["dp"]), axes_of("s", mesh.shape["seq"])
    names = dp_axes + seq_axes
    fine = jax.sharding.Mesh(mesh.devices.reshape((2,) * len(names)), names)
    big, vec, mat = P(dp_axes, seq_axes, None), P(dp_axes), P(dp_axes, None)
    args = (big, big, P(), P()) + (vec,) * 7 + (mat,) * 4 + (vec,) * 4 + (mat,) * 3
    outs = (big, big) + (vec,) * 7 + (mat,) * 4 + (vec,) * 4 + (mat,) * 3 + (P(),) * 3
    return jax.shard_map(
        functools.partial(per_device, dp_axes, seq_axes),
        mesh=fine, in_specs=args, out_specs=outs, check_vma=False,
    )
```

```python
import functools

import jax
import jax.numpy as jnp
from jax import lax
from jax.experimental import pallas as pl
from jax.experimental.layout import Layout, with_layout_constraint
from jax.experimental.pallas import tpu as pltpu
from jax.sharding import PartitionSpec as P

D = 1024
EPS = 1e-05
F32 = jnp.float32
BF16 = jnp.bfloat16


LIGHT = pl.CostEstimate(flops=1 << 20, bytes_accessed=1 << 16, transcendentals=0)


def axes_of(letter, size):
    return tuple(f"{letter}{bit}" for bit in reversed(range(size.bit_length() - 1)))


def swap(value, key):
    return lax.ppermute(value, key, [(0, 1), (1, 0)])


def place(held, key):
    rank = lambda k: (k[0] == "s", -int(k[1:]))
    return sum(1 for other in held if rank(other) < rank(key))


def join(mine, other, key, at):
    shape = mine.shape[:at] + (2,) + mine.shape[at:]
    side = lax.broadcasted_iota(jnp.int32, shape, at)
    return jnp.where(side == lax.axis_index(key), jnp.expand_dims(mine, at), jnp.expand_dims(other, at))


def half(value, which, at):
    return lax.dynamic_index_in_dim(value, which, at, keepdims=False)


def add_low(mine, other):
    return (mine.astype(F32) + other.astype(F32)).astype(BF16)


def tie(*values):
    return lax.optimization_barrier(values)


def row_major(value):
    return with_layout_constraint(value, Layout(tuple(range(value.ndim))))


class Moving:
    def start(self, key):
        self.prepare(key)
        self.go()

    def go(self):
        self.got = swap(self.send, self.key)

    def finish(self):
        pass


class Plain(Moving):
    def __init__(self, value, key):
        self.send, self.key = value, key


class Growing(Moving):
    def __init__(self, value):
        self.value, self.held = value, []

    def prepare(self, key):
        self.key, self.send = key, self.value

    def finish(self):
        at = place(self.held, self.key)
        self.held.append(self.key)
        self.value = join(self.value, self.got, self.key, at)


class Shrinking(Moving):
    def __init__(self, parts, merge, held):
        self.parts, self.merge, self.held = parts, merge, list(held)

    def prepare(self, key):
        self.key = key
        self.held.remove(key)
        self.at = place(self.held, key)
        self.bit = lax.axis_index(key)
        self.send = self.merge([half(p, 1 - self.bit, self.at) for p in self.parts])

    def finish(self):
        self.value = add_low(self.merge([half(p, self.bit, self.at) for p in self.parts]), self.got)
        self.parts, self.merge = [self.value], only


class Summing(Moving):
    def __init__(self, value):
        self.value = value

    def prepare(self, key):
        self.key, self.send = key, self.value

    def finish(self):
        self.value = self.value + self.got


def fire(items, *others):
    tied = tie(*[item.send for item in items], *others)
    for item, send in zip(items, tied):
        item.send = send
        item.go()
    return tied[len(items) :]


def only(parts):
    (part,) = parts
    return part


def stacked(parts):
    return jnp.stack(parts, axis=-3)


def settle(items, *others):
    tied = tie(*[item.got for item in items], *others)
    for item, got in zip(items, tied):
        item.got = got
        item.finish()
    return tied[len(items) :]


ROWS = 8


def fwd_kernel(k_ref, v_ref, r_ref, rate_ref, u_ref, a0_ref, b0_ref, w_ref, a_ref, b_ref):
    rate = rate_ref[...]
    boost = jnp.exp(u_ref[...])
    width = rate.shape[1]
    row = lax.broadcasted_iota(jnp.int32, (ROWS, width), 0)
    rowf = row.astype(F32)
    falling = jnp.exp(-rowf * rate)
    one = jnp.exp(-rate)
    steps = [(s, jnp.where(row >= s, jnp.exp(-s * rate), 0.0)) for s in (1, 2, 4)]
    inner = row >= 1

    def scan(tile, carry):
        before = jnp.where(inner, pltpu.roll(tile, 1, 0), 0.0)
        for s, factor in steps:
            before = before + factor * pltpu.roll(before, s, 0)
        before = before + falling * carry
        after = one * before[ROWS - 1 :, :] + tile[ROWS - 1 :, :]
        return before, after

    def tile_of(key, val, recept, carry):
        num, den = carry
        power = jnp.exp(key)
        num_before, num = scan(power * val, num)
        den_before, den = scan(power, den)
        now = boost * power
        mixed = (num_before + now * val) / (den_before + now)
        return (jax.nn.sigmoid(recept) * mixed, num_before, den_before), (num, den)

    def body(i, carry):
        at = pl.ds(pl.multiple_of(i * (2 * ROWS), 2 * ROWS), 2 * ROWS)
        key, val, recept = k_ref[at, :], v_ref[at, :].astype(F32), r_ref[at, :].astype(F32)
        low, carry = tile_of(key[:ROWS], val[:ROWS], recept[:ROWS], carry)
        high, carry = tile_of(key[ROWS:], val[ROWS:], recept[ROWS:], carry)
        for ref, a, b in zip((w_ref, a_ref, b_ref), low, high):
            ref[at, :] = jnp.concatenate([a, b], axis=0).astype(ref.dtype)
        return carry

    lax.fori_loop(
        0, k_ref.shape[0] // (2 * ROWS), body, (a0_ref[...], b0_ref[...]), unroll=2
    )


def bwd_kernel(
    k_ref, v_ref, a_ref, b_ref, p_ref, rate_ref, u_ref, ga_ref, gb_ref,
    dk_ref, dv_ref, first_ref, decay_ref,
):
    rate = rate_ref[...]
    boost = jnp.exp(u_ref[...])
    width = rate.shape[1]
    row = lax.broadcasted_iota(jnp.int32, (ROWS, width), 0)
    rowf = row.astype(F32)
    trailing = jnp.exp(-(ROWS - 1.0 - rowf) * rate)
    one = jnp.exp(-rate)
    steps = [(s, jnp.where(row < ROWS - s, jnp.exp(-s * rate), 0.0)) for s in (1, 2, 4)]
    inner = row < ROWS - 1

    def scan(tile, carry):
        later = jnp.where(inner, pltpu.roll(tile, ROWS - 1, 0), 0.0)
        for s, factor in steps:
            later = later + factor * pltpu.roll(later, ROWS - s, 0)
        later = later + trailing * carry
        before = one * later[:1, :] + tile[:1, :]
        return later, before

    def tile_of(tiles, carry):
        num, den, first, decay = carry
        key, val, num_before, den_before, p = tiles
        power = jnp.exp(key)
        now = boost * power
        q = -p * (num_before + now * val) / (den_before + now)
        num_later, num = scan(p, num)
        den_later, den = scan(q, den)
        diagonal = now * (val * p + q)
        d_key = power * (val * num_later + den_later) + diagonal
        d_val = power * num_later + now * p
        first = first + diagonal
        decay = decay + (num_later * num_before + den_later * den_before)
        return (d_key, d_val), (num, den, first, decay)

    count = k_ref.shape[0] // (2 * ROWS)

    def body(i, carry):
        at = pl.ds(pl.multiple_of((count - 1 - i) * (2 * ROWS), 2 * ROWS), 2 * ROWS)
        tiles = [ref[at, :].astype(F32) for ref in (k_ref, v_ref, a_ref, b_ref, p_ref)]
        high, carry = tile_of([tile[ROWS:] for tile in tiles], carry)
        low, carry = tile_of([tile[:ROWS] for tile in tiles], carry)
        for ref, a, b in zip((dk_ref, dv_ref), low, high):
            ref[at, :] = jnp.concatenate([a, b], axis=0).astype(BF16)
        return carry

    zero = jnp.zeros((ROWS, width), F32)
    done = lax.fori_loop(0, count, body, (ga_ref[...], gb_ref[...], zero, zero), unroll=2)
    first_ref[...] = done[2]
    decay_ref[...] = done[3]


def share_kernel(
    da_ref, w_ref, k_ref, v_ref, r_ref, a_ref, b_ref, rate_ref, u_ref,
    p_ref, dr_ref, ga_ref, gb_ref, dw_ref,
):
    dw_ref[...] = lax.dot_general(
        da_ref[...], w_ref[...], (((1,), (1,)), ((), ())), preferred_element_type=F32
    )
    rate = rate_ref[...]
    boost = jnp.exp(u_ref[...])
    rows = 2 * ROWS
    rowf = lax.broadcasted_iota(jnp.int32, (rows, rate.shape[1]), 0).astype(F32)
    near = jnp.exp(-rowf * rate)

    def body(i, carry):
        ga, gb = carry
        at = pl.ds(pl.multiple_of(i * rows, rows), rows)
        now = boost * jnp.exp(k_ref[at, :])
        inverse = 1.0 / (b_ref[at, :].astype(F32) + now)
        mixed = (a_ref[at, :].astype(F32) + now * v_ref[at, :].astype(F32)) * inverse
        gate = jax.nn.sigmoid(r_ref[at, :].astype(F32))
        d_mixed = dw_ref[at, :] * gate
        dr_ref[at, :] = (d_mixed * mixed * (1.0 - gate)).astype(BF16)
        p_low = (d_mixed * inverse).astype(BF16)
        p_ref[at, :] = p_low
        p = p_low.astype(F32)
        q = -p * mixed
        fall = near * jnp.exp(-(i * rows).astype(F32) * rate)
        return ga + fall * p, gb + fall * q

    zero = jnp.zeros((rows, rate.shape[1]), F32)
    ga, gb = lax.fori_loop(0, k_ref.shape[0] // rows, body, (zero, zero), unroll=2)
    ga_ref[...] = ga[:ROWS] + ga[ROWS:]
    gb_ref[...] = gb[:ROWS] + gb[ROWS:]


WIDTH = 512


def wkv_specs(rows):
    big = pl.BlockSpec((rows, WIDTH), lambda s, c: (s, c))
    row = pl.BlockSpec((1, WIDTH), lambda s, c: (0, c))
    state = pl.BlockSpec((None, 1, WIDTH), lambda s, c: (s, 0, c))
    partial = pl.BlockSpec((None, ROWS, WIDTH), lambda s, c: (s, 0, c))
    return big, row, state, partial


def wkv_forward(keys, vals, recepts, rate, first, num, den, seqs):
    total = keys.shape[0]
    big, row, state, _ = wkv_specs(total // seqs)
    cells = total * D
    return pl.pallas_call(
        fwd_kernel,
        grid=(seqs, D // WIDTH),
        in_specs=[big, big, big, row, row, state, state],
        out_specs=[big, big, big],
        out_shape=[
            jax.ShapeDtypeStruct((total, D), BF16),
            jax.ShapeDtypeStruct((total, D), F32),
            jax.ShapeDtypeStruct((total, D), F32),
        ],
        compiler_params=pltpu.CompilerParams(vmem_limit_bytes=58 << 20),
        cost_estimate=LIGHT,
    )(keys, vals, recepts, rate, first, num, den)


def wkv_backward(keys, vals, num_before, den_before, p, rate, first, num, den, seqs):
    total = keys.shape[0]
    big, row, state, partial = wkv_specs(total // seqs)
    cells = total * D
    return pl.pallas_call(
        bwd_kernel,
        grid=(seqs, D // WIDTH),
        in_specs=[big, big, big, big, big, row, row, state, state],
        out_specs=[big, big, partial, partial],
        out_shape=[
            jax.ShapeDtypeStruct((total, D), BF16),
            jax.ShapeDtypeStruct((total, D), BF16),
            jax.ShapeDtypeStruct((seqs, ROWS, D), F32),
            jax.ShapeDtypeStruct((seqs, ROWS, D), F32),
        ],
        compiler_params=pltpu.CompilerParams(vmem_limit_bytes=58 << 20),
        cost_estimate=LIGHT,
    )(keys, vals, num_before, den_before, p, rate, first, num, den)


def share_back(d_attn, weight, keys, vals, recepts, num_before, den_before, rate, first, seqs):
    total = keys.shape[0]
    span = total // seqs
    big, row, _, partial = wkv_specs(span)
    cells = total * D
    return pl.pallas_call(
        share_kernel,
        grid=(seqs, D // WIDTH),
        in_specs=[
            pl.BlockSpec((span, D), lambda s, c: (s, 0)),
            pl.BlockSpec((WIDTH, D), lambda s, c: (c, 0)),
            big, big, big, big, big, row, row,
        ],
        out_specs=[big, big, partial, partial],
        out_shape=[
            jax.ShapeDtypeStruct((total, D), BF16),
            jax.ShapeDtypeStruct((total, D), BF16),
            jax.ShapeDtypeStruct((seqs, ROWS, D), F32),
            jax.ShapeDtypeStruct((seqs, ROWS, D), F32),
        ],
        scratch_shapes=[pltpu.VMEM((span, WIDTH), F32)],
        compiler_params=pltpu.CompilerParams(vmem_limit_bytes=58 << 20),
        cost_estimate=LIGHT,
    )(d_attn, weight, keys, vals, recepts, num_before, den_before, rate, first)


PIECES = 8


def load_pieces(refs, held, sems):
    left, right = refs[:4], refs[4:]
    per = 4 // held.shape[0]
    whole = held.shape[2] // per
    copies = []
    for p in range(4):
        at = (p % per) * whole
        for ref in (left[p], right[p % 2].at[p // 2]):
            width = ref.shape[-1]
            copies.append(
                pltpu.make_async_copy(ref, held.at[p // per, :, pl.ds(at, width)], sems.at[len(copies)])
            )
            at += width
    return copies


def feed_kernel(s_ref, left_ref, x_ref, *rest):
    refs = rest[:6]
    fv_ref, xr_ref, fr_ref, mid_ref, cot_ref = rest[6:11]
    sq_ref, out_ref, dval_ref, dgate_ref, sums = rest[11:16]
    held, held_v, acc, gate_acc, sems, sems_v = rest[16:]
    copies = load_pieces(refs, held, sems)
    deep = held_v.shape[1]
    copies_v = [
        pltpu.make_async_copy(fv_ref.at[pl.ds(h * deep, deep)], held_v.at[h], sems_v.at[h])
        for h in range(2)
    ]
    first = pl.program_id(0) == 0
    width = held.shape[2]

    @pl.when(first)
    def _():
        for copy in copies + copies_v:
            copy.start()

    for p in range(4):

        @pl.when(first)
        def _(p=p):
            copies[2 * p].wait()
            copies[2 * p + 1].wait()

        hidden = jnp.maximum(jnp.dot(x_ref[...], held[p], preferred_element_type=F32), 0.0)
        at = pl.multiple_of(jnp.bitwise_xor(s_ref[0], p) * width, width)
        sq_ref[:, pl.ds(at, width)] = (hidden * hidden).astype(BF16)

    gate_acc[...] = jnp.dot(xr_ref[...], fr_ref[...], preferred_element_type=F32)
    total = None
    for h in range(2):

        @pl.when(first)
        def _(h=h):
            copies_v[h].wait()

        part = jnp.dot(sq_ref[:, pl.ds(h * deep, deep)], held_v[h], preferred_element_type=F32)
        total = part if total is None else total + part
    acc[...] = total

    left = left_ref[pl.program_id(0)]
    sums[...] = jnp.zeros_like(sums)

    def body(i, _):
        start = pl.multiple_of(i * 2 * ROWS, 2 * ROWS)
        at = pl.ds(start, 2 * ROWS)
        rows = start + lax.broadcasted_iota(jnp.int32, (2 * ROWS, 1), 0)
        keep = rows < left
        gate = jax.nn.sigmoid(gate_acc[at, :])
        feed = jnp.where(keep, gate * acc[at, :], 0.0)
        result = jnp.where(keep, mid_ref[at, :], 0.0) + feed
        g = jnp.where(keep, cot_ref[at, :].astype(F32), 0.0)
        out_ref[at, :] = result.astype(BF16)
        dval_ref[at, :] = (g * gate).astype(BF16)
        dgate_ref[at, :] = (g * feed * (1.0 - gate)).astype(BF16)
        sums[0] += fold(result * result)
        sums[1] += fold(feed * feed)
        return 0

    lax.fori_loop(0, mid_ref.shape[0] // (2 * ROWS), body, 0, unroll=2)


def feed_forward(my_seq, left, inputs, pieces, weight, gate_inputs, gate_weight, middle, cotangent, seqs):
    total = inputs.shape[0]
    width = pieces[0].shape[1] + pieces[4].shape[2]
    span = total // seqs
    ff = 4 * width
    big = pl.BlockSpec((span, D), lambda i, *_: (i, 0))
    return pl.pallas_call(
        feed_kernel,
        grid_spec=pltpu.PrefetchScalarGridSpec(
            num_scalar_prefetch=2,
            grid=(seqs,),
            in_specs=[big]
            + [pl.BlockSpec(memory_space=pl.ANY)] * 7
            + [big, pl.BlockSpec((D, D), lambda i, *_: (0, 0), pipeline_mode=pl.Buffered(1)), big, big],
            out_specs=[
                pl.BlockSpec((span, ff), lambda i, *_: (i, 0)), big, big, big,
                pl.BlockSpec((None, 2, ROWS, D), lambda i, *_: (i, 0, 0, 0)),
            ],
            scratch_shapes=[
                pltpu.VMEM((4, D, width), BF16),
                pltpu.VMEM((2, 2 * width, D), BF16),
                pltpu.VMEM((span, D), F32),
                pltpu.VMEM((span, D), F32),
                pltpu.SemaphoreType.DMA((PIECES,)),
                pltpu.SemaphoreType.DMA((2,)),
            ],
        ),
        out_shape=[
            jax.ShapeDtypeStruct((total, ff), BF16),
            jax.ShapeDtypeStruct((total, D), BF16),
            jax.ShapeDtypeStruct((total, D), BF16),
            jax.ShapeDtypeStruct((total, D), BF16),
            jax.ShapeDtypeStruct((seqs, 2, ROWS, D), F32),
        ],
        compiler_params=pltpu.CompilerParams(vmem_limit_bytes=60 << 20),
        cost_estimate=LIGHT,
    )(my_seq[None], left, inputs, *pieces, weight, gate_inputs, gate_weight, middle, cotangent)


CHUNK = 128


def stats_of(values):
    centre = values - jnp.mean(values, axis=-1, keepdims=True)
    inverse = lax.rsqrt(jnp.mean(centre * centre, axis=-1, keepdims=True) + EPS)
    return centre * inverse, inverse


def norm_back(grads, normed, inverse):
    return inverse * (
        grads
        - jnp.mean(grads, axis=-1, keepdims=True)
        - normed * jnp.mean(grads * normed, axis=-1, keepdims=True)
    )


def fold(values):
    return jnp.sum(values.reshape(values.shape[0] // ROWS, ROWS, values.shape[1]), axis=0)


def next_rows(values, carry):
    last = lax.broadcasted_iota(jnp.int32, values.shape, 0) == CHUNK - 1
    return jnp.where(last, carry, pltpu.roll(values, CHUNK - 1, 0))


def previous_rows(values, carry):
    first = lax.broadcasted_iota(jnp.int32, values.shape, 0) == 0
    return jnp.where(first, carry, pltpu.roll(values, 1, 0))


def mid_kernel(
    left_ref, w_ref, weight_ref, x_ref, gain_ref, bias_ref, mk_ref, mr_ref,
    mid_ref, fk_ref, fr_ref, first_ref, sq_ref,
):
    mid_ref[...] = jnp.dot(w_ref[...], weight_ref[...], preferred_element_type=F32)
    left = left_ref[pl.program_id(0)]
    gain, bias, mix_k, mix_r = gain_ref[...], bias_ref[...], mk_ref[...], mr_ref[...]
    sq_ref[...] = jnp.zeros_like(sq_ref)

    def body(i, carry):
        start = pl.multiple_of(i * CHUNK, CHUNK)
        at = pl.ds(start, CHUNK)
        attn = mid_ref[at, :]
        rows = start + lax.broadcasted_iota(jnp.int32, (CHUNK, 1), 0)
        sq_ref[...] += fold(jnp.where(rows < left, attn * attn, 0.0))
        middle = x_ref[at, :].astype(F32) + attn
        mid_ref[at, :] = middle
        b = stats_of(middle)[0] * gain + bias
        before = previous_rows(b, carry)
        fk_ref[at, :] = (b * mix_k + before * (1.0 - mix_k)).astype(BF16)
        fr_ref[at, :] = (b * mix_r + before * (1.0 - mix_r)).astype(BF16)

        @pl.when(i == 0)
        def _():
            first_ref[...] = b[:1, :]

        return b[CHUNK - 1 :, :]

    lax.fori_loop(0, x_ref.shape[0] // CHUNK, body, jnp.zeros_like(gain), unroll=2)


def mid_forward(left, weighted, weight, tokens, gain, bias, mix_k, mix_r, seqs):
    total = tokens.shape[0]
    span = total // seqs
    big = pl.BlockSpec((span, D), lambda s, _: (s, 0))
    row = pl.BlockSpec((1, D), lambda s, _: (0, 0))
    tile = lambda rows: pl.BlockSpec((None, rows, D), lambda s, _: (s, 0, 0))
    return pl.pallas_call(
        mid_kernel,
        grid_spec=pltpu.PrefetchScalarGridSpec(
            num_scalar_prefetch=1,
            grid=(seqs,),
            in_specs=[big, pl.BlockSpec((D, D), lambda s, _: (0, 0)), big, row, row, row, row],
            out_specs=[big, big, big, tile(1), tile(ROWS)],
        ),
        out_shape=[
            jax.ShapeDtypeStruct((total, D), F32),
            jax.ShapeDtypeStruct((total, D), BF16),
            jax.ShapeDtypeStruct((total, D), BF16),
            jax.ShapeDtypeStruct((seqs, 1, D), F32),
            jax.ShapeDtypeStruct((seqs, ROWS, D), F32),
        ],
        compiler_params=pltpu.CompilerParams(vmem_limit_bytes=58 << 20),
        cost_estimate=LIGHT,
    )(left, weighted, weight, tokens, gain, bias, mix_k, mix_r)


def down_kernel(s_ref, left_ref, dval_ref, fv_ref, sq_ref, *rest):
    refs = rest[:6]
    gate_ref, fr_ref, mid_ref, cot_ref, gain_ref, bias_ref, mk_ref, mr_ref = rest[6:14]
    dh_ref, out_ref, low_ref, first_k, first_r, tail_ref, sums = rest[14:21]
    held, held_v, held_sq, acc_k, acc_r, sems, sems_v, sems_sq = rest[21:]
    copies = load_pieces(refs, held, sems)
    width = held_v.shape[1]
    places = [pl.multiple_of(jnp.bitwise_xor(s_ref[0], p) * width, width) for p in range(4)]
    copies_v = [
        pltpu.make_async_copy(fv_ref.at[pl.ds(places[p], width)], held_v.at[p], sems_v.at[p])
        for p in range(4)
    ]
    span = held_sq.shape[1]
    rows = pl.ds(pl.multiple_of(pl.program_id(0) * span, span), span)
    copies_sq = [
        pltpu.make_async_copy(sq_ref.at[rows, pl.ds(places[p], width)], held_sq.at[p], sems_sq.at[p])
        for p in range(4)
    ]
    first = pl.program_id(0) == 0
    back = (((1,), (1,)), ((), ()))
    for copy in copies_sq[:1]:
        copy.start()

    @pl.when(first)
    def _():
        copies_v[0].start()

    for copy in copies_sq[1:]:
        copy.start()

    @pl.when(first)
    def _():
        for copy in copies_v[1:] + copies:
            copy.start()

    for p in range(4):
        copies_sq[p].wait()

        @pl.when(first)
        def _(p=p):
            copies_v[p].wait()

        for side in range(2):
            part = pl.ds(side * (width // 2), width // 2)
            d_sq = lax.dot_general(dval_ref[...], held_v[p, part, :], back, preferred_element_type=F32)
            squared = held_sq[p, :, part].astype(F32)
            twice = 2.0 * squared * lax.rsqrt(jnp.maximum(squared, 1e-37))
            dh_ref[p, :, part] = (twice * d_sq).astype(BF16)

    acc_r[...] = lax.dot_general(gate_ref[...], fr_ref[...], back, preferred_element_type=F32)
    for h in range(2):

        @pl.when(first)
        def _(h=h):
            for copy in copies[4 * h : 4 * h + 4]:
                copy.wait()

        part = lax.dot_general(
            jnp.concatenate([dh_ref[2 * h], dh_ref[2 * h + 1]], axis=1), held[h],
            back, preferred_element_type=F32,
        )
        acc_k[...] = part if h == 0 else acc_k[...] + part

    left = left_ref[pl.program_id(0)]
    gain, bias, mix_k, mix_r = gain_ref[...], bias_ref[...], mk_ref[...], mr_ref[...]
    sums[...] = jnp.zeros_like(sums)
    count = mid_ref.shape[0] // CHUNK

    def body(i, carry):
        later_k, later_r = carry
        start = pl.multiple_of((count - 1 - i) * CHUNK, CHUNK)
        at = pl.ds(start, CHUNK)
        d_fk, d_fr = acc_k[at, :], acc_r[at, :]
        next_k, next_r = next_rows(d_fk, later_k), next_rows(d_fr, later_r)
        n, inverse = stats_of(mid_ref[at, :])
        b = n * gain + bias
        db = d_fk * mix_k + next_k * (1.0 - mix_k) + d_fr * mix_r + next_r * (1.0 - mix_r)
        sums[0] += fold(b * (d_fk - next_k))
        sums[1] += fold(b * (d_fr - next_r))
        sums[2] += fold(n * db)
        sums[3] += fold(db)
        rows = start + lax.broadcasted_iota(jnp.int32, (CHUNK, 1), 0)
        g = jnp.where(rows < left, cot_ref[at, :].astype(F32), 0.0)
        d_middle = g + norm_back(db * gain, n, inverse)
        out_ref[at, :] = d_middle
        low_ref[at, :] = d_middle.astype(BF16)

        @pl.when(i == 0)
        def _():
            tail_ref[0] = d_middle[CHUNK - 1 :, :]
            tail_ref[1] = n[CHUNK - 1 :, :]
            tail_ref[2] = jnp.broadcast_to(inverse[CHUNK - 1 :, :], gain.shape)

        return d_fk[:1, :], d_fr[:1, :]

    zero = jnp.zeros_like(gain)
    first_k[...], first_r[...] = lax.fori_loop(0, count, body, (zero, zero), unroll=2)


def down(
    my_seq, left, grads, weight, squared, pieces, gate_grads, gate_weight,
    middle, cotangent, gain, bias, mix_k, mix_r, seqs,
):
    total, ff = squared.shape
    span = total // seqs
    width = ff // 4
    big = pl.BlockSpec((span, D), lambda s, *_: (s, 0))
    alone = pl.BlockSpec((span, D), lambda s, *_: (s, 0), pipeline_mode=pl.Buffered(1))
    row = pl.BlockSpec((1, D), lambda s, *_: (0, 0))
    one = pl.BlockSpec((None, 1, D), lambda s, *_: (s, 0, 0))
    return pl.pallas_call(
        down_kernel,
        grid_spec=pltpu.PrefetchScalarGridSpec(
            num_scalar_prefetch=2,
            grid=(seqs,),
            in_specs=[
                big,
                pl.BlockSpec(memory_space=pl.ANY),
                pl.BlockSpec(memory_space=pl.ANY),
            ]
            + [pl.BlockSpec(memory_space=pl.ANY)] * 6
            + [big, pl.BlockSpec((D, D), lambda s, *_: (0, 0), pipeline_mode=pl.Buffered(1)), alone, big]
            + [row] * 4,
            out_specs=[
                pl.BlockSpec((4, span, width), lambda s, *_: (0, s, 0)),
                big, big, one, one,
                pl.BlockSpec((None, 3, 1, D), lambda s, *_: (s, 0, 0, 0)),
                pl.BlockSpec((None, 4, ROWS, D), lambda s, *_: (s, 0, 0, 0)),
            ],
            scratch_shapes=[
                pltpu.VMEM((2, D, 2 * width), BF16),
                pltpu.VMEM((4, width, D), BF16),
                pltpu.VMEM((4, span, width), BF16),
                pltpu.VMEM((span, D), F32),
                pltpu.VMEM((span, D), F32),
                pltpu.SemaphoreType.DMA((PIECES,)),
                pltpu.SemaphoreType.DMA((4,)),
                pltpu.SemaphoreType.DMA((4,)),
            ],
        ),
        out_shape=[
            jax.ShapeDtypeStruct((4, total, width), BF16),
            jax.ShapeDtypeStruct((total, D), F32),
            jax.ShapeDtypeStruct((total, D), BF16),
            jax.ShapeDtypeStruct((seqs, 1, D), F32),
            jax.ShapeDtypeStruct((seqs, 1, D), F32),
            jax.ShapeDtypeStruct((seqs, 3, 1, D), F32),
            jax.ShapeDtypeStruct((seqs, 4, ROWS, D), F32),
        ],
        compiler_params=pltpu.CompilerParams(vmem_limit_bytes=60 << 20),
        cost_estimate=LIGHT,
    )(
        my_seq[None], left, grads, weight, squared, *pieces, gate_grads, gate_weight,
        middle, cotangent, gain, bias, mix_k, mix_r,
    )


def mix_kernel(
    dk_ref, dv_ref, dr_ref, wk_ref, wv_ref, wr_ref, x_ref, dm_ref,
    gain_ref, bias_ref, mk_ref, mv_ref, mr_ref,
    out_ref, firsts, tail_ref, sums, acc, held, sems,
):
    first = pl.program_id(0) == 0
    copies = [
        pltpu.make_async_copy(ref, held.at[i], sems.at[i]) for i, ref in enumerate((wk_ref, wv_ref, wr_ref))
    ]

    @pl.when(first)
    def _():
        for copy in copies:
            copy.start()

    for i, grads in enumerate((dk_ref, dv_ref, dr_ref)):

        @pl.when(first)
        def _(i=i):
            copies[i].wait()

        acc[i] = lax.dot_general(
            grads[...], held[i], (((1,), (1,)), ((), ())), preferred_element_type=F32
        )
    gain, bias = gain_ref[...], bias_ref[...]
    mixes = (mk_ref[...], mv_ref[...], mr_ref[...])
    sums[...] = jnp.zeros_like(sums)
    count = x_ref.shape[0] // CHUNK

    def body(i, carry):
        start = pl.multiple_of((count - 1 - i) * CHUNK, CHUNK)
        at = pl.ds(start, CHUNK)
        n, inverse = stats_of(x_ref[at, :].astype(F32))
        a = n * gain + bias
        da, heads = None, []
        for j in range(3):
            d = acc[j, at, :]
            later = next_rows(d, carry[j])
            sums[j] += fold(a * (d - later))
            part = d * mixes[j] + later * (1.0 - mixes[j])
            da = part if da is None else da + part
            heads.append(d[:1, :])
        sums[3] += fold(n * da)
        sums[4] += fold(da)
        total = dm_ref[at, :] + norm_back(da * gain, n, inverse)
        out_ref[at, :] = total.astype(BF16)

        @pl.when(i == 0)
        def _():
            tail_ref[0] = total[CHUNK - 1 :, :]
            tail_ref[1] = n[CHUNK - 1 :, :]
            tail_ref[2] = jnp.broadcast_to(inverse[CHUNK - 1 :, :], gain.shape)

        return tuple(heads)

    zero = jnp.zeros_like(gain)
    heads = lax.fori_loop(0, count, body, (zero, zero, zero), unroll=2)
    for j in range(3):
        firsts[j] = heads[j]


def mix_back(d_keys, d_vals, d_recepts, w_k, w_v, w_r, tokens, d_middle, gain, bias, mix_k, mix_v, mix_r, seqs):
    total = tokens.shape[0]
    span = total // seqs
    big = pl.BlockSpec((span, D), lambda s: (s, 0))
    row = pl.BlockSpec((1, D), lambda s: (0, 0))
    full = pl.BlockSpec(memory_space=pl.ANY)
    return pl.pallas_call(
        mix_kernel,
        grid=(seqs,),
        in_specs=[big, big, big, full, full, full, big, big] + [row] * 5,
        out_specs=[
            big,
            pl.BlockSpec((None, 3, 1, D), lambda s: (s, 0, 0, 0)),
            pl.BlockSpec((None, 3, 1, D), lambda s: (s, 0, 0, 0)),
            pl.BlockSpec((None, 5, ROWS, D), lambda s: (s, 0, 0, 0)),
        ],
        out_shape=[
            jax.ShapeDtypeStruct((total, D), BF16),
            jax.ShapeDtypeStruct((seqs, 3, 1, D), F32),
            jax.ShapeDtypeStruct((seqs, 3, 1, D), F32),
            jax.ShapeDtypeStruct((seqs, 5, ROWS, D), F32),
        ],
        scratch_shapes=[
            pltpu.VMEM((3, span, D), F32),
            pltpu.VMEM((3, D, D), BF16),
            pltpu.SemaphoreType.DMA((3,)),
        ],
        compiler_params=pltpu.CompilerParams(vmem_limit_bytes=58 << 20),
        cost_estimate=LIGHT,
    )(d_keys, d_vals, d_recepts, w_k, w_v, w_r, tokens, d_middle, gain, bias, mix_k, mix_v, mix_r)


def put_rows(values, rows, at):
    seqs = rows.shape[0]
    whole = values.reshape(seqs, values.shape[0] // seqs, D)
    return lax.dynamic_update_slice(whole, rows.astype(values.dtype), (0, at, 0)).reshape(values.shape)


def cut_kernel(_, k, v, r, o, fk, rows, kv_out, ro_out, f1_out, f2_out, row_out):
    kv_out[0], kv_out[1] = k[...], v[...]
    ro_out[0], ro_out[1] = r[...], o[...]
    left = f1_out.shape[1]
    f1_out[...], f2_out[...] = fk[:, :left], fk[:, left:]
    last = rows.shape[1] - 1
    row_out[...] = rows[...].astype(F32)[:, last:, :]


def cut(my_seq, quarter, key, value, recept, output, feed_key, tokens):
    seqs, span, _ = tokens.shape
    shard, ff = feed_key.shape
    part = pl.BlockSpec((quarter, D), lambda i, at: (at[0], 0))
    side = pl.BlockSpec((shard, ff // 4), lambda i, at: (0, at[0]))
    left = ff // 32 * 5
    full = lambda *shape: pl.BlockSpec(shape, lambda i, at: (0,) * len(shape))
    shapes = [(2, quarter, D), (2, quarter, D)] + [(shard, left), (shard, ff // 4 - left), (seqs, 1, D)]
    kinds = [BF16] * 4 + [F32]
    return pl.pallas_call(
        cut_kernel,
        grid_spec=pltpu.PrefetchScalarGridSpec(
            num_scalar_prefetch=1,
            grid=(1,),
            in_specs=[part] * 4
            + [side, pl.BlockSpec((seqs, 2 * ROWS, D), lambda i, at: (0, span // (2 * ROWS) - 1, 0))],
            out_specs=[full(*shape) for shape in shapes],
        ),
        out_shape=[jax.ShapeDtypeStruct(shape, kind) for shape, kind in zip(shapes, kinds)],
    )(my_seq[None], key, value, recept, output, feed_key, tokens)


def dot(left, right):
    return jnp.dot(left, right, preferred_element_type=F32)


def dot_back(grads, weight):
    return lax.dot_general(grads, weight, (((1,), (1,)), ((), ())), preferred_element_type=F32)


def dot_weight(inputs, grads):
    return lax.dot_general(inputs, grads, (((0,), (0,)), ((), ())), preferred_element_type=F32)


def normalize(values):
    centre = values - jnp.mean(values, axis=-1, keepdims=True)
    spread = jnp.mean(centre * centre, axis=-1, keepdims=True)
    inverse = lax.rsqrt(spread + EPS)
    return centre * inverse, inverse


def from_behind(value, axes, by):
    count = lax.axis_size(axes)
    pairs = [(i, i + by) for i in range(count) if 0 <= i + by < count]
    return lax.ppermute(value, axes, pairs)


def shifted(rows, edge):
    return jnp.concatenate([edge, rows[:, :-1]], axis=1)


def pulled(rows, edge):
    return jnp.concatenate([rows[:, 1:], edge], axis=1)


def blend(now, before, share):
    return (now * share + before * (1.0 - share)).astype(BF16)


def earlier_state(decay, num, den, axes, backward):
    count = lax.axis_size(axes)
    mine = lax.axis_index(axes)
    packed = lax.all_gather(jnp.concatenate([num, den], axis=0), axes)
    seqs = num.shape[0]
    state = jnp.zeros_like(packed[0])
    for hop in range(count - 1):
        source = count - 1 - hop if backward else hop
        longer = decay * state + packed[source]
        keep = source > mine if backward else source < mine
        state = jnp.where(keep, longer, state)
    return state[:seqs, None, :], state[seqs:, None, :]


def per_device(
    dp_axes, seq_axes,
    tokens, cotangent, lengths, assignment,
    mix_norm_gain, mix_norm_bias, shift_key, shift_value, shift_recept, time_decay, time_first,
    key_weight, value_weight, recept_weight, output_weight,
    feed_norm_gain, feed_norm_bias, feed_shift_key, feed_shift_recept,
    feed_key_weight, feed_recept_weight, feed_value_weight,
):
    seqs, span, _ = tokens.shape
    total = seqs * span
    dp, seq = lax.axis_size(dp_axes), lax.axis_size(seq_axes)
    my_dp, my_seq = lax.axis_index(dp_axes), lax.axis_index(seq_axes)
    every = dp_axes + seq_axes
    z_axes, x = dp_axes[:-1], dp_axes[-1]
    y, c = seq_axes
    ff = feed_key_weight.shape[1]
    flat = lambda v: v.reshape(total, v.shape[-1])
    deep = lambda v: v.reshape(seqs, span, v.shape[-1])

    shard = D // dp
    quarter = shard // seq

    def own_rows(weight):
        return lax.dynamic_slice_in_dim(weight, my_seq * quarter, quarter, 0)

    hid = feed_value_weight.shape[0]
    halves = lambda w: half(w.reshape(2, w.shape[0] // 2, D), lax.axis_index(c), 0)
    gathered = lambda w: lax.all_gather(w, dp_axes + (c,), axis=0, tiled=True)
    w_fr = gathered(halves(feed_recept_weight))
    *cuts, last_token = cut(
        my_seq, quarter, key_weight, value_weight, recept_weight, output_weight, feed_key_weight, tokens
    )
    kv, ro, f1, f2 = [Growing(part) for part in cuts]
    kv.start(z_axes[0])
    ro.start(z_axes[0])
    kv.value, tokens, *vectors = tie(
        kv.value, tokens,
        mix_norm_gain, mix_norm_bias, shift_key, shift_value, shift_recept, time_decay, time_first,
        feed_norm_gain, feed_norm_bias, feed_shift_key, feed_shift_recept,
    )
    vectors = Growing(jnp.stack(vectors))
    vectors.start(z_axes[0])
    edge1 = from_behind(last_token, seq_axes, 1)
    for z in z_axes[1:]:
        (edge1,) = settle([kv, ro, vectors], edge1)
        kv.start(z)
        ro.start(z)
        vectors.start(z)
    f1.value, f2.value = settle([kv, ro, vectors], f1.value, f2.value)
    kv.start(x)
    ro.start(y)
    vectors.start(x)
    f1.start(z_axes[0])
    f2.start(z_axes[0])
    settle([kv, ro, vectors, f1, f2])
    kv.start(y)
    ro.start(x)
    for z in z_axes[1:]:
        f1.start(z)
        f2.start(z)
        if z != z_axes[-1]:
            settle([f1, f2])
    fv_part, w_fr = settle([f1, f2, kv, ro], halves(feed_value_weight), w_fr)
    w_fv = gathered(fv_part)
    kv.prepare(c)
    ro.prepare(c)
    f1.prepare(x)
    f2y = Plain(f2.value, y)
    tokens, vectors.value = fire([kv, ro, f1, f2y], tokens, vectors.value)
    settle([kv, ro])
    pick = lambda v, i: jnp.moveaxis(v, -3, 0)[i].reshape(D, D)
    w_k, w_v, w_r, w_o = pick(kv.value, 0), pick(kv.value, 1), pick(ro.value, 0), pick(ro.value, 1)
    vectors = jnp.swapaxes(vectors.value.reshape(dp, 11, D // dp), 0, 1).reshape(11, D).astype(F32)
    gain1, bias1, mix_k, mix_v, mix_r, log_rate, first, gain2, bias2, fmix_k, fmix_r = [
        vectors[i : i + 1] for i in range(11)
    ]
    rate = jnp.exp(log_rate)
    lam = jnp.exp(-rate)

    slot_ids = jnp.arange(assignment.shape[0])
    my_slots = my_dp * seqs + jnp.arange(seqs)
    seq_ids = jnp.sum(jnp.where(slot_ids[None, :] == my_slots[:, None], assignment[None, :], 0), axis=1)
    my_lens = jnp.sum(jnp.where(slot_ids[None, :] == seq_ids[:, None], lengths[None, :], 0), axis=1)
    positions = my_seq * span + jnp.arange(span)
    valid = flat((positions[None, :] < my_lens[:, None]).astype(F32)[..., None])
    inside = (my_seq > 0).astype(F32)

    xin = tokens.astype(F32)
    edge1 = (normalize(edge1)[0] * gain1 + bias1) * inside
    n1, inv1 = normalize(xin)
    a = n1 * gain1 + bias1
    a_prev = shifted(a, edge1)
    key_in = flat(blend(a, a_prev, mix_k))
    value_in = flat(blend(a, a_prev, mix_v))
    recept_in = flat(blend(a, a_prev, mix_r))
    keys = dot(key_in, w_k)
    vals = dot(value_in, w_v)
    recepts = dot(recept_in, w_r)

    offsets = jnp.arange(span).astype(F32)[:, None]
    power = deep(jnp.exp(keys))
    left = jnp.exp(-(span - 1.0 - offsets) * rate)
    span_decay = jnp.exp(-span * rate)
    num_end = jnp.sum(left * power * deep(vals), axis=1)
    vals, recepts = vals.astype(BF16), recepts.astype(BF16)
    den_end = jnp.sum(left * power, axis=1)
    num0, den0 = earlier_state(span_decay, num_end, den_end, seq_axes, False)
    num0, den0 = settle([f1, f2y], num0, den0)
    f2y = f2y.got
    f1_0 = row_major(f1.value).reshape(D, -1)
    f2.value = jnp.stack([f2.value, f2y], axis=len(f2.held))
    f1_y = Plain(f1_0, y)
    f2.prepare(x)
    num0, den0 = fire([f1_y, f2], num0, den0)
    weighted, num_before, den_before = wkv_forward(keys, vals, recepts, rate, first, num0, den0, seqs)
    (weighted,) = settle([f1_y, f2], weighted)
    f1_y = f1_y.got
    f2_0 = row_major(jnp.moveaxis(f2.value, -3, 0)).reshape(2, D, -1)
    f1_c, f1_yc, f2_c = Plain(f1_0, c), Plain(f1_y, c), Plain(f2_0, c)
    (weighted,) = fire([f1_c, f1_yc, f2_c], weighted)
    last_row = last_token[:, 0] + dot(deep(weighted)[:, -1], w_o)
    edge2 = from_behind(last_row[:, None], seq_axes, 1)
    left_rows = (my_lens - my_seq * span).astype(jnp.int32)
    flat_tokens = flat(tokens)
    middle, feed_key_in, feed_recept_in, b_first, attn_sq = mid_forward(
        left_rows, weighted, w_o, flat_tokens, gain2, bias2, fmix_k, fmix_r, seqs
    )

    edge2 = (normalize(edge2)[0] * gain2 + bias2) * inside
    feed_key_in = put_rows(feed_key_in, blend(b_first, edge2, fmix_k), 0)
    feed_recept_in = put_rows(feed_recept_in, blend(b_first, edge2, fmix_r), 0)
    (feed_key_in,) = settle([f1_c, f1_yc, f2_c], feed_key_in)
    f1_c, f1_yc, f2_c = f1_c.got, f1_yc.got, f2_c.got
    pieces = (f1_0, f1_c, f1_y, f1_yc, f2_0, f2_c)
    sq, block_out, d_fval, d_fgate, squares = feed_forward(
        my_seq, left_rows, feed_key_in, pieces, w_fv, feed_recept_in, w_fr, middle, flat(cotangent), seqs
    )
    block_out = deep(block_out)
    stats = jnp.stack([jnp.sum(squares[:, 0]), jnp.sum(attn_sq), jnp.sum(squares[:, 1])])

    gfv = dot_weight(sq, d_fval).astype(BF16)
    gfv = lax.psum_scatter(gfv, dp_axes + (c,), scatter_dimension=0, tiled=True)
    gfr = dot_weight(feed_recept_in, d_fgate).astype(BF16)
    dh, d_middle, d_attn, first_k, first_r, tail, sums2 = down(
        my_seq, left_rows, d_fval, w_fv, sq, pieces, d_fgate, w_fr,
        middle, flat(cotangent), gain2, bias2, fmix_k, fmix_r, seqs,
    )
    gfk_1 = dot_weight(feed_key_in, dh[1]).astype(BF16)
    gfk_3 = dot_weight(feed_key_in, dh[3]).astype(BF16)

    lead = (2,) * len(every)
    split = lambda g_: Shrinking([g_.reshape(lead + (quarter, D))], only, every)
    side = ff // PIECES
    got_1, got_3 = Plain(gfk_1, c), Plain(gfk_3, c)
    (dh,) = fire([got_1, got_3], dh)
    gfk_0 = dot_weight(feed_key_in, dh[0]).astype(BF16)
    gfk_2 = dot_weight(feed_key_in, dh[2]).astype(BF16)
    edge3 = from_behind(first_k * (1.0 - fmix_k) + first_r * (1.0 - fmix_r), seq_axes, -1)
    d_middle, gfk_0, gfk_2, tail, sums2 = settle([got_1, got_3], d_middle, gfk_0, gfk_2, tail, sums2)
    low = lambda mine, got, at: add_low(mine[:, at : at + side], got.got[:, at : at + side])
    by_dp = lambda g_: g_.reshape((2,) * len(dp_axes) + (shard, g_.shape[1]))
    got_a = Plain(low(gfk_2, got_3, 0), y)
    r2 = Shrinking([by_dp(low(gfk_0, got_1, side)), by_dp(low(gfk_2, got_3, side))], stacked, dp_axes)
    r2.prepare(x)
    (d_attn,) = fire([got_a, r2], d_attn)
    a_0 = low(gfk_0, got_1, 0)

    d_last = tail[:, 0] + norm_back(edge3 * gain2, tail[:, 1], tail[:, 2])
    d_middle = put_rows(d_middle, d_last, span - 1)
    d_attn = put_rows(d_attn, d_last.astype(BF16), span - 1)
    small2 = sums2.sum((0, 2)) + jnp.concatenate(
        [
            -jnp.sum(edge2 * first_k, axis=0), -jnp.sum(edge2 * first_r, axis=0),
            jnp.sum(tail[:, 1] * edge3, axis=0), jnp.sum(edge3, axis=0),
        ]
    )
    p, d_recepts, ga_part, gb_part = share_back(
        d_attn, w_o, keys, vals, recepts, num_before, den_before, rate, first, seqs
    )
    r_o = dot_weight(weighted, d_attn).astype(BF16)
    r_r = dot_weight(recept_in, d_recepts).astype(BF16)
    ga_part, r_o, r_r = settle([r2, got_a], ga_part, r_o, r_r)

    orf = jnp.concatenate([r_o, r_r, gfr], axis=1)
    orf = lax.psum_scatter(orf, dp_axes + (c,), scatter_dimension=0, tiled=True)
    r1 = Shrinking([by_dp(add_low(a_0, got_a.got))], only, dp_axes)
    r1.prepare(x)
    b_got = Plain(r2.value[..., 1, :, :], y)
    ga0, gb0 = earlier_state(span_decay, ga_part.sum(1), gb_part.sum(1), seq_axes, True)
    ga0, gb0 = fire([r1, b_got], ga0, gb0)
    d_keys, d_vals, first_part, decay_part = wkv_backward(
        keys, vals, num_before, den_before, p, rate, first, ga0, gb0, seqs
    )
    d_keys, d_vals, gfv, first_part, decay_part = settle(
        [r1, b_got], d_keys, d_vals, gfv, first_part, decay_part
    )
    z1, z2 = z_axes[-1], z_axes[:-1]
    rows_of = lambda g_: g_.reshape(lead + (quarter, D))
    r_kv = Shrinking(
        [
            rows_of(dot_weight(key_in, d_keys).astype(BF16)),
            rows_of(dot_weight(value_in, d_vals).astype(BF16)),
        ],
        stacked, every,
    )
    r_kv.prepare(c)
    r_f = Shrinking([r1.value, add_low(r2.value[..., 0, :, :], b_got.got)], stacked, r1.held)
    r_f.prepare(z1)
    gfv_got = Plain(gfv, y)
    small2, first_part, decay_part = fire([r_kv, r_f, gfv_got], small2, first_part, decay_part)
    small2 = jnp.concatenate(
        [
            -(lam * rate) * jnp.sum(decay_part, axis=(0, 1))[None], jnp.sum(first_part, axis=(0, 1))[None],
            small2, jnp.pad(stats, (0, D - 3))[None],
        ]
    )
    d_keys, small2 = settle([r_kv, gfv_got], d_keys, small2)

    r_kv.prepare(y)
    out_v = Growing(add_low(gfv, gfv_got.got))
    out_v.prepare(c)
    d_keys, d_middle = fire([r_kv, out_v], d_keys, d_middle)
    mix_outs = mix_back(
        d_keys, d_vals, d_recepts, w_k, w_v, w_r, flat_tokens, d_middle,
        gain1, bias1, mix_k, mix_v, mix_r, seqs,
    )
    input_grad, firsts, tail1, sums1 = settle([r_kv, r_f, out_v], *mix_outs)

    r_kv.prepare(x)
    for z in reversed(z2):
        r_f.prepare(z)
        if z != z2[0]:
            r_f.go()
            settle([r_f])
    (firsts,) = fire([r_kv, r_f], firsts)
    mixes = (mix_k, mix_v, mix_r)
    edge4 = from_behind(sum(firsts[:, i] * (1.0 - m) for i, m in enumerate(mixes)), seq_axes, -1)
    input_last = (tail1[:, 0] + norm_back(edge4 * gain1, tail1[:, 1], tail1[:, 2])).astype(BF16)
    input_grad = deep(put_rows(input_grad, input_last, span - 1))
    small1 = sums1.sum((0, 2)) + jnp.concatenate(
        [
            -jnp.sum(edge1[:, None] * firsts, axis=(0, 2)),
            jnp.sum(tail1[:, 1] * edge4, axis=0), jnp.sum(edge4, axis=0),
        ]
    )

    small = jnp.concatenate([small1, small2])
    small, input_grad = settle([r_kv], small, input_grad)
    small = Summing(small)
    r_kv.start(z1)
    small.start(c)
    small.finish()
    small.start(y)
    (orf,) = settle([r_kv, small, r_f], orf)
    for z in reversed(z2):
        r_kv.start(z)
        if z != z2[0]:
            settle([r_kv])
    out_f = Growing(r_f.value)
    out_f.start(y)
    orf_got = swap(orf, y)
    small.start(x)
    small.finish()
    small.start(z1)
    grad_fv = out_v.value.reshape(hid, D).astype(F32)
    orf_got, grad_fv = settle([r_kv, small, out_f], orf_got, grad_fv)
    out_f.start(c)
    orf = add_low(orf, orf_got)
    orf_c = swap(orf, c)
    own = r_kv.value
    last_z = list(reversed(z2))
    for z in last_z[:-1]:
        small.start(z)
        small.finish()
    small.start(last_z[-1])
    at_y, at_c = swap(own, y), swap(own, c)
    at_both = lax.ppermute(own, (y, c), [(i, 3 - i) for i in range(4)])
    at_y, at_c, at_both, orf_c = settle([small, out_f], at_y, at_c, at_both, orf_c)
    small = small.value
    out_kv = join(join(own, at_c, c, 0), join(at_y, at_both, c, 0), y, 0)

    wide_out = lambda v, i: v[:, :, i].reshape(shard, -1)
    out_f = out_f.value.reshape(2 * seq, shard, side)
    grad_fk = jnp.concatenate([out_f[i] for i in range(2 * seq)], axis=1).astype(F32)
    orf = join(orf, orf_c, c, 0).reshape(shard, 3 * D).astype(F32)
    grad_o, grad_r, grad_fr = [orf[:, i * D : i * D + D] for i in range(3)]
    grad_k, grad_v = [wide_out(out_kv, i).astype(F32) for i in range(2)]
    rows = lax.dynamic_slice_in_dim(small[:11], my_dp * shard, shard, 1)
    rms = jnp.sqrt(small[11, :3] / (jnp.sum(lengths).astype(F32) * D))
    v = [rows[i] for i in range(11)]
    return (
        block_out, input_grad,
        v[3], v[4], v[0], v[1], v[2], v[5], v[6],
        grad_k, grad_v, grad_r, grad_o,
        v[9], v[10], v[7], v[8],
        grad_fk, grad_fr, grad_fv,
        rms[0], rms[1], rms[2],
    )


def solution(mesh):
    dp_axes, seq_axes = axes_of("d", mesh.shape["dp"]), axes_of("s", mesh.shape["seq"])
    names = dp_axes + seq_axes
    fine = jax.sharding.Mesh(mesh.devices.reshape((2,) * len(names)), names)
    big, vec, mat = P(dp_axes, seq_axes, None), P(dp_axes), P(dp_axes, None)
    args = (big, big, P(), P()) + (vec,) * 7 + (mat,) * 4 + (vec,) * 4 + (mat,) * 3
    outs = (big, big) + (vec,) * 7 + (mat,) * 4 + (vec,) * 4 + (mat,) * 3 + (P(),) * 3
    return jax.shard_map(
        functools.partial(per_device, dp_axes, seq_axes),
        mesh=fine, in_specs=args, out_specs=outs, check_vma=False,
    )
```
